32 devices in a mesh: clip: 8 (over z, x), tm: 4 (over y, core).
Axes of the slice: x: 2, y: 2, z: 4, core: 2. Of those that a mesh axis runs over, the one named last changes fastest.
Arguments:
- features: bfloat16 [16, 1024, 512], P('clip', 'tm'), may hold values from -6 to 6
- cotangent: bfloat16 [16, 1024, 512], P('clip', 'tm'), may hold values from -6 to 6
- clip_lengths: int32 [16], P('clip'), may hold values from 128 to 1024, as said below
- code_ids: int32 [4, 16, 1024], P(None, 'clip', 'tm'), may hold values from 0 to 1023
- step_count: int32 [1], replicated, may hold values from 2 to 20
- dilated_kernel_weight: float32 [3, 512, 256], P(None, None, 'clip'), may hold values from -0.15625 to 0.15625
- pointwise_conv: float32 [256, 512], P(None, 'clip'), may hold values from -0.75 to 0.75
- codebooks: float32 [4, 1024, 256], P(None, 'clip'), may hold values from -6 to 6
- dilated_first_moment: float32 [3, 512, 256], P(None, None, 'clip'), may hold values from -1 to 1
- dilated_second_moment: float32 [3, 512, 256], P(None, None, 'clip'), may hold values from 0.028995216 to 0.11598086
- pointwise_first: float32 [256, 512], P(None, 'clip'), may hold values from -1 to 1
- pointwise_second: float32 [256, 512], P(None, 'clip'), may hold values from 0.028995216 to 0.11598086
- codebook_first: float32 [4, 1024, 256], P(None, 'clip'), may hold values from -0.01953125 to 0.01953125
- codebook_second: float32 [4, 1024, 256], P(None, 'clip'), may hold values from 9.745614e-06 to 3.8982456e-05
Outputs:
- quantized: bfloat16 [16, 1024, 512], P('clip', 'tm')
- features_gradient: float32 [16, 1024, 512], P('clip', 'tm')
- grad_norm: float32 [1], replicated
- dilated_new: float32 [3, 512, 256], P(None, None, 'clip')
- dilated_grad: float32 [3, 512, 256], P(None, None, 'clip')
- dilated_square: float32 [3, 512, 256], P(None, None, 'clip')
- pointwise_new: float32 [256, 512], P(None, 'clip')
- pointwise_grad: float32 [256, 512], P(None, 'clip')
- pointwise_square: float32 [256, 512], P(None, 'clip')
- codebook_new: float32 [4, 1024, 256], P(None, 'clip')
- codebook_grad: float32 [4, 1024, 256], P(None, 'clip')
- codebook_square: float32 [4, 1024, 256], P(None, 'clip')
The draws below stay inside these ranges and needn't reach their ends.
Inputs may be any that keep to these rules, and one draw needn't show every extreme that they name: `clip_lengths`: the number of valid frames of each clip; frames from it on are padding; clip 0 is always full.
All inputs are finite; a program needn't handle non-finite values.
Results may differ from the reference program's by a relative error of at most 0.001.
The reference program's roundings to bfloat16 on the way count: a program that leaves them out, or rounds other values in their place, can miss the bound.
Values may be sent and summed in bfloat16 or wider, within the bound.
No kernel may reach another device: no remote copies, remote signals or barrier semaphores. Data moves between devices by JAX's collectives and lax.ppermute only.
A program may use at most 64 MiB of HBM per device.

```python
import math
import jax
import jax.numpy as jnp
from jax import lax

D = 512
HID = 256
CODES = 1024
GROUPS = 2
LEVELS = 2
KERNEL = 3
DILATION = 3
DG = 256
B = 16
L = 1024


def draw_clip_lengths(key, part):
    first = jax.random.randint(jax.random.fold_in(key, 11), (B,), L // 8, L + 1)
    second = jax.random.randint(jax.random.fold_in(key, 12), (B,), L // 8, L + 1)
    lengths = jnp.minimum(first, second)
    return lengths.at[0].set(L).astype(jnp.int32)


def with_ends(array, own_key, least, top_value):
    dims = array.shape
    place = [jax.random.randint(jax.random.fold_in(own_key, axis), (), 0, dims[axis]) for axis in range(len(dims))]
    array = array.at[tuple(place)].set(least)
    longest = dims.index(max(dims))
    place[longest] = (place[longest] + 1) % dims[longest]
    return array.at[tuple(place)].set(top_value)


def shard_levels(rng, dims, shards, least, high):
    level, own = 1.0, jax.random.fold_in(rng, 6)
    for position, shards_of in shards:
        steps = jnp.exp(jax.random.uniform(jax.random.fold_in(own, position), (shards_of,), jnp.float32, least / len(shards), high / len(shards)))
        level = level * jnp.repeat(steps, dims[position] // shards_of).reshape([-1 if axis == position else 1 for axis in range(len(dims))])
    return level


def gaussian(own_key, extent, spread, most, split=(), kind=jnp.bfloat16):
    level = shard_levels(own_key, extent, split, -0.22, 0.18) if split else 1.0
    values = jax.random.normal(own_key, extent, jnp.float32) * spread * level
    return jnp.minimum(jnp.maximum(values, -most), most).astype(kind)


def setup_inputs(seed: int = 0) -> dict:
    key_list = jax.random.split(jax.random.key(seed), 15)
    return {
        "features": gaussian(key_list[0], (B, L, D), 1.0, 6.0, ((0, 8), (1, 4))),
        "cotangent": gaussian(key_list[1], (B, L, D), 1.0, 6.0, ((0, 8), (1, 4))),
        "clip_lengths": draw_clip_lengths(jax.random.fold_in(key_list[14], 71), 0),
        "code_ids": with_ends(jax.random.randint(key_list[3], (GROUPS * LEVELS, B, L), 0, CODES), jax.random.fold_in(key_list[3], 1), 0, CODES - 1).astype(jnp.int32),
        "step_count": jax.random.randint(key_list[4], (1,), 2, 21).astype(jnp.int32),
        "dilated_kernel_weight": gaussian(key_list[5], (KERNEL, D, HID), (KERNEL * D) ** -0.5, 0.15625, ((2, 8),), jnp.float32),
        "pointwise_conv": gaussian(key_list[6], (HID, D), (HID // 4) ** -0.5, 0.75, ((1, 8),), jnp.float32),
        "codebooks": gaussian(key_list[7], (GROUPS * LEVELS, CODES, DG), 1.0, 6.0, ((1, 8),), jnp.float32),
        "dilated_first_moment": gaussian(key_list[8], (KERNEL, D, HID), (0.111 * 0.6 * ((4 * D * HID + 2 * CODES * D) / (1.44 * D * HID + 0.0162 * CODES * D)) ** 0.5), 1.0, ((2, 8),), jnp.float32),
        "dilated_second_moment": jnp.clip(jnp.exp(math.log(0.11598086) - 1.3862944 * jax.random.uniform(key_list[9], (KERNEL, D, HID), jnp.float32) ** shard_levels(key_list[9], (KERNEL, D, HID), ((2, 8),), -0.2, 0.2)), 0.028995216, 0.11598086),
        "pointwise_first": gaussian(key_list[10], (HID, D), (0.111 * 0.6 * ((4 * D * HID + 2 * CODES * D) / (1.44 * D * HID + 0.0162 * CODES * D)) ** 0.5), 1.0, ((1, 8),), jnp.float32),
        "pointwise_second": jnp.clip(jnp.exp(math.log(0.11598086) - 1.3862944 * jax.random.uniform(key_list[11], (HID, D), jnp.float32) ** shard_levels(key_list[11], (HID, D), ((1, 8),), -0.2, 0.2)), 0.028995216, 0.11598086),
        "codebook_first": gaussian(key_list[12], (GROUPS * LEVELS, CODES, DG), (0.111 * 0.011 * ((4 * D * HID + 2 * CODES * D) / (1.44 * D * HID + 0.0162 * CODES * D)) ** 0.5), 0.01953125, ((1, 8),), jnp.float32),
        "codebook_second": jnp.clip(jnp.exp(math.log(3.8982456317171454e-05) - 1.3862944 * jax.random.uniform(key_list[13], (GROUPS * LEVELS, CODES, DG), jnp.float32) ** shard_levels(key_list[13], (GROUPS * LEVELS, CODES, DG), ((1, 8),), -0.2, 0.2)), 9.745614079292864e-06, 3.8982456317171454e-05),
    }


@jax.custom_vjp
def low(v):
    return lax.optimization_barrier(v.astype(jnp.bfloat16)).astype(jnp.float32)

@jax.custom_vjp
def low_back(v):
    return v

def low_keep(v):
    return (low(v), None)

def low_pass(kept, grad):
    return (grad,)

def back_keep(v):
    return (v, None)

def back_low(kept, grad):
    return (low(grad),)
low.defvjp(low_keep, low_pass)
low_back.defvjp(back_keep, back_low)
PRECISE = lax.Precision.HIGHEST
COMMIT = 0.25
FIRST_DECAY = 0.9
SECOND_DECAY = 0.99
EPSILON = 1e-08
WEIGHT_DECAY = 0.01
BITRATE_FACTOR = 0.02
RATE_CODE = 0.5

def dilated(padded, kernel):
    frames = padded.shape[1] - 2 * DILATION
    result = jnp.zeros((padded.shape[0], frames, kernel.shape[2]), jnp.float32)
    for tap_index in range(KERNEL):
        window = padded[:, tap_index * DILATION:tap_index * DILATION + frames]
        result = result + jnp.einsum('btc,cd->btd', window, kernel[tap_index], precision=PRECISE)
    return result

def branch_out(inputs, frame_mask, dilated_kernel_weight, pointwise_conv):
    start = inputs * frame_mask
    activated = low(jax.nn.elu(start))
    padded = jnp.pad(activated, ((0, 0), (DILATION, DILATION), (0, 0)))
    hidden = low_back(dilated(padded, low(dilated_kernel_weight)))
    gated = low(jax.nn.elu(hidden))
    branch = low_back(jnp.einsum('btk,kd->btd', gated, low(pointwise_conv), precision=PRECISE))
    return start + branch

def clip_terms(clip_feat, clip_cot, length, clip_codes, dilated_kernel_weight, pointwise_conv, codebooks):
    positions = lax.broadcasted_iota(jnp.int32, (1, L, 1), 1)
    frame_mask = (positions < length).astype(jnp.float32)
    rounded = low(codebooks)
    picked = [jnp.take(rounded[slot], clip_codes[slot], axis=0) for slot in range(GROUPS * LEVELS)]
    latent = branch_out(clip_feat, frame_mask, dilated_kernel_weight, pointwise_conv)

    def objective(inputs, first_weight, second_weight, table):
        current = branch_out(inputs, frame_mask, first_weight, second_weight)
        table_low = low(table)
        value = jnp.sum(clip_cot * frame_mask * current)
        for group in range(GROUPS):
            moving = current[..., group * DG:(group + 1) * DG]
            fixed = latent[..., group * DG:(group + 1) * DG]
            for level in range(LEVELS):
                slot = group * LEVELS + level
                chosen = jnp.take(table_low[slot], clip_codes[slot], axis=0)
                value = value + COMMIT * jnp.sum(frame_mask * (moving - picked[slot]) ** 2)
                value = value + jnp.sum(frame_mask * (fixed - chosen) ** 2)
                moving = moving - picked[slot]
                fixed = fixed - picked[slot]
        return value
    value, pull = jax.vjp(objective, clip_feat, dilated_kernel_weight, pointwise_conv, codebooks)
    grads = pull(jnp.ones_like(value))
    parts = []
    for group in range(GROUPS):
        summed = picked[group * LEVELS]
        for level in range(1, LEVELS):
            summed = summed + picked[group * LEVELS + level]
        parts.append(summed)
    quantized = (jnp.concatenate(parts, axis=-1) * frame_mask).astype(jnp.bfloat16)
    return (grads, quantized)

def adamw_update(weight, first, second, grad, rate, completed_steps):
    first_new = FIRST_DECAY * first + (1.0 - FIRST_DECAY) * grad
    second_new = SECOND_DECAY * second + (1.0 - SECOND_DECAY) * grad * grad
    first_hat = first_new / (1.0 - FIRST_DECAY ** completed_steps)
    second_hat = second_new / (1.0 - SECOND_DECAY ** completed_steps)
    weight_new = weight - rate * (first_hat / (jnp.sqrt(second_hat) + EPSILON) + WEIGHT_DECAY * weight)
    return (weight_new, grad, second_new)

def reference(features, cotangent, clip_lengths, code_ids, step_count, dilated_kernel_weight, pointwise_conv, codebooks, dilated_first_moment, dilated_second_moment, pointwise_first, pointwise_second, codebook_first, codebook_second):
    inputs = features.astype(jnp.float32)
    backs = cotangent.astype(jnp.float32)

    def one_clip(running, clip_item):
        clip_feat, clip_cot, length, clip_codes = clip_item
        grads, quantized = clip_terms(clip_feat[None], clip_cot[None], length, clip_codes[:, None], dilated_kernel_weight, pointwise_conv, codebooks)
        running = tuple((sofar + piece for sofar, piece in zip(running, grads[1:])))
        return (running, (grads[0][0], quantized[0]))
    zeros = (jnp.zeros_like(dilated_kernel_weight), jnp.zeros_like(pointwise_conv), jnp.zeros_like(codebooks))
    partial_sums, (features_gradient, quantized) = lax.scan(one_clip, zeros, (inputs, backs, clip_lengths, jnp.moveaxis(code_ids, 1, 0)))
    count = dilated_kernel_weight.size + pointwise_conv.size + codebooks.size
    limit = jnp.sqrt(jnp.float32(count))
    squared = sum((jnp.sum(piece * piece) for piece in partial_sums))
    gradient_norm_total = jnp.sqrt(squared)
    clip_scale_factor = limit / jnp.maximum(gradient_norm_total, limit)
    completed_steps = step_count[0].astype(jnp.float32)
    dilation_factor = adamw_update(dilated_kernel_weight, dilated_first_moment, dilated_second_moment, partial_sums[0] * clip_scale_factor, BITRATE_FACTOR, completed_steps)
    pointwise_kernel = adamw_update(pointwise_conv, pointwise_first, pointwise_second, partial_sums[1] * clip_scale_factor, BITRATE_FACTOR, completed_steps)
    codebook_tensor = adamw_update(codebooks, codebook_first, codebook_second, partial_sums[2] * clip_scale_factor, RATE_CODE, completed_steps)
    return (quantized, features_gradient, gradient_norm_total.reshape(1), dilation_factor[0], dilation_factor[1], dilation_factor[2], pointwise_kernel[0], pointwise_kernel[1], pointwise_kernel[2], codebook_tensor[0], codebook_tensor[1], codebook_tensor[2])
```

```python
import functools

import jax
import jax.numpy as jnp
from jax import lax
from jax.experimental import pallas as pl
from jax.experimental.pallas import tpu as pltpu
from jax.sharding import PartitionSpec as P

D = 512
HID = 256
CODES = 1024
GROUPS = 2
LEVELS = 2
SLOTS = 4
KERNEL = 3
DILATION = 3
DG = 256
PAD = 8
HALO = 6

COMMIT = 0.25
FIRST_DECAY = 0.9
SECOND_DECAY = 0.99
EPSILON = 1e-08
WEIGHT_DECAY = 0.01
BITRATE_FACTOR = 0.02
RATE_CODE = 0.5

F32 = jnp.float32
BF16 = jnp.bfloat16
NT = (((1,), (1,)), ((), ()))
TN = (((0,), (0,)), ((), ()))
LEVEL_STEPS = 256.0
TOP = 32000.0
SCALE_GROUPS = 4
VMEM_LIMIT = 56 * 1024 * 1024


def params():
    return pltpu.CompilerParams(vmem_limit_bytes=VMEM_LIMIT)


def whole(count):
    return [pl.BlockSpec(memory_space=pltpu.VMEM)] * count


def mm(a, b):
    return jnp.dot(a, b, preferred_element_type=F32)


def mmg(a, b, dims):
    return lax.dot_general(a, b, dims, preferred_element_type=F32)


def slope(v):
    return jnp.where(v > 0, 1.0, jnp.exp(jnp.minimum(v, 0.0)))


def elu(v):
    return jnp.where(v > 0, v, jnp.exp(jnp.minimum(v, 0.0)) - 1.0)


def swap(value, clip_mask, time_mask):
    clips, times = lax.axis_size("clip"), lax.axis_size("tm")
    pairs = [
        (c * times + t, (c ^ clip_mask) * times + (t ^ time_mask))
        for c in range(clips)
        for t in range(times)
    ]
    return lax.ppermute(value, ("clip", "tm"), pairs)


def forward_kernel(
    clips,
    frames,
    half,
    block,
    meta_ref,
    f_ref,
    c_ref,
    idc_ref,
    idr_ref,
    d_ref,
    pwt_ref,
    *refs,
):
    pieces = refs[:8]
    (
        quant_ref,
        keep_ref,
        send_ref,
        act_ref,
        gated_ref,
        bg_ref,
        lg_ref,
        hs_ref,
        tab_ref,
        cho_ref,
        cgs_ref,
    ) = refs[8:]
    span = frames + 2 * PAD
    rows = clips * span
    me = meta_ref[0]
    base = meta_ref[1]
    row = lax.broadcasted_iota(jnp.int32, (span, DG), 0)
    where = row - PAD + base
    marks = []
    inner = (row >= PAD) & (row < PAD + frames)
    inside = []
    for clip in range(clips):
        good = (where >= 0) & (where < meta_ref[2 + clip])
        marks.append(jnp.where(good, 1.0, 0.0))
        inside.append(jnp.where(good & inner, 2.0, 0.0))
    mask = jnp.concatenate(marks, axis=0)
    twice = jnp.concatenate(inside, axis=0)
    mask2 = jnp.concatenate([mask, mask], axis=1)
    start = f_ref[...].astype(F32) * mask2
    act = elu(start).astype(BF16)
    act_ref[...] = act
    taps = mmg(act, d_ref[...], NT)
    hidden = (
        pltpu.roll(taps[:, :HID], DILATION, 0)
        + taps[:, HID : 2 * HID]
        + pltpu.roll(taps[:, 2 * HID :], rows - DILATION, 0)
    )
    hs_ref[...] = slope(hidden)
    gated = elu(hidden).astype(BF16)
    gated_ref[...] = gated
    latent = start + mmg(gated, pwt_ref[...], NT)
    codes = lax.broadcasted_iota(jnp.int32, (rows, CODES), 1)
    for other in range(SLOTS):
        slot = me ^ other
        for x in range(2):
            piece = pieces[other * 2 + x]
            for z in range(half):
                spot = (x * half + z) * block
                tab_ref[spot : spot + block, :] = piece[z, 64 * 8 // (2 * half) :, :]
        hot = jnp.where(codes == idc_ref[slot], 1.0, 0.0).astype(BF16)
        cho_ref[slot] = mm(hot, tab_ref[...])
    for group in range(GROUPS):
        at = slice(group * DG, (group + 1) * DG)
        first = cho_ref[2 * group]
        second = cho_ref[2 * group + 1]
        residual = latent[:, at]
        gap = residual - first
        gap2 = gap - second
        grad = mask * (c_ref[:, at].astype(F32) + 2.0 * COMMIT * (gap + gap2))
        quant = (mask * (first + second)).astype(BF16)
        bg_ref[:, at] = grad.astype(BF16)
        for clip in range(clips):
            local = slice(clip * span + PAD, clip * span + PAD + frames)
            to = slice(clip * frames, (clip + 1) * frames)
            lg_ref[to, at] = grad[local]
            quant_ref[to, at] = quant[local]
            for level, diff in ((0, gap), (1, gap2)):
                code_grad = -(twice * diff)[local]
                high = code_grad.astype(BF16)
                cgs_ref[2 * group + level, to, :DG] = high
                cgs_ref[2 * group + level, to, DG:] = (code_grad - high.astype(F32)).astype(BF16)
    codes = lax.broadcasted_iota(jnp.int32, (CODES, clips * frames), 0)
    for other in range(SLOTS):
        slot = me ^ other
        hot = jnp.where(codes == idr_ref[slot], 1.0, 0.0).astype(BF16)
        both = mm(hot, cgs_ref[slot])
        total = both[:, :DG] + both[:, DG:]
        if other % 2 == 0:
            keep_ref[other // 2] = total
        else:
            send_ref[other // 2] = total


def backward_kernel(
    clips,
    frames,
    meta_ref,
    f_ref,
    act_ref,
    gated_ref,
    bg_ref,
    lg_ref,
    hs_ref,
    d_ref,
    pwt_ref,
    fg_ref,
    dil_ref,
    pw_ref,
):
    span = frames + 2 * PAD
    rows = clips * span
    base = meta_ref[1]

    def local(value):
        return jnp.concatenate(
            [value[c * span + PAD : c * span + PAD + frames] for c in range(clips)], axis=0
        )

    bg = bg_ref[...]
    hidden_grad = (mm(bg, pwt_ref[...]) * hs_ref[...]).astype(BF16)
    wide = hidden_grad.astype(F32)
    mine = local(hidden_grad)
    pw_ref[...] = mmg(local(bg), local(gated_ref[...]), TN)
    act = act_ref[...].astype(F32)
    windows = [
        local(pltpu.roll(act, DILATION, 0).astype(BF16)),
        local(act_ref[...]),
        local(pltpu.roll(act, rows - DILATION, 0).astype(BF16)),
    ]
    for tap in range(KERNEL):
        dil_ref[tap] = mmg(mine, windows[tap], TN)
    shifted = jnp.concatenate(
        [
            local(pltpu.roll(wide, rows - DILATION, 0).astype(BF16)),
            mine,
            local(pltpu.roll(wide, DILATION, 0).astype(BF16)),
        ],
        axis=1,
    )
    act_grad = mm(shifted, d_ref[...])
    row = lax.broadcasted_iota(jnp.int32, (frames, D), 0) + base
    mask = jnp.concatenate(
        [jnp.where(row < meta_ref[2 + c], 1.0, 0.0) for c in range(clips)], axis=0
    )
    start = local(f_ref[...].astype(F32)) * mask
    fg_ref[...] = mask * (lg_ref[...] + slope(start) * act_grad)


def pack_part(value):
    count = SCALE_GROUPS
    rows = value.shape[0]
    size = rows // count
    steps, levels = [], []
    for group in range(count):
        part = value[group * size : (group + 1) * size]
        top = jnp.maximum(jnp.max(jnp.abs(part), axis=0, keepdims=True), 1e-30)
        level = jnp.ceil(jnp.log2(top) * LEVEL_STEPS)
        scale = jnp.exp2(level / -LEVEL_STEPS) * TOP
        steps.append(jnp.round(part * scale).astype(jnp.int32))
        levels.append(level)
    return steps, levels


def unpack_part(steps, level):
    return steps.astype(jnp.int32).astype(F32) * (
        jnp.exp2(level.astype(jnp.int32).astype(F32) / LEVEL_STEPS) / TOP
    )


def plane_kernel(half, rows, keep_ref, got_ref, own_ref, *outs):
    for part in range(4):
        jy, x = part // 2, part % 2
        levels = []
        for z in range(half):
            at = slice((x * half + z) * rows, (x * half + z + 1) * rows)
            value = keep_ref[jy, at, :] + got_ref[jy, at, :]
            if part == 0:
                own_ref[z] = value
                continue
            out = outs[part - 1]
            steps, more = pack_part(value)
            size = rows // SCALE_GROUPS
            for group, step in enumerate(steps):
                out[z * rows + group * size : z * rows + (group + 1) * size, :] = step.astype(
                    jnp.int16
                )
            levels += more
        if part:
            tail = jnp.concatenate(levels, axis=0).astype(jnp.int32)
            outs[part - 1][half * rows :, :] = tail.astype(jnp.int16)


def line_kernel(half, sizes, *refs):
    kinds = len(sizes)
    owns = refs[:kinds]
    gots = refs[kinds : kinds + 3 * kinds]
    own_ref = refs[4 * kinds]
    outs = refs[4 * kinds + 1 :]
    for z in range(half):
        place = 0
        levels = []
        for kind, rows in enumerate(sizes):
            size = rows // SCALE_GROUPS
            value = owns[kind][z]
            pieces = [value[g * size : (g + 1) * size] for g in range(SCALE_GROUPS)]
            for got in gots[3 * kind : 3 * kind + 3]:
                tail = got[half * rows :, :]
                for g in range(SCALE_GROUPS):
                    index = z * SCALE_GROUPS + g
                    pieces[g] = pieces[g] + unpack_part(
                        got[z * rows + g * size : z * rows + (g + 1) * size, :],
                        tail[index : index + 1],
                    )
            if z == 0:
                for g in range(SCALE_GROUPS):
                    own_ref[place + g * size : place + (g + 1) * size, :] = pieces[g]
            else:
                steps, more = pack_part(jnp.concatenate(pieces, axis=0))
                for g, step in enumerate(steps):
                    outs[z - 1][place + g * size : place + (g + 1) * size, :] = step.astype(
                        jnp.int16
                    )
                levels += more
            place += rows
        if z:
            pad = jnp.zeros((outs[z - 1].shape[0] - place - len(levels), DG), F32)
            tail = jnp.concatenate(levels + [pad], axis=0).astype(jnp.int32)
            outs[z - 1][place:, :] = tail.astype(jnp.int16)


def final_kernel(half, sizes, own_ref, *refs):
    gots, out_ref = refs[:-1], refs[-1]
    place, index = 0, 0
    total = sum(sizes)
    for rows in sizes:
        size = rows // SCALE_GROUPS
        for _ in range(SCALE_GROUPS):
            at = slice(place, place + size)
            value = own_ref[at, :]
            for got in gots:
                tail = got[total:, :]
                value = value + unpack_part(got[at, :], tail[index : index + 1])
            out_ref[at, :] = value
            place += size
            index += 1


def adamw_update(weight, first, second, grad, rate, completed_steps):
    first_new = FIRST_DECAY * first + (1.0 - FIRST_DECAY) * grad
    second_new = SECOND_DECAY * second + (1.0 - SECOND_DECAY) * grad * grad
    first_hat = first_new / (1.0 - FIRST_DECAY**completed_steps)
    second_hat = second_new / (1.0 - SECOND_DECAY**completed_steps)
    weight_new = weight - rate * (
        first_hat / (jnp.sqrt(second_hat) + EPSILON) + WEIGHT_DECAY * weight
    )
    return (weight_new, grad, second_new)


def halo(features, cotangent, code_ids):
    times = lax.axis_size("tm")
    clips, frames, _ = features.shape
    ids = jnp.moveaxis(code_ids, 0, 2)
    high, low = ids // 32, ids % 32
    packed = jnp.concatenate(
        [features, cotangent, high.astype(BF16), low.astype(BF16)], axis=2
    )
    from_left = lax.ppermute(
        packed[:, frames - HALO :], "tm", [(i, i + 1) for i in range(times - 1)]
    )
    from_right = lax.ppermute(packed[:, :HALO], "tm", [(i + 1, i) for i in range(times - 1)])
    gap = ((0, 0), (PAD - HALO, 0), (0, 0)), ((0, 0), (0, PAD - HALO), (0, 0))
    left, right = jnp.pad(from_left, gap[0]), jnp.pad(from_right, gap[1])

    def around(value, low_at, high_at):
        return jnp.concatenate([left[..., low_at:high_at], value, right[..., low_at:high_at]], axis=1)

    f = around(features, 0, D)
    c = around(cotangent, D, 2 * D)

    def decoded(part):
        part = part.astype(jnp.int32)
        return part[..., 2 * D : 2 * D + SLOTS] * 32 + part[..., 2 * D + SLOTS :]

    i = jnp.concatenate([decoded(left), ids, decoded(right)], axis=1)
    rows = clips * (frames + 2 * PAD)
    return f.reshape(rows, D), c.reshape(rows, D), i.reshape(rows, SLOTS)


def shards(
    features,
    cotangent,
    clip_lengths,
    code_ids,
    step_count,
    dilated_kernel_weight,
    pointwise_conv,
    codebooks,
    dilated_first_moment,
    dilated_second_moment,
    pointwise_first,
    pointwise_second,
    codebook_first,
    codebook_second,
):
    ranks, times = lax.axis_size("clip"), lax.axis_size("tm")
    rank, time = lax.axis_index("clip"), lax.axis_index("tm")
    clips, frames, _ = features.shape
    half = ranks // 2
    out_rows = HID // ranks
    block = CODES // ranks
    small = 2 * out_rows
    rows = clips * (frames + 2 * PAD)

    taps = dilated_kernel_weight.astype(BF16).transpose(0, 2, 1)
    taps = taps.reshape(KERNEL, out_rows, 2, DG).transpose(0, 2, 1, 3).reshape(KERNEL, small, DG)
    points = pointwise_conv.astype(BF16).transpose(1, 0)[None]
    quarters = jnp.concatenate(
        [jnp.concatenate([taps, points], axis=0), codebooks.astype(BF16)], axis=1
    )
    mine = lax.dynamic_index_in_dim(quarters, time, 0, keepdims=False)

    f, c, ids = halo(features, cotangent, code_ids)

    line = [mine] + [swap(mine, 2 * z, 0) for z in range(1, half)]
    line = jnp.stack(line, axis=0)
    plane = {
        (0, 0): line,
        (0, 1): swap(line, 1, 0),
        (2, 0): swap(line, 0, 2),
        (2, 1): swap(line, 1, 2),
    }
    pieces = []
    for other in range(4):
        for x in range(2):
            value = plane[(other & 2, x)]
            pieces.append(swap(value, 0, 1) if other & 1 else value)

    order = rank ^ jnp.arange(ranks)
    stacked = jnp.stack(
        [
            jnp.stack([pieces[o * 2][:, :small], pieces[o * 2 + 1][:, :small]], axis=1).reshape(
                ranks, small, DG
            )
            for o in range(4)
        ],
        axis=0,
    )
    stacked = jnp.take(jnp.take(stacked, time ^ jnp.arange(4), axis=0), order, axis=1)
    dil = stacked[:KERNEL].reshape(KERNEL, ranks, 2, out_rows, DG)
    dil = dil.transpose(0, 1, 3, 2, 4).reshape(KERNEL * HID, D)
    pwt = stacked[3].reshape(D, HID)

    def renamed(values):
        step = (values // block) ^ rank
        place = (step & 1) * half + (step >> 1)
        return place * block + values % block

    idc = renamed(ids).T[:, :, None]
    idr = renamed(code_ids).reshape(SLOTS, 1, clips * frames)
    meta = jnp.concatenate([jnp.stack([time, time * frames]), clip_lengths]).astype(jnp.int32)

    smem = pl.BlockSpec(memory_space=pltpu.SMEM)
    shape = jax.ShapeDtypeStruct
    quant, keep, send, act, gated, bg, lg, hs = pl.pallas_call(
        functools.partial(forward_kernel, clips, frames, half, block),
        out_shape=(
            shape((clips * frames, D), BF16),
            shape((2, CODES, DG), F32),
            shape((2, CODES, DG), F32),
            shape((rows, D), BF16),
            shape((rows, HID), BF16),
            shape((rows, D), BF16),
            shape((clips * frames, D), F32),
            shape((rows, HID), F32),
        ),
        in_specs=[smem] + whole(14),
        out_specs=tuple(whole(8)),
        scratch_shapes=[
            pltpu.VMEM((CODES, DG), BF16),
            pltpu.VMEM((SLOTS, rows, DG), F32),
            pltpu.VMEM((SLOTS, clips * frames, 2 * DG), BF16),
        ],
        compiler_params=params(),
        name="forward",
    )(meta, f, c, idc, idr, dil, pwt, *pieces)

    fg, dil_grad, pw_grad = pl.pallas_call(
        functools.partial(backward_kernel, clips, frames),
        out_shape=(
            shape((clips * frames, D), F32),
            shape((KERNEL, HID, D), F32),
            shape((D, HID), F32),
        ),
        in_specs=[smem] + whole(8),
        out_specs=tuple(whole(3)),
        compiler_params=params(),
        name="backward",
    )(meta, f, act, gated, bg, lg, hs, dil, pwt)

    parts = jnp.concatenate(
        [
            dil_grad.reshape(KERNEL, ranks, out_rows, 2, DG)
            .transpose(0, 1, 3, 2, 4)
            .reshape(KERNEL, ranks, small, DG),
            pw_grad.reshape(1, ranks, small, DG),
        ],
        axis=0,
    )
    seq = jnp.concatenate([jnp.arange(0, ranks, 2), jnp.arange(1, ranks, 2)])
    parts = jnp.take(jnp.take(parts, time ^ jnp.arange(4), axis=0), rank ^ seq, axis=1)
    parts = parts.reshape(2, 2, ranks * small, DG)

    def plane_reduce(keep, send, size):
        got = swap(send, 0, 1)
        packed = half * size + half * SCALE_GROUPS
        own, to_x, to_y, to_xy = pl.pallas_call(
            functools.partial(plane_kernel, half, size),
            out_shape=(shape((half, size, DG), F32),) + (shape((packed, DG), jnp.int16),) * 3,
            in_specs=whole(2),
            out_specs=tuple(whole(4)),
            compiler_params=params(),
            name="plane",
        )(keep, got)
        return own, (swap(to_x, 1, 0), swap(to_y, 0, 2), swap(to_xy, 1, 2))

    own_c, gots_c = plane_reduce(keep, send, block)
    own_d, gots_d = plane_reduce(parts[:, 0], parts[:, 1], small)
    sizes = (small, block)
    total = small + block
    out = pl.pallas_call(
        functools.partial(line_kernel, half, sizes),
        out_shape=(shape((total, DG), F32),)
        + (shape((total + 16, DG), jnp.int16),) * (half - 1),
        in_specs=whole(8),
        out_specs=tuple(whole(half)),
        compiler_params=params(),
        name="line",
    )(own_d, own_c, *gots_d, *gots_c)
    arrived = [swap(out[z], 2 * z, 0) for z in range(1, half)]
    piece = pl.pallas_call(
        functools.partial(final_kernel, half, sizes),
        out_shape=shape((total, DG), F32),
        in_specs=whole(half),
        out_specs=whole(1)[0],
        compiler_params=params(),
        name="final",
    )(out[0], *arrived)

    pair = jnp.stack([piece, swap(piece, 0, 2)], axis=0)
    four = jnp.stack([pair, swap(pair, 0, 1)], axis=1).reshape(4, total, DG)
    four = jnp.take(four, time ^ jnp.arange(4), axis=0)
    squared = jnp.sum(four * four).reshape(1, 1)
    step = 1
    while step < ranks:
        squared = squared + swap(squared, step, 0)
        step *= 2
    squared = squared.reshape(())

    dil_raw = four[:KERNEL, :small].reshape(KERNEL, 2, out_rows, DG)
    dil_raw = dil_raw.transpose(0, 1, 3, 2).reshape(KERNEL, D, out_rows)
    pw_raw = four[3, :small].T
    table_raw = four[:, small:]
    count = KERNEL * D * HID + D * HID + SLOTS * CODES * DG
    limit = jnp.sqrt(jnp.float32(count))
    norm = jnp.sqrt(squared)
    clip_scale = limit / jnp.maximum(norm, limit)
    steps = step_count[0].astype(F32)
    dil_out = adamw_update(
        dilated_kernel_weight,
        dilated_first_moment,
        dilated_second_moment,
        dil_raw * clip_scale,
        BITRATE_FACTOR,
        steps,
    )
    pw_out = adamw_update(
        pointwise_conv,
        pointwise_first,
        pointwise_second,
        pw_raw * clip_scale,
        BITRATE_FACTOR,
        steps,
    )
    table_out = adamw_update(
        codebooks,
        codebook_first,
        codebook_second,
        table_raw * clip_scale,
        RATE_CODE,
        steps,
    )
    return (
        quant.reshape(clips, frames, D),
        fg.reshape(clips, frames, D),
        norm.reshape(1),
        *dil_out,
        *pw_out,
        *table_out,
    )


def solution(mesh):
    in_specs = (
        P("clip", "tm", None),
        P("clip", "tm", None),
        P("clip"),
        P(None, "clip", "tm"),
        P(),
        P(None, None, "clip"),
        P(None, "clip"),
        P(None, "clip", None),
        P(None, None, "clip"),
        P(None, None, "clip"),
        P(None, "clip"),
        P(None, "clip"),
        P(None, "clip", None),
        P(None, "clip", None),
    )
    out_specs = (
        P("clip", "tm", None),
        P("clip", "tm", None),
        P(),
        P(None, None, "clip"),
        P(None, None, "clip"),
        P(None, None, "clip"),
        P(None, "clip"),
        P(None, "clip"),
        P(None, "clip"),
        P(None, "clip", None),
        P(None, "clip", None),
        P(None, "clip", None),
    )
    return jax.shard_map(shards, mesh=mesh, in_specs=in_specs, out_specs=out_specs, check_vma=False)
```

```python
import functools

import jax
import jax.numpy as jnp
from jax import lax
from jax.experimental import pallas as pl
from jax.experimental.pallas import tpu as pltpu
from jax.sharding import PartitionSpec as P

D = 512
HID = 256
CODES = 1024
GROUPS = 2
LEVELS = 2
SLOTS = 4
KERNEL = 3
DILATION = 3
DG = 256
PAD = 8

COMMIT = 0.25
FIRST_DECAY = 0.9
SECOND_DECAY = 0.99
EPSILON = 1e-08
WEIGHT_DECAY = 0.01
BITRATE_FACTOR = 0.02
RATE_CODE = 0.5

F32 = jnp.float32
BF16 = jnp.bfloat16
NT = (((1,), (1,)), ((), ()))
TN = (((0,), (0,)), ((), ()))
LEVEL_STEPS = 256.0
TOP = 32000.0
SCALE_GROUPS = 4
MIB = 1024 * 1024


def params(mib=6):
    return pltpu.CompilerParams(vmem_limit_bytes=mib * MIB)


def whole(count):
    return [pl.BlockSpec(memory_space=pltpu.VMEM)] * count


def mm(a, b):
    return jnp.dot(a, b, preferred_element_type=F32)


def mmg(a, b, dims):
    return lax.dot_general(a, b, dims, preferred_element_type=F32)


def slope(v):
    return jnp.where(v > 0, 1.0, jnp.exp(jnp.minimum(v, 0.0)))


def elu(v):
    return jnp.where(v > 0, v, jnp.exp(jnp.minimum(v, 0.0)) - 1.0)


def swap(value, clip_mask, time_mask):
    clips, times = lax.axis_size("clip"), lax.axis_size("tm")
    pairs = [
        (c * times + t, (c ^ clip_mask) * times + (t ^ time_mask))
        for c in range(clips)
        for t in range(times)
    ]
    return lax.ppermute(value, ("clip", "tm"), pairs)


def prep_kernel(dil_ref, pw_ref, table_ref, out_ref):
    time = lax.axis_index("tm")
    out_rows = dil_ref.shape[1]

    @pl.when(time < KERNEL)
    def _():
        tap = jnp.minimum(time, KERNEL - 1)
        for side in range(2):
            out_ref[side * out_rows : (side + 1) * out_rows, :] = dil_ref[
                tap, :, side * DG : (side + 1) * DG
            ].astype(BF16)

    @pl.when(time == KERNEL)
    def _():
        out_ref[: 2 * out_rows, :] = pw_ref[...].astype(BF16)

    out_ref[2 * out_rows :, :] = table_ref[time].astype(BF16)


def renamed(values, ranks):
    block = CODES // ranks
    step = (values // block) ^ lax.axis_index("clip")
    place = (step % 2) * (ranks // 2) + step // 2
    return place * block + values % block


def masks(clips, frames, len_ref, columns):
    span = frames + 2 * PAD
    row = lax.broadcasted_iota(jnp.int32, (span, columns), 0)
    where = row - PAD + lax.axis_index("tm") * frames
    inner = (row >= PAD) & (row < PAD + frames)
    marks, inside = [], []
    for clip in range(clips):
        good = (where >= 0) & (where < len_ref[clip])
        marks.append(jnp.where(good, 1.0, 0.0))
        inside.append(jnp.where(good & inner, 2.0, 0.0))
    return jnp.concatenate(marks, axis=0), jnp.concatenate(inside, axis=0)


def early_kernel(ranks, len_ref, f_ref, left_ref, right_ref, ids_ref, start_ref, act_ref, hot_ref, hott_ref):
    clips, frames, _ = f_ref.shape
    mask, _ = masks(clips, frames, len_ref, D)
    start = mask * jnp.concatenate(
        [
            part[c].astype(F32)
            for c in range(clips)
            for part in (left_ref.at[:, :, :D], f_ref, right_ref.at[:, :, :D])
        ],
        axis=0,
    )
    start_ref[...] = start
    act_ref[...] = elu(start).astype(BF16)
    rows = start.shape[0]
    codes = lax.broadcasted_iota(jnp.int32, (rows, CODES), 1)
    spots = lax.broadcasted_iota(jnp.int32, (CODES, frames), 0)
    ids = ids_ref[...]
    turned = []
    for c in range(clips):
        own = jnp.concatenate([ids[:, c].astype(F32), jnp.zeros((8 - SLOTS, frames), F32)], axis=0)
        for part in (left_ref, None, right_ref):
            if part is None:
                turned.append(own.T[:, :SLOTS].astype(jnp.int32))
            else:
                high = part[c, :, 2 * D : 2 * D + SLOTS].astype(F32)
                low = part[c, :, 2 * D + SLOTS :].astype(F32)
                turned.append((high * 32.0 + low).astype(jnp.int32))
    turned = renamed(jnp.concatenate(turned, axis=0), ranks)
    for slot in range(SLOTS):
        hot_ref[slot] = jnp.where(codes == turned[:, slot : slot + 1], 1.0, 0.0).astype(BF16)
        for c in range(clips):
            line = renamed(ids[slot, c : c + 1, :], ranks)
            hott_ref[slot, :, c * frames : (c + 1) * frames] = jnp.where(
                spots == line, 1.0, 0.0
            ).astype(BF16)


def assembled(ranks, pieces, d_ref, pwt_ref, all_ref):
    half, small = ranks // 2, 2 * HID // ranks
    out_rows = small // 2
    time, rank = lax.axis_index("tm"), lax.axis_index("clip")
    for other in range(4):
        for x in range(2):
            piece = pieces[other * 2 + x]
            for z in range(half):
                at = pl.multiple_of((rank ^ (2 * z + x)) * out_rows, out_rows)
                for side in range(2):
                    all_ref[time ^ other, pl.ds(at, out_rows), side * DG : (side + 1) * DG] = piece[
                        z, side * out_rows : (side + 1) * out_rows, :
                    ]
    for tap in range(KERNEL):
        d_ref[tap * HID : (tap + 1) * HID, :] = all_ref[tap]
    for r in range(ranks):
        for side in range(2):
            to = r * small + side * out_rows
            pwt_ref[to : to + out_rows, :] = all_ref[
                KERNEL, r * out_rows : (r + 1) * out_rows, side * DG : (side + 1) * DG
            ]


def conv_kernel(ranks, assemble, start_ref, act_ref, *refs):
    if assemble:
        pieces, refs = refs[:8], refs[8:]
        d_ref, pwt_ref, gated_ref, hs_ref, latent_ref, all_ref = refs
        assembled(ranks, pieces, d_ref, pwt_ref, all_ref)
    else:
        d_ref, pwt_ref, gated_ref, hs_ref, latent_ref = refs
    rows = start_ref.shape[0]
    taps = mmg(act_ref[...], d_ref[...], NT)
    hidden = (
        pltpu.roll(taps[:, :HID], DILATION, 0)
        + taps[:, HID : 2 * HID]
        + pltpu.roll(taps[:, 2 * HID :], rows - DILATION, 0)
    )
    hs_ref[...] = slope(hidden)
    gated = elu(hidden).astype(BF16)
    gated_ref[...] = gated
    latent_ref[...] = start_ref[...] + mmg(gated, pwt_ref[...], NT)


def quant_kernel(ranks, len_ref, latent_ref, c_ref, left_ref, right_ref, hot_ref, hott_ref, *refs):
    half, block = ranks // 2, CODES // ranks
    pieces = refs[:8]
    quant_ref, keep_ref, send_ref, bg_ref, lg_ref, tab_ref, cgs_ref = refs[8:]
    clips, frames, _ = c_ref.shape
    span = frames + 2 * PAD
    time = lax.axis_index("tm")
    mask, twice = masks(clips, frames, len_ref, DG)
    for other in range(SLOTS):
        slot = time ^ other
        for x in range(2):
            piece = pieces[other * 2 + x]
            for z in range(half):
                spot = (x * half + z) * block
                tab_ref[slot, spot : spot + block, :] = piece[z, 2 * HID // ranks :, :]
    for group in range(GROUPS):
        at = slice(group * DG, (group + 1) * DG)
        beyond = slice(D + group * DG, D + (group + 1) * DG)
        first = mm(hot_ref[2 * group], tab_ref[2 * group])
        second = mm(hot_ref[2 * group + 1], tab_ref[2 * group + 1])
        cot = jnp.concatenate(
            [
                part.astype(F32)
                for c in range(clips)
                for part in (left_ref[c, :, beyond], c_ref[c, :, at], right_ref[c, :, beyond])
            ],
            axis=0,
        )
        residual = latent_ref[:, at]
        gap = residual - first
        gap2 = gap - second
        grad = mask * (cot + 2.0 * COMMIT * (gap + gap2))
        quant = (mask * (first + second)).astype(BF16)
        bg_ref[:, at] = grad.astype(BF16)
        for clip in range(clips):
            local = slice(clip * span + PAD, clip * span + PAD + frames)
            to = slice(clip * frames, (clip + 1) * frames)
            lg_ref[to, at] = grad[local]
            quant_ref[clip, :, at] = quant[local]
            for level, diff in ((0, gap), (1, gap2)):
                code_grad = -(twice * diff)[local]
                high = code_grad.astype(BF16)
                cgs_ref[2 * group + level, to, :DG] = high
                cgs_ref[2 * group + level, to, DG:] = (code_grad - high.astype(F32)).astype(BF16)
    for other in range(SLOTS):
        slot = time ^ other
        both = mm(hott_ref[slot], cgs_ref[slot])
        total = both[:, :DG] + both[:, DG:]
        if other % 2 == 0:
            keep_ref[other // 2] = total
        else:
            send_ref[other // 2] = total


def backward_kernel(
    ranks,
    assemble,
    clips,
    len_ref,
    start_ref,
    act_ref,
    gated_ref,
    bg_ref,
    lg_ref,
    hs_ref,
    d_ref,
    pwt_ref,
    fg_ref,
    *outs,
):
    rows = start_ref.shape[0]
    span = rows // clips
    frames = span - 2 * PAD

    def local(value):
        return jnp.concatenate(
            [value[c * span + PAD : c * span + PAD + frames] for c in range(clips)], axis=0
        )

    bg = bg_ref[...]
    hidden_grad = (mm(bg, pwt_ref[...]) * hs_ref[...]).astype(BF16)
    wide = hidden_grad.astype(F32)
    mine = local(hidden_grad)
    pw_grad = mmg(local(bg), local(gated_ref[...]), TN)
    act = act_ref[...].astype(F32)
    windows = [
        local(pltpu.roll(act, DILATION, 0).astype(BF16)),
        local(act_ref[...]),
        local(pltpu.roll(act, rows - DILATION, 0).astype(BF16)),
    ]
    dil_grads = [mmg(mine, windows[tap], TN) for tap in range(KERNEL)]
    if assemble:
        keep_ref, send_ref, all_ref = outs
        half, small = ranks // 2, 2 * HID // ranks
        out_rows = small // 2
        time, rank = lax.axis_index("tm"), lax.axis_index("clip")
        for tap in range(KERNEL):
            all_ref[tap] = dil_grads[tap]
        for r in range(ranks):
            for side in range(2):
                at = r * small + side * out_rows
                all_ref[KERNEL, r * out_rows : (r + 1) * out_rows, side * DG : (side + 1) * DG] = (
                    pw_grad[at : at + out_rows]
                )
        for other in range(4):
            out = (keep_ref, send_ref)[other % 2]
            for x in range(2):
                for z in range(half):
                    at = pl.multiple_of((rank ^ (2 * z + x)) * out_rows, out_rows)
                    to = (x * half + z) * small
                    for side in range(2):
                        out[other // 2, to + side * out_rows : to + (side + 1) * out_rows, :] = (
                            all_ref[
                                time ^ other, pl.ds(at, out_rows), side * DG : (side + 1) * DG
                            ]
                        )
    else:
        dil_ref, pw_ref = outs
        for tap in range(KERNEL):
            dil_ref[tap] = dil_grads[tap]
        pw_ref[...] = pw_grad
    shifted = jnp.concatenate(
        [
            local(pltpu.roll(wide, rows - DILATION, 0).astype(BF16)),
            mine,
            local(pltpu.roll(wide, DILATION, 0).astype(BF16)),
        ],
        axis=1,
    )
    act_grad = mm(shifted, d_ref[...])
    row = lax.broadcasted_iota(jnp.int32, (frames, D), 0) + lax.axis_index("tm") * frames
    for c in range(clips):
        to = slice(c * frames, (c + 1) * frames)
        mask = jnp.where(row < len_ref[c], 1.0, 0.0)
        start = start_ref[c * span + PAD : c * span + PAD + frames, :]
        fg_ref[c] = mask * (lg_ref[to, :] + slope(start) * act_grad[to])


def pack_part(value):
    count = SCALE_GROUPS
    rows = value.shape[0]
    size = rows // count
    steps, levels = [], []
    for group in range(count):
        part = value[group * size : (group + 1) * size]
        top = jnp.maximum(jnp.max(jnp.abs(part), axis=0, keepdims=True), 1e-30)
        level = jnp.ceil(jnp.log2(top) * LEVEL_STEPS)
        scale = jnp.exp2(level / -LEVEL_STEPS) * TOP
        steps.append(jnp.round(part * scale).astype(jnp.int32))
        levels.append(level)
    return steps, levels


def unpack_part(steps, level):
    return steps.astype(jnp.int32).astype(F32) * (
        jnp.exp2(level.astype(jnp.int32).astype(F32) / LEVEL_STEPS) / TOP
    )


def plane_kernel(half, rows, keep_ref, got_ref, own_ref, *outs):
    for part in range(4):
        jy, x = part // 2, part % 2
        levels = []
        for z in range(half):
            at = slice((x * half + z) * rows, (x * half + z + 1) * rows)
            value = keep_ref[jy, at, :] + got_ref[jy, at, :]
            if part == 0:
                own_ref[z] = value
                continue
            out = outs[part - 1]
            steps, more = pack_part(value)
            size = rows // SCALE_GROUPS
            for group, step in enumerate(steps):
                out[z * rows + group * size : z * rows + (group + 1) * size, :] = step.astype(
                    jnp.int16
                )
            levels += more
        if part:
            tail = jnp.concatenate(levels, axis=0).astype(jnp.int32)
            outs[part - 1][half * rows :, :] = tail.astype(jnp.int16)


def line_kernel(half, rows, own_in, *refs):
    gots, own_ref, outs = refs[:3], refs[3], refs[4:]
    size = rows // SCALE_GROUPS
    for z in range(half):
        value = own_in[z]
        pieces = [value[g * size : (g + 1) * size] for g in range(SCALE_GROUPS)]
        for got in gots:
            tail = got[half * rows :, :]
            for g in range(SCALE_GROUPS):
                index = z * SCALE_GROUPS + g
                pieces[g] = pieces[g] + unpack_part(
                    got[z * rows + g * size : z * rows + (g + 1) * size, :],
                    tail[index : index + 1],
                )
        if z == 0:
            for g in range(SCALE_GROUPS):
                own_ref[g * size : (g + 1) * size, :] = pieces[g]
            continue
        steps, levels = pack_part(jnp.concatenate(pieces, axis=0))
        out = outs[z - 1]
        for g, step in enumerate(steps):
            out[g * size : (g + 1) * size, :] = step.astype(jnp.int16)
        pad = jnp.zeros((out.shape[0] - rows - len(levels), DG), F32)
        tail = jnp.concatenate(levels + [pad], axis=0).astype(jnp.int32)
        out[rows:, :] = tail.astype(jnp.int16)


def final_kernel(half, sizes, *refs):
    out_ref, square_ref = refs[-2:]
    squares = jnp.zeros((1, DG), F32)
    place = 0
    for kind, rows in enumerate(sizes):
        own_ref, *gots = refs[kind * half : (kind + 1) * half]
        size = rows // SCALE_GROUPS
        for g in range(SCALE_GROUPS):
            at = slice(g * size, (g + 1) * size)
            value = own_ref[at, :]
            for got in gots:
                value = value + unpack_part(got[at, :], got[rows:, :][g : g + 1])
            out_ref[place : place + size, :] = value
            squares = squares + jnp.sum(value * value, axis=0, keepdims=True)
            place += size
    square_ref[...] = jnp.broadcast_to(jnp.sum(squares, axis=1, keepdims=True), (8, 128))


def stepped(weight, first, second, grad, rate, fix1, fix2):
    first_new = FIRST_DECAY * first + (1.0 - FIRST_DECAY) * grad
    second_new = SECOND_DECAY * second + (1.0 - SECOND_DECAY) * grad * grad
    change = (first_new * fix1) / (jnp.sqrt(second_new * fix2) + EPSILON) + WEIGHT_DECAY * weight
    return weight - rate * change, second_new


def update_kernel(fix_ref, square_ref, *refs):
    pieces = refs[:4]
    dil, pw, table = refs[4:7], refs[7:10], refs[10:13]
    norm_ref = refs[13]
    dil_out, pw_out, table_out = refs[14:17], refs[17:20], refs[20:23]
    out_rows = dil[0].shape[1]
    small = 2 * out_rows
    time = lax.axis_index("tm")
    count = KERNEL * D * HID + D * HID + SLOTS * CODES * DG
    norm = jnp.sqrt(square_ref[...][:1, :1])
    limit = jnp.sqrt(jnp.full((1, 1), float(count), F32))
    scale = limit / jnp.maximum(norm, limit)
    norm_ref[...] = jnp.broadcast_to(norm, norm_ref.shape)
    fixes = (fix_ref[0], fix_ref[1])
    for other in range(4):
        quarter = time ^ other
        piece = pieces[other]
        grad = piece[small:, :] * scale
        state = [v[quarter] for v in table]
        weight, second = stepped(*state, grad, RATE_CODE, *fixes)
        table_out[0][quarter] = weight
        table_out[1][quarter] = grad
        table_out[2][quarter] = second

        @pl.when(quarter < KERNEL)
        def _():
            tap = jnp.minimum(quarter, KERNEL - 1)
            for side in range(2):
                to = slice(side * DG, (side + 1) * DG)
                grad = piece[side * out_rows : (side + 1) * out_rows, :] * scale
                state = [v[tap, :, to] for v in dil]
                weight, second = stepped(*state, grad, BITRATE_FACTOR, *fixes)
                dil_out[0][tap, :, to] = weight
                dil_out[1][tap, :, to] = grad
                dil_out[2][tap, :, to] = second

        @pl.when(quarter == KERNEL)
        def _():
            grad = piece[:small, :] * scale
            weight, second = stepped(*[v[...] for v in pw], grad, BITRATE_FACTOR, *fixes)
            pw_out[0][...] = weight
            pw_out[1][...] = grad
            pw_out[2][...] = second


def halo(features, cotangent, code_ids):
    times = lax.axis_size("tm")
    frames = features.shape[1]
    ids = jnp.moveaxis(code_ids, 0, 2)

    def packed(low, high):
        part = ids[:, low:high]
        return jnp.concatenate(
            [
                features[:, low:high],
                cotangent[:, low:high],
                (part // 32).astype(BF16),
                (part % 32).astype(BF16),
            ],
            axis=2,
        )

    from_left = lax.ppermute(
        packed(frames - PAD, frames), "tm", [(i, i + 1) for i in range(times - 1)]
    )
    from_right = lax.ppermute(packed(0, PAD), "tm", [(i + 1, i) for i in range(times - 1)])
    return from_left, from_right


def shards(
    features,
    cotangent,
    clip_lengths,
    code_ids,
    step_count,
    dilated_kernel_weight,
    pointwise_conv,
    codebooks,
    dilated_first_moment,
    dilated_second_moment,
    pointwise_first,
    pointwise_second,
    codebook_first,
    codebook_second,
):
    ranks = lax.axis_size("clip")
    rank, time = lax.axis_index("clip"), lax.axis_index("tm")
    clips, frames, _ = features.shape
    half = ranks // 2
    out_rows = HID // ranks
    block = CODES // ranks
    small = 2 * out_rows
    rows = clips * (frames + 2 * PAD)
    smem = pl.BlockSpec(memory_space=pltpu.SMEM)
    shape = jax.ShapeDtypeStruct
    assemble = out_rows % 16 == 0
    dil_state = [
        v.transpose(0, 2, 1)
        for v in (dilated_kernel_weight, dilated_first_moment, dilated_second_moment)
    ]
    pw_state = [v.T for v in (pointwise_conv, pointwise_first, pointwise_second)]
    table_state = [codebooks, codebook_first, codebook_second]

    if assemble:
        mine = pl.pallas_call(
            prep_kernel,
            out_shape=shape((small + block, DG), BF16),
            in_specs=whole(3),
            out_specs=whole(1)[0],
            compiler_params=params(),
            name="prep",
        )(dil_state[0], pw_state[0], codebooks)
    else:
        taps = dil_state[0].astype(BF16).reshape(KERNEL, out_rows, 2, DG).transpose(0, 2, 1, 3)
        quarters = jnp.concatenate(
            [taps.reshape(KERNEL, small, DG), pw_state[0].astype(BF16)[None]], axis=0
        )
        quarters = jnp.concatenate([quarters, codebooks.astype(BF16)], axis=1)
        mine = lax.dynamic_index_in_dim(quarters, time, 0, keepdims=False)

    line = jnp.stack([mine] + [swap(mine, 2 * z, 0) for z in range(1, half)], axis=0)
    features, cotangent, code_ids, line = lax.optimization_barrier(
        (features, cotangent, code_ids, line)
    )
    plane = [line, swap(line, 1, 0), swap(line, 0, 2), swap(line, 1, 2)]
    left, right = halo(features, cotangent, code_ids)

    start, act, hot, hott = pl.pallas_call(
        functools.partial(early_kernel, ranks),
        out_shape=(
            shape((rows, D), F32),
            shape((rows, D), BF16),
            shape((SLOTS, rows, CODES), BF16),
            shape((SLOTS, CODES, clips * frames), BF16),
        ),
        in_specs=[smem] + whole(4),
        out_specs=tuple(whole(4)),
        compiler_params=params(8),
        name="early",
    )(clip_lengths, features, left, right, code_ids)

    plane[3], hot = lax.optimization_barrier((plane[3], hot))
    pieces = []
    for other in range(4):
        for value in plane[other & 2 : (other & 2) + 2]:
            pieces.append(swap(value, 0, 1) if other & 1 else value)

    weights = (shape((KERNEL * HID, D), BF16), shape((D, HID), BF16))
    given = pieces
    if not assemble:
        order = rank ^ jnp.arange(ranks)
        stacked = jnp.stack(
            [
                jnp.stack([v[:, :small] for v in pieces[2 * o : 2 * o + 2]], axis=1).reshape(
                    ranks, small, DG
                )
                for o in range(4)
            ],
            axis=0,
        )
        stacked = jnp.take(jnp.take(stacked, time ^ jnp.arange(4), axis=0), order, axis=1)
        dil = stacked[:KERNEL].reshape(KERNEL, ranks, 2, out_rows, DG)
        dil = dil.transpose(0, 1, 3, 2, 4).reshape(KERNEL * HID, D)
        given = [dil, stacked[3].reshape(D, HID)]
    outs = pl.pallas_call(
        functools.partial(conv_kernel, ranks, assemble),
        out_shape=(weights if assemble else ())
        + (shape((rows, HID), BF16), shape((rows, HID), F32), shape((rows, D), F32)),
        in_specs=whole(2 + len(given)),
        out_specs=tuple(whole(5 if assemble else 3)),
        scratch_shapes=[pltpu.VMEM((4, HID, D), BF16)] if assemble else [],
        compiler_params=params(10),
        name="conv",
    )(start, act, *given)
    dil, pwt, gated, hs, latent = tuple(outs) if assemble else tuple(given) + tuple(outs)

    quant, keep, send, bg, lg = pl.pallas_call(
        functools.partial(quant_kernel, ranks),
        out_shape=(
            shape((clips, frames, D), BF16),
            shape((2, CODES, DG), F32),
            shape((2, CODES, DG), F32),
            shape((rows, D), BF16),
            shape((clips * frames, D), F32),
        ),
        in_specs=[smem] + whole(14),
        out_specs=tuple(whole(5)),
        scratch_shapes=[
            pltpu.VMEM((SLOTS, CODES, DG), BF16),
            pltpu.VMEM((SLOTS, clips * frames, 2 * DG), BF16),
        ],
        compiler_params=params(16),
        name="quant",
    )(clip_lengths, latent, cotangent, left, right, hot, hott, *pieces)

    if assemble:
        grads = (shape((2, ranks * small, DG), F32),) * 2
    else:
        grads = (shape((KERNEL, HID, D), F32), shape((D, HID), F32))
    fg, first_grad, second_grad = pl.pallas_call(
        functools.partial(backward_kernel, ranks, assemble, clips),
        out_shape=(shape((clips, frames, D), F32),) + grads,
        in_specs=[smem] + whole(8),
        out_specs=tuple(whole(3)),
        scratch_shapes=[pltpu.VMEM((4, HID, D), F32)] if assemble else [],
        compiler_params=params(16),
        name="backward",
    )(clip_lengths, start, act, gated, bg, lg, hs, dil, pwt)

    if assemble:
        keep_d, send_d = first_grad, second_grad
    else:
        parts = jnp.concatenate(
            [
                first_grad.reshape(KERNEL, ranks, out_rows, 2, DG)
                .transpose(0, 1, 3, 2, 4)
                .reshape(KERNEL, ranks, small, DG),
                second_grad.reshape(1, ranks, small, DG),
            ],
            axis=0,
        )
        seq = jnp.concatenate([jnp.arange(0, ranks, 2), jnp.arange(1, ranks, 2)])
        parts = jnp.take(jnp.take(parts, time ^ jnp.arange(4), axis=0), rank ^ seq, axis=1)
        parts = parts.reshape(2, 2, ranks * small, DG)
        keep_d, send_d = parts[:, 0], parts[:, 1]

    def plane_sent(keep, got, size, tag):
        packed = half * size + half * SCALE_GROUPS
        own, to_x, to_y, to_xy = pl.pallas_call(
            functools.partial(plane_kernel, half, size),
            out_shape=(shape((half, size, DG), F32),) + (shape((packed, DG), jnp.int16),) * 3,
            in_specs=whole(2),
            out_specs=tuple(whole(4)),
            compiler_params=params(),
            name="plane_" + tag,
        )(keep, got)
        return own, swap(to_x, 1, 0), swap(to_y, 0, 2), swap(to_xy, 1, 2)

    def line_sent(parts, size, tag):
        out = pl.pallas_call(
            functools.partial(line_kernel, half, size),
            out_shape=(shape((size, DG), F32),)
            + (shape((size + 16, DG), jnp.int16),) * (half - 1),
            in_specs=whole(4),
            out_specs=tuple(whole(half)),
            compiler_params=params(),
            name="line_" + tag,
        )(*parts)
        return [out[0]] + [swap(out[z], 2 * z, 0) for z in range(1, half)]

    got_c, got_d = swap(send, 0, 1), swap(send_d, 0, 1)
    parts_c = plane_sent(keep, got_c, block, "codes")
    own_c, keep_d = lax.optimization_barrier((parts_c[0], keep_d))
    parts_d = plane_sent(keep_d, got_d, small, "conv")
    parts_c = line_sent((own_c,) + parts_c[1:], block, "codes")
    own_d, first_c = lax.optimization_barrier((parts_d[0], parts_c[0]))
    parts_c = [first_c] + parts_c[1:]
    parts_d = line_sent((own_d,) + parts_d[1:], small, "conv")
    total = small + block
    piece, squared = pl.pallas_call(
        functools.partial(final_kernel, half, (small, block)),
        out_shape=(shape((total, DG), F32), shape((8, 128), F32)),
        in_specs=whole(2 * half),
        out_specs=tuple(whole(2)),
        compiler_params=params(),
        name="final",
    )(*parts_d, *parts_c)

    fours = [piece, None, swap(piece, 0, 2), None]
    step = 1
    while step < ranks:
        squared = squared + swap(squared, step, 0)
        step *= 2
    across, squared = lax.optimization_barrier((fours[2], squared))
    fours[1], fours[2], fours[3] = swap(piece, 0, 1), across, swap(across, 0, 1)
    squared = squared + swap(squared, 0, 2)
    squared = squared + swap(squared, 0, 1)
    steps = step_count[0].astype(F32)
    decays = jnp.stack([1.0 / (1.0 - FIRST_DECAY**steps), 1.0 / (1.0 - SECOND_DECAY**steps)])
    if assemble:
        state = dil_state + pw_state + table_state
        norm, *new = pl.pallas_call(
            update_kernel,
            out_shape=(shape((8, 128), F32),) + tuple(shape(v.shape, F32) for v in state),
            in_specs=[smem] + whole(14),
            out_specs=tuple(whole(10)),
            compiler_params=params(),
            name="update",
        )(decays, squared, *fours, *state)
        norm = norm[0, :1]
        dil_new, pw_new, table_new = new[:3], new[3:6], new[6:]
    else:
        four = jnp.take(jnp.stack(fours, axis=0), time ^ jnp.arange(4), axis=0)
        raw = four[:KERNEL, :small].reshape(KERNEL, 2, out_rows, DG)
        raw = raw.transpose(0, 2, 1, 3).reshape(KERNEL, out_rows, D)
        count = KERNEL * D * HID + D * HID + SLOTS * CODES * DG
        limit = jnp.sqrt(jnp.float32(count))
        norm = jnp.sqrt(squared[0, :1])
        scale = limit / jnp.maximum(norm[0], limit)
        new = []
        for state, grad, rate in (
            (dil_state, raw, BITRATE_FACTOR),
            (pw_state, four[3, :small], BITRATE_FACTOR),
            (table_state, four[:, small:], RATE_CODE),
        ):
            grad = grad * scale
            weight, second = stepped(*state, grad, rate, decays[0], decays[1])
            new.append((weight, grad, second))
        dil_new, pw_new, table_new = new
    return (
        quant,
        fg,
        norm,
        *[v.transpose(0, 2, 1) for v in dil_new],
        *[v.T for v in pw_new],
        *table_new,
    )


def solution(mesh):
    in_specs = (
        P("clip", "tm", None),
        P("clip", "tm", None),
        P("clip"),
        P(None, "clip", "tm"),
        P(),
        P(None, None, "clip"),
        P(None, "clip"),
        P(None, "clip", None),
        P(None, None, "clip"),
        P(None, None, "clip"),
        P(None, "clip"),
        P(None, "clip"),
        P(None, "clip", None),
        P(None, "clip", None),
    )
    out_specs = (
        P("clip", "tm", None),
        P("clip", "tm", None),
        P(),
        P(None, None, "clip"),
        P(None, None, "clip"),
        P(None, None, "clip"),
        P(None, "clip"),
        P(None, "clip"),
        P(None, "clip"),
        P(None, "clip", None),
        P(None, "clip", None),
        P(None, "clip", None),
    )
    return jax.shard_map(shards, mesh=mesh, in_specs=in_specs, out_specs=out_specs, check_vma=False)
```

```python
import functools

import jax
import jax.numpy as jnp
from jax import lax
from jax.experimental import pallas as pl
from jax.experimental.pallas import tpu as pltpu
from jax.sharding import PartitionSpec as P

D = 512
HID = 256
CODES = 1024
GROUPS = 2
LEVELS = 2
SLOTS = 4
KERNEL = 3
DILATION = 3
DG = 256
PAD = 8

COMMIT = 0.25
FIRST_DECAY = 0.9
SECOND_DECAY = 0.99
EPSILON = 1e-08
WEIGHT_DECAY = 0.01
BITRATE_FACTOR = 0.02
RATE_CODE = 0.5

F32 = jnp.float32
BF16 = jnp.bfloat16
NT = (((1,), (1,)), ((), ()))
TN = (((0,), (0,)), ((), ()))
LEVEL_STEPS = 256.0
TOP = 32000.0
SCALE_GROUPS = 4
MIB = 1024 * 1024


def params(mib=6):
    return pltpu.CompilerParams(vmem_limit_bytes=mib * MIB)


def whole(count):
    return [pl.BlockSpec(memory_space=pltpu.VMEM)] * count


def mm(a, b):
    return jnp.dot(a, b, preferred_element_type=F32)


def mmg(a, b, dims):
    return lax.dot_general(a, b, dims, preferred_element_type=F32)


def slope(v):
    return jnp.where(v > 0, 1.0, jnp.exp(jnp.minimum(v, 0.0)))


def elu(v):
    return jnp.where(v > 0, v, jnp.exp(jnp.minimum(v, 0.0)) - 1.0)


def swap(value, clip_mask, time_mask):
    clips, times = lax.axis_size("clip"), lax.axis_size("tm")
    pairs = [
        (c * times + t, (c ^ clip_mask) * times + (t ^ time_mask))
        for c in range(clips)
        for t in range(times)
    ]
    return lax.ppermute(value, ("clip", "tm"), pairs)


def prep_kernel(dil_hbm, pw_hbm, table_hbm, conv_ref, code_ref, dil_ref, pw_ref, table_ref, sems):
    time = lax.axis_index("tm")
    bit = time % 2
    out_rows = pw_ref.shape[0] // 2
    second = jnp.minimum(2 + bit, KERNEL - 1)
    copies = [
        pltpu.make_async_copy(table_hbm.at[time], table_ref, sems.at[0]),
        pltpu.make_async_copy(dil_hbm.at[bit], dil_ref.at[0], sems.at[1]),
        pltpu.make_async_copy(dil_hbm.at[second], dil_ref.at[1], sems.at[2]),
        pltpu.make_async_copy(pw_hbm, pw_ref, sems.at[3]),
    ]
    for copy in copies:
        copy.start()
    copies[0].wait()
    code_ref[...] = table_ref[...].astype(BF16)
    for copy in copies[1:]:
        copy.wait()
    for side in range(2):
        for part in range(2):
            conv_ref[part, side * out_rows : (side + 1) * out_rows, :] = dil_ref[
                part, :, side * DG : (side + 1) * DG
            ].astype(BF16)

    @pl.when(bit == 1)
    def _():
        conv_ref[1] = pw_ref[...].astype(BF16)


def renamed(values, ranks):
    block = CODES // ranks
    step = (values // block) ^ lax.axis_index("clip")
    place = (step % 2) * (ranks // 2) + step // 2
    return place * block + values % block


def masks(clips, frames, len_ref, columns):
    base = lax.axis_index("tm") * frames

    def mark(first, count, clip):
        where = lax.broadcasted_iota(jnp.int32, (count, columns), 0) + first
        return jnp.where((where >= 0) & (where < len_ref[clip]), 1.0, 0.0)

    own = [mark(base, frames, c) for c in range(clips)]
    margins = [
        mark(first, PAD, c) for c in range(clips) for first in (base - PAD, base + frames)
    ]
    return jnp.concatenate(own + margins, axis=0)


def widened(value, clip, clips, frames):
    at = clips * frames + 2 * PAD * clip
    return jnp.concatenate(
        [
            value[at : at + PAD],
            value[clip * frames : (clip + 1) * frames],
            value[at + PAD : at + 2 * PAD],
        ],
        axis=0,
    )


def pack_kernel(f_hbm, c_hbm, ids_hbm, near_ref, far_ref, buf, ids_ref, sems):
    clips, frames, _ = f_hbm.shape
    edge = 2 * PAD
    odd = lax.axis_index("tm") % 2
    copies = [pltpu.make_async_copy(ids_hbm, ids_ref, sems.at[4])]
    for kind, source in enumerate((f_hbm, c_hbm)):
        for side, at in enumerate((frames - edge, 0)):
            copies.append(
                pltpu.make_async_copy(
                    source.at[:, pl.ds(at, edge), :], buf.at[kind, side], sems.at[2 * kind + side]
                )
            )
    for copy in copies:
        copy.start()
    for copy in copies:
        copy.wait()
    outs = []
    for side in range(2):
        at = slice(PAD, 2 * PAD) if side == 0 else slice(0, PAD)
        parts = []
        for c in range(clips):
            ids = ids_ref[:, c, :]
            if side == 0:
                ids = pltpu.roll(ids, PAD, 1)
            both = jnp.concatenate([ids // 32, ids % 32], axis=0).astype(F32)
            both = jnp.concatenate([both, jnp.zeros((8, 2 * D - frames), F32)], axis=1)
            ends = [buf[kind, side, c].astype(F32)[at] for kind in range(2)]
            parts.append(jnp.concatenate([jnp.concatenate(ends, axis=1), both], axis=0))
        outs.append(parts)
    for c in range(clips):
        last, first = outs[0][c], outs[1][c]
        near_ref[c] = jnp.where(odd == 1, first, last).astype(BF16)
        far_ref[c] = jnp.where(odd == 1, last, first).astype(BF16)


def own_kernel(ranks, ids_ref, hot_ref, hott_ref):
    _, clips, frames = ids_ref.shape
    codes = lax.broadcasted_iota(jnp.int32, (frames, CODES), 1)
    spots = lax.broadcasted_iota(jnp.int32, (CODES, frames), 0)
    for c in range(clips):
        ids = renamed(ids_ref[:, c, :], ranks)
        turned = jnp.concatenate([ids.astype(F32), jnp.zeros((8 - SLOTS, frames), F32)], axis=0)
        turned = turned.T.astype(jnp.int32)
        at = slice(c * frames, (c + 1) * frames)
        for slot in range(SLOTS):
            hot_ref[slot, at, :] = jnp.where(codes == turned[:, slot : slot + 1], 1.0, 0.0).astype(
                BF16
            )
            hott_ref[slot, :, at] = jnp.where(spots == ids[slot : slot + 1], 1.0, 0.0).astype(BF16)
    hot_ref[:, clips * frames :, :] = jnp.zeros((SLOTS, 2 * PAD * clips, CODES), BF16)


def margin_kernel(ranks, len_ref, f_ref, near_ref, far_ref, old_ref, start_ref, act_ref, cot_ref, hot_ref):
    del old_ref
    clips, frames, _ = f_ref.shape
    odd = lax.axis_index("tm") % 2
    both = []
    for c in range(clips):
        near, far = near_ref[c].astype(F32), far_ref[c].astype(F32)
        both += [jnp.where(odd == 1, near, far), jnp.where(odd == 1, far, near)]
    start = masks(clips, frames, len_ref, D) * jnp.concatenate(
        [f_ref[c].astype(F32) for c in range(clips)] + [part[:PAD, :D] for part in both], axis=0
    )
    start_ref[...] = start
    act_ref[...] = elu(start).astype(BF16)
    cot_ref[...] = jnp.concatenate([part[:PAD, D:] for part in both], axis=0)
    turned = jnp.concatenate([part[PAD:, :128].T[:PAD] for part in both], axis=0)
    ids = renamed((turned[:, :SLOTS] * 32.0 + turned[:, SLOTS : 2 * SLOTS]).astype(jnp.int32), ranks)
    codes = lax.broadcasted_iota(jnp.int32, (2 * PAD * clips, CODES), 1)
    for slot in range(SLOTS):
        hot_ref[slot, clips * frames :, :] = jnp.where(
            codes == ids[:, slot : slot + 1], 1.0, 0.0
        ).astype(BF16)


def assembled(ranks, pieces, d_ref, pwt_ref, all_ref):
    half, small = ranks // 2, 2 * HID // ranks
    out_rows = small // 2
    bit, rank = lax.axis_index("tm") % 2, lax.axis_index("clip")
    for other in range(2):
        for z in range(half):
            piece = pieces[other * half + z]
            for x in range(2):
                at = pl.multiple_of((rank ^ (2 * z + x)) * out_rows, out_rows)
                for part in range(2):
                    for side in range(2):
                        all_ref[
                            2 * part + (bit ^ other),
                            pl.ds(at, out_rows),
                            side * DG : (side + 1) * DG,
                        ] = piece[x, part, side * out_rows : (side + 1) * out_rows, :]
    for tap in range(KERNEL):
        d_ref[tap * HID : (tap + 1) * HID, :] = all_ref[tap]
    for r in range(ranks):
        for side in range(2):
            to = r * small + side * out_rows
            pwt_ref[to : to + out_rows, :] = all_ref[
                KERNEL, r * out_rows : (r + 1) * out_rows, side * DG : (side + 1) * DG
            ]


def conv_kernel(ranks, assemble, clips, start_ref, act_ref, *refs):
    if assemble:
        pieces, refs = refs[:ranks], refs[ranks:]
        d_ref, pwt_ref, gated_ref, hs_ref, latent_ref, all_ref = refs
        assembled(ranks, pieces, d_ref, pwt_ref, all_ref)
    else:
        d_ref, pwt_ref, gated_ref, hs_ref, latent_ref = refs
    rows = start_ref.shape[0]
    taps = mmg(act_ref[...], d_ref[...], NT)
    frames = rows // clips - 2 * PAD
    span = frames + 2 * PAD
    own, margins = [], []
    for c in range(clips):
        wide = widened(taps, c, clips, frames)
        part = (
            pltpu.roll(wide[:, :HID], DILATION, 0)
            + wide[:, HID : 2 * HID]
            + pltpu.roll(wide[:, 2 * HID :], span - DILATION, 0)
        )
        own.append(part[PAD : PAD + frames])
        margins += [part[:PAD], part[PAD + frames :]]
    hidden = jnp.concatenate(own + margins, axis=0)
    hs_ref[...] = slope(hidden)
    gated = elu(hidden).astype(BF16)
    gated_ref[...] = gated
    latent_ref[...] = start_ref[...] + mmg(gated, pwt_ref[...], NT)


def quant_kernel(ranks, len_ref, latent_ref, c_ref, cot_ref, hot_ref, hott_ref, *refs):
    half, block = ranks // 2, CODES // ranks
    pieces, refs = refs[:8], refs[8:]
    quant_ref, keep_ref, send_ref, bg_ref, lg_ref, tab_ref, cgs_ref = refs
    clips, frames, _ = c_ref.shape
    time = lax.axis_index("tm")
    mask = masks(clips, frames, len_ref, DG)
    local = clips * frames
    twice = 2.0 * mask[:local]
    for other in range(SLOTS):
        slot = time ^ other
        for x in range(2):
            for z in range(half):
                spot = (x * half + z) * block
                tab_ref[slot, spot : spot + block, :] = pieces[2 * other + x][z]
    for group in range(GROUPS):
        at = slice(group * DG, (group + 1) * DG)
        first = mm(hot_ref[2 * group], tab_ref[2 * group])
        second = mm(hot_ref[2 * group + 1], tab_ref[2 * group + 1])
        cot = jnp.concatenate(
            [c_ref[c, :, at].astype(F32) for c in range(clips)] + [cot_ref[:, at]], axis=0
        )
        residual = latent_ref[:, at]
        gap = residual - first
        gap2 = gap - second
        grad = mask * (cot + 2.0 * COMMIT * (gap + gap2))
        quant = (mask * (first + second))[:local].astype(BF16)
        bg_ref[:, at] = grad.astype(BF16)
        lg_ref[:, at] = grad[:local]
        for clip in range(clips):
            quant_ref[clip, :, at] = quant[clip * frames : (clip + 1) * frames]
        for level, diff in ((0, gap), (1, gap2)):
            code_grad = -(twice * diff[:local])
            high = code_grad.astype(BF16)
            cgs_ref[2 * group + level, :, :DG] = high
            cgs_ref[2 * group + level, :, DG:] = (code_grad - high.astype(F32)).astype(BF16)
    for other in range(SLOTS):
        slot = time ^ other
        pair = mm(hott_ref[slot], cgs_ref[slot])
        total = pair[:, :DG] + pair[:, DG:]
        if other % 2 == 0:
            keep_ref[other // 2] = total
        else:
            send_ref[other // 2] = total


def backward_kernel(
    ranks,
    assemble,
    clips,
    len_ref,
    start_ref,
    act_ref,
    gated_ref,
    bg_ref,
    lg_ref,
    hs_ref,
    d_ref,
    pwt_ref,
    fg_ref,
    *outs,
):
    rows = start_ref.shape[0]
    span = rows // clips
    frames = span - 2 * PAD
    local = clips * frames
    bg = bg_ref[...]
    hidden_grad = (mm(bg, pwt_ref[...]) * hs_ref[...]).astype(BF16)
    mine = hidden_grad[:local]
    pw_grad = mmg(bg[:local], gated_ref[:local, :], TN)

    def moved(value, shift):
        return jnp.concatenate(
            [
                pltpu.roll(widened(value, c, clips, frames), shift % span, 0)[PAD : PAD + frames]
                for c in range(clips)
            ],
            axis=0,
        ).astype(BF16)

    act = act_ref[...].astype(F32)
    windows = [moved(act, DILATION), act_ref[:local, :], moved(act, -DILATION)]
    dil_grads = [mmg(mine, windows[tap], TN) for tap in range(KERNEL)]
    if assemble:
        keep_ref, send_ref, all_ref = outs
        half, small = ranks // 2, 2 * HID // ranks
        out_rows = small // 2
        time, rank = lax.axis_index("tm"), lax.axis_index("clip")
        for tap in range(KERNEL):
            all_ref[tap] = dil_grads[tap]
        for r in range(ranks):
            for side in range(2):
                at = r * small + side * out_rows
                all_ref[KERNEL, r * out_rows : (r + 1) * out_rows, side * DG : (side + 1) * DG] = (
                    pw_grad[at : at + out_rows]
                )
        for other in range(4):
            out = (keep_ref, send_ref)[other % 2]
            for x in range(2):
                for z in range(half):
                    at = pl.multiple_of((rank ^ (2 * z + x)) * out_rows, out_rows)
                    to = (x * half + z) * small
                    for side in range(2):
                        out[other // 2, to + side * out_rows : to + (side + 1) * out_rows, :] = (
                            all_ref[
                                time ^ other, pl.ds(at, out_rows), side * DG : (side + 1) * DG
                            ]
                        )
    else:
        dil_ref, pw_ref = outs
        for tap in range(KERNEL):
            dil_ref[tap] = dil_grads[tap]
        pw_ref[...] = pw_grad
    wide = hidden_grad.astype(F32)
    shifted = jnp.concatenate([moved(wide, -DILATION), mine, moved(wide, DILATION)], axis=1)
    act_grad = mm(shifted, d_ref[...])
    row = lax.broadcasted_iota(jnp.int32, (frames, D), 0) + lax.axis_index("tm") * frames
    for c in range(clips):
        to = slice(c * frames, (c + 1) * frames)
        mask = jnp.where(row < len_ref[c], 1.0, 0.0)
        start = start_ref[to, :]
        fg_ref[c] = mask * (lg_ref[to, :] + slope(start) * act_grad[to])


def pack_part(value):
    count = SCALE_GROUPS
    rows = value.shape[0]
    size = rows // count
    steps, levels = [], []
    for group in range(count):
        part = value[group * size : (group + 1) * size]
        top = jnp.maximum(jnp.max(jnp.abs(part), axis=0, keepdims=True), 1e-30)
        level = jnp.ceil(jnp.log2(top) * LEVEL_STEPS)
        scale = jnp.exp2(level / -LEVEL_STEPS) * TOP
        steps.append(jnp.round(part * scale).astype(jnp.int32))
        levels.append(level)
    return steps, levels


def unpack_part(steps, level):
    return steps.astype(jnp.int32).astype(F32) * (
        jnp.exp2(level.astype(jnp.int32).astype(F32) / LEVEL_STEPS) / TOP
    )


def send_kernel(groups, rows, keep_ref, got_ref, own_ref, *outs):
    size = rows // SCALE_GROUPS
    for part, blocks in enumerate(groups):
        levels = []
        for place, (jy, start) in enumerate(blocks):
            at = slice(start * rows, (start + 1) * rows)
            value = keep_ref[jy, at, :] + got_ref[jy, at, :]
            if part == 0:
                own_ref[place] = value
                continue
            steps, more = pack_part(value)
            for group, step in enumerate(steps):
                spot = place * rows + group * size
                outs[part - 1][spot : spot + size, :] = step.astype(jnp.int16)
            levels += more
        if part:
            tail = jnp.concatenate(levels, axis=0).astype(jnp.int32)
            outs[part - 1][len(blocks) * rows :, :] = tail.astype(jnp.int16)


def pass_kernel(rows, own_in, *refs):
    blocks = own_in.shape[0]
    gots, own_ref, outs = refs[:-blocks], refs[-blocks], refs[1 - blocks :]
    size = rows // SCALE_GROUPS
    for place in range(blocks):
        value = own_in[place]
        pieces = [value[g * size : (g + 1) * size] for g in range(SCALE_GROUPS)]
        for got in gots:
            tail = got[blocks * rows :, :]
            for g in range(SCALE_GROUPS):
                index = place * SCALE_GROUPS + g
                spot = place * rows + g * size
                pieces[g] = pieces[g] + unpack_part(
                    got[spot : spot + size, :], tail[index : index + 1]
                )
        if place == 0:
            for g in range(SCALE_GROUPS):
                own_ref[g * size : (g + 1) * size, :] = pieces[g]
            continue
        steps, levels = pack_part(jnp.concatenate(pieces, axis=0))
        out = outs[place - 1]
        for g, step in enumerate(steps):
            out[g * size : (g + 1) * size, :] = step.astype(jnp.int16)
        pad = jnp.zeros((out.shape[0] - rows - len(levels), DG), F32)
        tail = jnp.concatenate(levels + [pad], axis=0).astype(jnp.int32)
        out[rows:, :] = tail.astype(jnp.int16)


def final_kernel(sizes, counts, *refs):
    out_ref, square_ref = refs[-2:]
    squares = jnp.zeros((1, DG), F32)
    place = 0
    for kind, rows in enumerate(sizes):
        own_ref, *gots = refs[sum(counts[:kind]) : sum(counts[: kind + 1])]
        size = rows // SCALE_GROUPS
        for g in range(SCALE_GROUPS):
            at = slice(g * size, (g + 1) * size)
            value = own_ref[at, :]
            for got in gots:
                value = value + unpack_part(got[at, :], got[rows:, :][g : g + 1])
            out_ref[place : place + size, :] = value
            squares = squares + jnp.sum(value * value, axis=0, keepdims=True)
            place += size
    square_ref[...] = jnp.broadcast_to(jnp.sum(squares, axis=1, keepdims=True), (8, 128))


def stepped(weight, first, second, grad, rate, fix1, fix2):
    first_new = FIRST_DECAY * first + (1.0 - FIRST_DECAY) * grad
    second_new = SECOND_DECAY * second + (1.0 - SECOND_DECAY) * grad * grad
    change = (first_new * fix1) / (jnp.sqrt(second_new * fix2) + EPSILON) + WEIGHT_DECAY * weight
    return weight - rate * change, second_new


def update_kernel(fix_ref, square_ref, *refs):
    pieces = refs[:4]
    dil, pw, table = refs[4:7], refs[7:10], refs[10:13]
    norm_ref = refs[13]
    dil_hbm, pw_hbm, table_hbm = refs[14:17], refs[17:20], refs[20:23]
    dil_out, pw_out, table_out = refs[23:26], refs[26:29], refs[29:32]
    sems = refs[32]
    out_rows = dil[0].shape[1]
    small = 2 * out_rows
    time = lax.axis_index("tm")
    count = KERNEL * D * HID + D * HID + SLOTS * CODES * DG
    norm = jnp.sqrt(square_ref[...][:1, :1])
    limit = jnp.sqrt(jnp.full((1, 1), float(count), F32))
    scale = limit / jnp.maximum(norm, limit)
    norm_ref[...] = norm
    fixes = (fix_ref[0], fix_ref[1])
    copies = []
    for other in range(4):
        quarter = time ^ other
        piece = pieces[other]
        grad = piece[small:, :] * scale
        state = [v[quarter] for v in table]
        weight, second = stepped(*state, grad, RATE_CODE, *fixes)
        for kind, value in enumerate((weight, grad, second)):
            table_out[kind][quarter] = value
            copies.append(
                pltpu.make_async_copy(
                    table_out[kind].at[quarter], table_hbm[kind].at[quarter], sems.at[len(copies)]
                )
            )
            copies[-1].start()

        @pl.when(quarter < KERNEL)
        def _():
            tap = jnp.minimum(quarter, KERNEL - 1)
            for side in range(2):
                to = slice(side * DG, (side + 1) * DG)
                grad = piece[side * out_rows : (side + 1) * out_rows, :] * scale
                state = [v[tap, :, to] for v in dil]
                weight, second = stepped(*state, grad, BITRATE_FACTOR, *fixes)
                dil_out[0][tap, :, to] = weight
                dil_out[1][tap, :, to] = grad
                dil_out[2][tap, :, to] = second

        @pl.when(quarter == KERNEL)
        def _():
            grad = piece[:small, :] * scale
            weight, second = stepped(*[v[...] for v in pw], grad, BITRATE_FACTOR, *fixes)
            pw_out[0][...] = weight
            pw_out[1][...] = grad
            pw_out[2][...] = second

    for kind in range(3):
        for outs, hbms in ((dil_out, dil_hbm), (pw_out, pw_hbm)):
            copies.append(pltpu.make_async_copy(outs[kind], hbms[kind], sems.at[len(copies)]))
            copies[-1].start()
    for copy in copies:
        copy.wait()


def shards(
    features,
    cotangent,
    clip_lengths,
    code_ids,
    step_count,
    dilated_kernel_weight,
    pointwise_conv,
    codebooks,
    dilated_first_moment,
    dilated_second_moment,
    pointwise_first,
    pointwise_second,
    codebook_first,
    codebook_second,
):
    ranks, times = lax.axis_size("clip"), lax.axis_size("tm")
    rank, time = lax.axis_index("clip"), lax.axis_index("tm")
    clips, frames, _ = features.shape
    half = ranks // 2
    out_rows = HID // ranks
    block = CODES // ranks
    small = 2 * out_rows
    rows = clips * (frames + 2 * PAD)
    smem = pl.BlockSpec(memory_space=pltpu.SMEM)
    hbm = pl.BlockSpec(memory_space=pltpu.HBM)
    shape = jax.ShapeDtypeStruct

    def held(*values):
        return [pltpu.with_memory_space_constraint(v, pltpu.HBM) for v in values]

    assemble = out_rows % 16 == 0
    dil_state = [
        v.transpose(0, 2, 1)
        for v in (dilated_kernel_weight, dilated_first_moment, dilated_second_moment)
    ]
    pw_state = [v.T for v in (pointwise_conv, pointwise_first, pointwise_second)]
    table_state = [codebooks, codebook_first, codebook_second]

    if assemble:
        mine_d, mine_c = pl.pallas_call(
            prep_kernel,
            out_shape=(shape((2, small, DG), BF16), shape((block, DG), BF16)),
            in_specs=[hbm] * 3,
            out_specs=tuple(whole(2)),
            scratch_shapes=[
                pltpu.VMEM((2, out_rows, D), F32),
                pltpu.VMEM((small, DG), F32),
                pltpu.VMEM((block, DG), F32),
                pltpu.SemaphoreType.DMA((4,)),
            ],
            compiler_params=params(),
            name="prep",
        )(*held(dil_state[0], pw_state[0], codebooks))
    else:
        taps = dil_state[0].astype(BF16).reshape(KERNEL, out_rows, 2, DG).transpose(0, 2, 1, 3)
        quarters = jnp.concatenate(
            [taps.reshape(KERNEL, small, DG), pw_state[0].astype(BF16)[None]], axis=0
        )
        mine_d = jnp.take(quarters, time % 2 + jnp.array([0, 2]), axis=0)
        mine_c = lax.dynamic_index_in_dim(codebooks, time, 0, keepdims=False).astype(BF16)

    mine_c, mine_d, late_ids = lax.optimization_barrier((mine_c, mine_d, code_ids))
    near, far = pl.pallas_call(
        pack_kernel,
        out_shape=(shape((clips, 2 * PAD, 2 * D), BF16),) * 2,
        in_specs=[hbm] * 3,
        out_specs=tuple(whole(2)),
        scratch_shapes=[
            pltpu.VMEM((2, 2, clips, 2 * PAD, D), BF16),
            pltpu.VMEM(code_ids.shape, jnp.int32),
            pltpu.SemaphoreType.DMA((5,)),
        ],
        compiler_params=params(),
        name="pack",
    )(*held(features, cotangent, late_ids))
    line_c = [swap(mine_c, 2 * z, 0) for z in range(1, half)]
    across = swap(mine_d, 1, 0)
    near = lax.ppermute(near, "tm", [(i, i ^ 1) for i in range(times)])
    pairs = [(i, i + 1) for i in range(1, times - 1, 2)]
    far = lax.ppermute(far, "tm", pairs + [(b, a) for a, b in pairs])
    near, far, across, *line_c = lax.optimization_barrier((near, far, across, *line_c))
    line_c = jnp.stack([mine_c] + line_c, axis=0)
    pair_d = jnp.stack([mine_d, across], axis=0)
    line_c, pair_d, late_ids = lax.optimization_barrier((line_c, pair_d, code_ids))
    hot, hott = pl.pallas_call(
        functools.partial(own_kernel, ranks),
        out_shape=(
            shape((SLOTS, rows, CODES), BF16),
            shape((SLOTS, CODES, clips * frames), BF16),
        ),
        in_specs=whole(1),
        out_specs=tuple(whole(2)),
        compiler_params=params(8),
        name="own",
    )(late_ids)
    plane_c = [line_c, swap(line_c, 1, 0), swap(line_c, 0, 2), swap(line_c, 1, 2)]
    line_d = [pair_d] + [swap(pair_d, 2 * z, 0) for z in range(1, half)]

    start, act, cot, hot = pl.pallas_call(
        functools.partial(margin_kernel, ranks),
        out_shape=(
            shape((rows, D), F32),
            shape((rows, D), BF16),
            shape((2 * PAD * clips, D), F32),
            shape(hot.shape, BF16),
        ),
        in_specs=[smem] + whole(4),
        out_specs=tuple(whole(4)),
        input_output_aliases={4: 3},
        compiler_params=params(8),
        name="margin",
    )(clip_lengths, features, near, far, hot)

    act, *gone = lax.optimization_barrier((act, *plane_c, *line_d))
    plane_c, line_d = gone[:4], gone[4:]
    pieces_d = line_d + [swap(v, 0, 1) for v in line_d]
    turned = [swap(v, 0, 1) for v in plane_c]
    pieces_c = plane_c[:2] + turned[:2] + plane_c[2:] + turned[2:]

    weights = (shape((KERNEL * HID, D), BF16), shape((D, HID), BF16))
    given = pieces_d
    if not assemble:
        order = rank ^ jnp.arange(ranks)
        stacked = jnp.stack(pieces_d, axis=0).reshape(2, half, 2, 2, small, DG)
        stacked = jnp.take(stacked, time % 2 ^ jnp.arange(2), axis=0)
        stacked = stacked.transpose(3, 0, 1, 2, 4, 5).reshape(4, ranks, small, DG)
        stacked = jnp.take(stacked, order, axis=1)
        dil = stacked[:KERNEL].reshape(KERNEL, ranks, 2, out_rows, DG)
        dil = dil.transpose(0, 1, 3, 2, 4).reshape(KERNEL * HID, D)
        given = [dil, stacked[3].reshape(D, HID)]
    outs = pl.pallas_call(
        functools.partial(conv_kernel, ranks, assemble, clips),
        out_shape=(weights if assemble else ())
        + (shape((rows, HID), BF16), shape((rows, HID), F32), shape((rows, D), F32)),
        in_specs=whole(2 + len(given)),
        out_specs=tuple(whole(5 if assemble else 3)),
        scratch_shapes=[pltpu.VMEM((4, HID, D), BF16)] if assemble else [],
        compiler_params=params(10),
        name="conv",
    )(start, act, *given)
    dil, pwt, gated, hs, latent = tuple(outs) if assemble else tuple(given) + tuple(outs)

    quant, keep, send, bg, lg = pl.pallas_call(
        functools.partial(quant_kernel, ranks),
        out_shape=(
            shape((clips, frames, D), BF16),
            shape((2, CODES, DG), F32),
            shape((2, CODES, DG), F32),
            shape((rows, D), BF16),
            shape((clips * frames, D), F32),
        ),
        in_specs=[smem] + whole(5 + len(pieces_c)),
        out_specs=tuple(whole(5)),
        scratch_shapes=[
            pltpu.VMEM((SLOTS, CODES, DG), BF16),
            pltpu.VMEM((SLOTS, clips * frames, 2 * DG), BF16),
        ],
        compiler_params=params(16),
        name="quant",
    )(clip_lengths, latent, cotangent, cot, hot, hott, *pieces_c)

    if assemble:
        grads = (shape((2, ranks * small, DG), F32),) * 2
    else:
        grads = (shape((KERNEL, HID, D), F32), shape((D, HID), F32))
    fg, first_grad, second_grad = pl.pallas_call(
        functools.partial(backward_kernel, ranks, assemble, clips),
        out_shape=(shape((clips, frames, D), F32),) + grads,
        in_specs=[smem] + whole(8),
        out_specs=tuple(whole(3)),
        scratch_shapes=[pltpu.VMEM((4, HID, D), F32)] if assemble else [],
        compiler_params=params(16),
        name="backward",
    )(clip_lengths, start, act, gated, bg, lg, hs, dil, pwt)

    if assemble:
        keep_d, send_d = first_grad, second_grad
    else:
        parts = jnp.concatenate(
            [
                first_grad.reshape(KERNEL, ranks, out_rows, 2, DG)
                .transpose(0, 1, 3, 2, 4)
                .reshape(KERNEL, ranks, small, DG),
                second_grad.reshape(1, ranks, small, DG),
            ],
            axis=0,
        )
        seq = jnp.concatenate([jnp.arange(0, ranks, 2), jnp.arange(1, ranks, 2)])
        parts = jnp.take(jnp.take(parts, time ^ jnp.arange(4), axis=0), rank ^ seq, axis=1)
        parts = parts.reshape(2, 2, ranks * small, DG)
        keep_d, send_d = parts[:, 0], parts[:, 1]

    def sent(keep, got, groups, size, tag):
        count = len(groups[0])
        packed = count * size + count * SCALE_GROUPS
        return pl.pallas_call(
            functools.partial(send_kernel, groups, size),
            out_shape=(shape((count, size, DG), F32),)
            + (shape((packed, DG), jnp.int16),) * (len(groups) - 1),
            in_specs=whole(2),
            out_specs=tuple(whole(len(groups))),
            compiler_params=params(),
            name="send_" + tag,
        )(keep, got)

    def passed(parts, size, tag):
        count = parts[0].shape[0]
        return pl.pallas_call(
            functools.partial(pass_kernel, size),
            out_shape=(shape((size, DG), F32),)
            + (shape((size + 16, DG), jnp.int16),) * (count - 1),
            in_specs=whole(len(parts)),
            out_specs=tuple(whole(count)),
            compiler_params=params(),
            name="pass_" + tag,
        )(*parts)

    def over_plane(parts):
        return [parts[0], swap(parts[1], 1, 0), swap(parts[2], 0, 2), swap(parts[3], 1, 2)]

    def over_line(parts):
        return [parts[0]] + [swap(parts[z], 2 * z, 0) for z in range(1, half)]

    by_plane = [[(jy, x * half + z) for z in range(half)] for jy in range(2) for x in range(2)]
    by_line = [[(jy, x * half + z) for jy in range(2) for x in range(2)] for z in range(half)]
    got_c, got_d = swap(send, 0, 1), swap(send_d, 0, 1)
    parts_c = over_plane(sent(keep, got_c, by_plane, block, "codes"))
    parts_c[0], keep_d = lax.optimization_barrier((parts_c[0], keep_d))
    parts_d = over_line(sent(keep_d, got_d, by_line, small, "conv"))
    parts_c = over_line(passed(parts_c, block, "codes"))
    parts_c[1], parts_d[0] = lax.optimization_barrier((parts_c[1], parts_d[0]))
    parts_d = over_plane(passed(parts_d, small, "conv"))
    total = small + block
    piece, squared = pl.pallas_call(
        functools.partial(final_kernel, (small, block), (4, half)),
        out_shape=(shape((total, DG), F32), shape((8, 128), F32)),
        in_specs=whole(4 + half),
        out_specs=tuple(whole(2)),
        compiler_params=params(),
        name="final",
    )(*parts_d, *parts_c)

    across = swap(piece, 0, 2)
    squared = squared + swap(squared, 0, 1)
    squared = (squared + swap(squared, 1, 0)) + (swap(squared, 0, 2) + swap(squared, 1, 2))
    step = 2
    while step < ranks:
        squared = squared + swap(squared, step, 0)
        if step == 2:
            across, squared = lax.optimization_barrier((across, squared))
        step *= 2
    fours = [piece, swap(piece, 0, 1), across, swap(across, 0, 1)]
    steps = step_count[0].astype(F32)
    decays = jnp.stack([1.0 / (1.0 - FIRST_DECAY**steps), 1.0 / (1.0 - SECOND_DECAY**steps)])
    if assemble:
        state = dil_state + pw_state + table_state
        norm, *new = pl.pallas_call(
            update_kernel,
            out_shape=(shape((1, 1), F32),) + tuple(shape(v.shape, F32) for v in state),
            in_specs=[smem] + whole(14),
            out_specs=tuple(whole(1) + [hbm] * 9),
            scratch_shapes=[pltpu.VMEM(v.shape, F32) for v in state]
            + [pltpu.SemaphoreType.DMA((18,))],
            compiler_params=params(8),
            name="update",
        )(decays, squared, *fours, *state)
        norm = norm.reshape(1)
        dil_new, pw_new, table_new = new[:3], new[3:6], new[6:]
    else:
        four = jnp.take(jnp.stack(fours, axis=0), time ^ jnp.arange(4), axis=0)
        raw = four[:KERNEL, :small].reshape(KERNEL, 2, out_rows, DG)
        raw = raw.transpose(0, 2, 1, 3).reshape(KERNEL, out_rows, D)
        count = KERNEL * D * HID + D * HID + SLOTS * CODES * DG
        limit = jnp.sqrt(jnp.float32(count))
        norm = jnp.sqrt(squared[0, :1])
        scale = limit / jnp.maximum(norm[0], limit)
        new = []
        for state, grad, rate in (
            (dil_state, raw, BITRATE_FACTOR),
            (pw_state, four[3, :small], BITRATE_FACTOR),
            (table_state, four[:, small:], RATE_CODE),
        ):
            grad = grad * scale
            weight, second = stepped(*state, grad, rate, decays[0], decays[1])
            new.append((weight, grad, second))
        dil_new, pw_new, table_new = new
    return (
        quant,
        fg,
        norm,
        *[v.transpose(0, 2, 1) for v in dil_new],
        *[v.T for v in pw_new],
        *table_new,
    )


def solution(mesh):
    in_specs = (
        P("clip", "tm", None),
        P("clip", "tm", None),
        P("clip"),
        P(None, "clip", "tm"),
        P(),
        P(None, None, "clip"),
        P(None, "clip"),
        P(None, "clip", None),
        P(None, None, "clip"),
        P(None, None, "clip"),
        P(None, "clip"),
        P(None, "clip"),
        P(None, "clip", None),
        P(None, "clip", None),
    )
    out_specs = (
        P("clip", "tm", None),
        P("clip", "tm", None),
        P(),
        P(None, None, "clip"),
        P(None, None, "clip"),
        P(None, None, "clip"),
        P(None, "clip"),
        P(None, "clip"),
        P(None, "clip"),
        P(None, "clip", None),
        P(None, "clip", None),
        P(None, "clip", None),
    )
    return jax.shard_map(shards, mesh=mesh, in_specs=in_specs, out_specs=out_specs, check_vma=False)
```

```python
import functools

import jax
import jax.numpy as jnp
from jax import lax
from jax.experimental import pallas as pl
from jax.experimental.pallas import tpu as pltpu
from jax.sharding import PartitionSpec as P

D = 512
HID = 256
CODES = 1024
GROUPS = 2
LEVELS = 2
SLOTS = 4
KERNEL = 3
DILATION = 3
DG = 256
PAD = 8

COMMIT = 0.25
FIRST_DECAY = 0.9
SECOND_DECAY = 0.99
EPSILON = 1e-08
WEIGHT_DECAY = 0.01
BITRATE_FACTOR = 0.02
RATE_CODE = 0.5

F32 = jnp.float32
BF16 = jnp.bfloat16
NT = (((1,), (1,)), ((), ()))
TN = (((0,), (0,)), ((), ()))
LEVEL_STEPS = 256.0
TOP = 32000.0
SCALE_GROUPS = 4
MIB = 1024 * 1024


def params(mib=6):
    return pltpu.CompilerParams(vmem_limit_bytes=mib * MIB)


def whole(count):
    return [pl.BlockSpec(memory_space=pltpu.VMEM)] * count


def mm(a, b):
    return jnp.dot(a, b, preferred_element_type=F32)


def mmg(a, b, dims):
    return lax.dot_general(a, b, dims, preferred_element_type=F32)


def slope(v):
    return jnp.where(v > 0, 1.0, jnp.exp(jnp.minimum(v, 0.0)))


def elu(v):
    return jnp.where(v > 0, v, jnp.exp(jnp.minimum(v, 0.0)) - 1.0)


def swap(value, clip_mask, time_mask):
    clips, times = lax.axis_size("clip"), lax.axis_size("tm")
    pairs = [
        (c * times + t, (c ^ clip_mask) * times + (t ^ time_mask))
        for c in range(clips)
        for t in range(times)
    ]
    return lax.ppermute(value, ("clip", "tm"), pairs)


def prep_kernel(dil_hbm, pw_hbm, table_hbm, conv_ref, code_ref, dil_ref, pw_ref, table_ref, sems):
    time = lax.axis_index("tm")
    bit = time % 2
    out_rows = pw_ref.shape[0] // 2
    second = jnp.minimum(2 + bit, KERNEL - 1)
    copies = [
        pltpu.make_async_copy(table_hbm.at[time], table_ref, sems.at[0]),
        pltpu.make_async_copy(dil_hbm.at[bit], dil_ref.at[0], sems.at[1]),
        pltpu.make_async_copy(dil_hbm.at[second], dil_ref.at[1], sems.at[2]),
        pltpu.make_async_copy(pw_hbm, pw_ref, sems.at[3]),
    ]
    for copy in copies:
        copy.start()
    copies[0].wait()
    code_ref[...] = table_ref[...].astype(BF16)
    for copy in copies[1:]:
        copy.wait()
    for side in range(2):
        for part in range(2):
            conv_ref[part, side * out_rows : (side + 1) * out_rows, :] = dil_ref[
                part, :, side * DG : (side + 1) * DG
            ].astype(BF16)

    @pl.when(bit == 1)
    def _():
        conv_ref[1] = pw_ref[...].astype(BF16)


def renamed(values, ranks):
    block = CODES // ranks
    step = (values // block) ^ lax.axis_index("clip")
    place = (step % 2) * (ranks // 2) + step // 2
    return place * block + values % block


def masks(clips, frames, len_ref, columns):
    base = lax.axis_index("tm") * frames

    def mark(first, count, clip):
        where = lax.broadcasted_iota(jnp.int32, (count, columns), 0) + first
        return jnp.where((where >= 0) & (where < len_ref[clip]), 1.0, 0.0)

    own = [mark(base, frames, c) for c in range(clips)]
    margins = [
        mark(first, PAD, c) for c in range(clips) for first in (base - PAD, base + frames)
    ]
    return jnp.concatenate(own + margins, axis=0)


def widened(value, clip, clips, frames):
    at = clips * frames + 2 * PAD * clip
    return jnp.concatenate(
        [
            value[at : at + PAD],
            value[clip * frames : (clip + 1) * frames],
            value[at + PAD : at + 2 * PAD],
        ],
        axis=0,
    )


def pack_kernel(f_hbm, c_hbm, ids_hbm, near_ref, far_ref, buf, ids_ref, sems):
    clips, frames, _ = f_hbm.shape
    edge = 2 * PAD
    odd = lax.axis_index("tm") % 2
    copies = [pltpu.make_async_copy(ids_hbm, ids_ref, sems.at[4])]
    for kind, source in enumerate((f_hbm, c_hbm)):
        for side, at in enumerate((frames - edge, 0)):
            copies.append(
                pltpu.make_async_copy(
                    source.at[:, pl.ds(at, edge), :], buf.at[kind, side], sems.at[2 * kind + side]
                )
            )
    for copy in copies:
        copy.start()
    for copy in copies:
        copy.wait()
    outs = []
    for side in range(2):
        at = slice(PAD, 2 * PAD) if side == 0 else slice(0, PAD)
        parts = []
        for c in range(clips):
            ids = ids_ref[:, c, :]
            if side == 0:
                ids = pltpu.roll(ids, PAD, 1)
            both = jnp.concatenate([ids // 32, ids % 32], axis=0).astype(F32)
            both = jnp.concatenate([both, jnp.zeros((8, 2 * D - frames), F32)], axis=1)
            ends = [buf[kind, side, c].astype(F32)[at] for kind in range(2)]
            parts.append(jnp.concatenate([jnp.concatenate(ends, axis=1), both], axis=0))
        outs.append(parts)
    for c in range(clips):
        last, first = outs[0][c], outs[1][c]
        near_ref[c] = jnp.where(odd == 1, first, last).astype(BF16)
        far_ref[c] = jnp.where(odd == 1, last, first).astype(BF16)


def own_kernel(ranks, ids_ref, hot_ref, hott_ref):
    _, clips, frames = ids_ref.shape
    codes = lax.broadcasted_iota(jnp.int32, (frames, CODES), 1)
    spots = lax.broadcasted_iota(jnp.int32, (CODES, frames), 0)
    for c in range(clips):
        ids = renamed(ids_ref[:, c, :], ranks)
        turned = jnp.concatenate([ids.astype(F32), jnp.zeros((8 - SLOTS, frames), F32)], axis=0)
        turned = turned.T.astype(jnp.int32)
        at = slice(c * frames, (c + 1) * frames)
        for slot in range(SLOTS):
            hot_ref[slot, at, :] = jnp.where(codes == turned[:, slot : slot + 1], 1.0, 0.0).astype(
                BF16
            )
            hott_ref[slot, :, at] = jnp.where(spots == ids[slot : slot + 1], 1.0, 0.0).astype(BF16)
    hot_ref[:, clips * frames :, :] = jnp.zeros((SLOTS, 2 * PAD * clips, CODES), BF16)


def margin_kernel(ranks, len_ref, f_ref, near_ref, far_ref, old_ref, start_ref, act_ref, cot_ref, hot_ref):
    del old_ref
    clips, frames, _ = f_ref.shape
    odd = lax.axis_index("tm") % 2
    both = []
    for c in range(clips):
        near, far = near_ref[c].astype(F32), far_ref[c].astype(F32)
        both += [jnp.where(odd == 1, near, far), jnp.where(odd == 1, far, near)]
    start = masks(clips, frames, len_ref, D) * jnp.concatenate(
        [f_ref[c].astype(F32) for c in range(clips)] + [part[:PAD, :D] for part in both], axis=0
    )
    start_ref[...] = start
    act_ref[...] = elu(start).astype(BF16)
    cot_ref[...] = jnp.concatenate([part[:PAD, D:] for part in both], axis=0)
    turned = jnp.concatenate([part[PAD:, :128].T[:PAD] for part in both], axis=0)
    ids = renamed((turned[:, :SLOTS] * 32.0 + turned[:, SLOTS : 2 * SLOTS]).astype(jnp.int32), ranks)
    codes = lax.broadcasted_iota(jnp.int32, (2 * PAD * clips, CODES), 1)
    for slot in range(SLOTS):
        hot_ref[slot, clips * frames :, :] = jnp.where(
            codes == ids[:, slot : slot + 1], 1.0, 0.0
        ).astype(BF16)


def assembled(ranks, pieces, d_ref, pwt_ref, all_ref):
    half, small = ranks // 2, 2 * HID // ranks
    out_rows = small // 2
    bit, rank = lax.axis_index("tm") % 2, lax.axis_index("clip")
    for other in range(2):
        for z in range(half):
            piece = pieces[other * half + z]
            for x in range(2):
                at = pl.multiple_of((rank ^ (2 * z + x)) * out_rows, out_rows)
                for part in range(2):
                    for side in range(2):
                        all_ref[
                            2 * part + (bit ^ other),
                            pl.ds(at, out_rows),
                            side * DG : (side + 1) * DG,
                        ] = piece[x, part, side * out_rows : (side + 1) * out_rows, :]
    for tap in range(KERNEL):
        d_ref[tap * HID : (tap + 1) * HID, :] = all_ref[tap]
    for r in range(ranks):
        for side in range(2):
            to = r * small + side * out_rows
            pwt_ref[to : to + out_rows, :] = all_ref[
                KERNEL, r * out_rows : (r + 1) * out_rows, side * DG : (side + 1) * DG
            ]


def conv_kernel(ranks, assemble, clips, start_ref, act_ref, *refs):
    if assemble:
        pieces, refs = refs[:ranks], refs[ranks:]
        d_ref, pwt_ref, gated_ref, hs_ref, latent_ref, all_ref = refs
        assembled(ranks, pieces, d_ref, pwt_ref, all_ref)
    else:
        d_ref, pwt_ref, gated_ref, hs_ref, latent_ref = refs
    rows = start_ref.shape[0]
    taps = mmg(act_ref[...], d_ref[...], NT)
    frames = rows // clips - 2 * PAD
    span = frames + 2 * PAD
    own, margins = [], []
    for c in range(clips):
        wide = widened(taps, c, clips, frames)
        part = (
            pltpu.roll(wide[:, :HID], DILATION, 0)
            + wide[:, HID : 2 * HID]
            + pltpu.roll(wide[:, 2 * HID :], span - DILATION, 0)
        )
        own.append(part[PAD : PAD + frames])
        margins += [part[:PAD], part[PAD + frames :]]
    hidden = jnp.concatenate(own + margins, axis=0)
    hs_ref[...] = slope(hidden)
    gated = elu(hidden).astype(BF16)
    gated_ref[...] = gated
    latent_ref[...] = start_ref[...] + mmg(gated, pwt_ref[...], NT)


def quant_kernel(ranks, len_ref, latent_ref, c_ref, cot_ref, hot_ref, hott_ref, *refs):
    half, block = ranks // 2, CODES // ranks
    pieces, refs = refs[:8], refs[8:]
    quant_ref, send_ref, bg_ref, lg_ref, cgs_ref, tab_ref = refs
    clips, frames, _ = c_ref.shape
    time = lax.axis_index("tm")
    mask = masks(clips, frames, len_ref, DG)
    local = clips * frames
    twice = 2.0 * mask[:local]
    for other in range(SLOTS):
        slot = time ^ other
        for x in range(2):
            for z in range(half):
                spot = (x * half + z) * block
                tab_ref[slot, spot : spot + block, :] = pieces[2 * other + x][z]
    for group in range(GROUPS):
        at = slice(group * DG, (group + 1) * DG)
        first = mm(hot_ref[2 * group], tab_ref[2 * group])
        second = mm(hot_ref[2 * group + 1], tab_ref[2 * group + 1])
        cot = jnp.concatenate(
            [c_ref[c, :, at].astype(F32) for c in range(clips)] + [cot_ref[:, at]], axis=0
        )
        residual = latent_ref[:, at]
        gap = residual - first
        gap2 = gap - second
        grad = mask * (cot + 2.0 * COMMIT * (gap + gap2))
        quant = (mask * (first + second))[:local].astype(BF16)
        bg_ref[:, at] = grad.astype(BF16)
        lg_ref[:, at] = grad[:local]
        for clip in range(clips):
            quant_ref[clip, :, at] = quant[clip * frames : (clip + 1) * frames]
        for level, diff in ((0, gap), (1, gap2)):
            code_grad = -(twice * diff[:local])
            high = code_grad.astype(BF16)
            cgs_ref[2 * group + level, :, :DG] = high
            cgs_ref[2 * group + level, :, DG:] = (code_grad - high.astype(F32)).astype(BF16)
    scattered(1, hott_ref, cgs_ref, send_ref)


def scattered(bit, hott_ref, cgs_ref, out_ref):
    time = lax.axis_index("tm")
    for far in range(2):
        slot = time ^ (2 * far + bit)
        pair = mm(hott_ref[slot], cgs_ref[slot])
        out_ref[far] = pair[:, :DG] + pair[:, DG:]


def keep_kernel(hott_ref, cgs_ref, keep_ref):
    scattered(0, hott_ref, cgs_ref, keep_ref)


def backward_kernel(
    ranks,
    assemble,
    clips,
    len_ref,
    start_ref,
    act_ref,
    gated_ref,
    bg_ref,
    lg_ref,
    hs_ref,
    d_ref,
    pwt_ref,
    fg_ref,
    *outs,
):
    rows = start_ref.shape[0]
    span = rows // clips
    frames = span - 2 * PAD
    local = clips * frames
    bg = bg_ref[...]
    hidden_grad = (mm(bg, pwt_ref[...]) * hs_ref[...]).astype(BF16)
    mine = hidden_grad[:local]
    pw_grad = mmg(bg[:local], gated_ref[:local, :], TN)

    def moved(value, shift):
        return jnp.concatenate(
            [
                pltpu.roll(widened(value, c, clips, frames), shift % span, 0)[PAD : PAD + frames]
                for c in range(clips)
            ],
            axis=0,
        ).astype(BF16)

    act = act_ref[...].astype(F32)
    windows = [moved(act, DILATION), act_ref[:local, :], moved(act, -DILATION)]
    dil_grads = [mmg(mine, windows[tap], TN) for tap in range(KERNEL)]
    if assemble:
        keep_ref, send_ref, all_ref = outs
        half, small = ranks // 2, 2 * HID // ranks
        out_rows = small // 2
        time, rank = lax.axis_index("tm"), lax.axis_index("clip")
        for tap in range(KERNEL):
            all_ref[tap] = dil_grads[tap]
        for r in range(ranks):
            for side in range(2):
                at = r * small + side * out_rows
                all_ref[KERNEL, r * out_rows : (r + 1) * out_rows, side * DG : (side + 1) * DG] = (
                    pw_grad[at : at + out_rows]
                )
        for other in range(4):
            out = (keep_ref, send_ref)[other % 2]
            for x in range(2):
                for z in range(half):
                    at = pl.multiple_of((rank ^ (2 * z + x)) * out_rows, out_rows)
                    to = (x * half + z) * small
                    for side in range(2):
                        out[other // 2, to + side * out_rows : to + (side + 1) * out_rows, :] = (
                            all_ref[
                                time ^ other, pl.ds(at, out_rows), side * DG : (side + 1) * DG
                            ]
                        )
    else:
        dil_ref, pw_ref = outs
        for tap in range(KERNEL):
            dil_ref[tap] = dil_grads[tap]
        pw_ref[...] = pw_grad
    wide = hidden_grad.astype(F32)
    shifted = jnp.concatenate([moved(wide, -DILATION), mine, moved(wide, DILATION)], axis=1)
    act_grad = mm(shifted, d_ref[...])
    row = lax.broadcasted_iota(jnp.int32, (frames, D), 0) + lax.axis_index("tm") * frames
    for c in range(clips):
        to = slice(c * frames, (c + 1) * frames)
        mask = jnp.where(row < len_ref[c], 1.0, 0.0)
        start = start_ref[to, :]
        fg_ref[c] = mask * (lg_ref[to, :] + slope(start) * act_grad[to])


def pack_part(value):
    count = SCALE_GROUPS
    rows = value.shape[0]
    size = rows // count
    steps, levels = [], []
    for group in range(count):
        part = value[group * size : (group + 1) * size]
        top = jnp.maximum(jnp.max(jnp.abs(part), axis=0, keepdims=True), 1e-30)
        level = jnp.ceil(jnp.log2(top) * LEVEL_STEPS)
        scale = jnp.exp2(level / -LEVEL_STEPS) * TOP
        steps.append(jnp.round(part * scale).astype(jnp.int32))
        levels.append(level)
    return steps, levels


def unpack_part(steps, level):
    return steps.astype(jnp.int32).astype(F32) * (
        jnp.exp2(level.astype(jnp.int32).astype(F32) / LEVEL_STEPS) / TOP
    )


def send_kernel(groups, rows, keep_ref, got_ref, own_ref, *outs):
    size = rows // SCALE_GROUPS
    for part, blocks in enumerate(groups):
        levels = []
        for place, (jy, start) in enumerate(blocks):
            at = slice(start * rows, (start + 1) * rows)
            value = keep_ref[jy, at, :] + got_ref[jy, at, :]
            if part == 0:
                own_ref[place] = value
                continue
            steps, more = pack_part(value)
            for group, step in enumerate(steps):
                spot = place * rows + group * size
                outs[part - 1][spot : spot + size, :] = step.astype(jnp.int16)
            levels += more
        if part:
            tail = jnp.concatenate(levels, axis=0).astype(jnp.int32)
            outs[part - 1][len(blocks) * rows :, :] = tail.astype(jnp.int16)


def pass_kernel(rows, own_in, *refs):
    blocks = own_in.shape[0]
    gots, own_ref, outs = refs[:-blocks], refs[-blocks], refs[1 - blocks :]
    size = rows // SCALE_GROUPS
    for place in range(blocks):
        value = own_in[place]
        pieces = [value[g * size : (g + 1) * size] for g in range(SCALE_GROUPS)]
        for got in gots:
            tail = got[blocks * rows :, :]
            for g in range(SCALE_GROUPS):
                index = place * SCALE_GROUPS + g
                spot = place * rows + g * size
                pieces[g] = pieces[g] + unpack_part(
                    got[spot : spot + size, :], tail[index : index + 1]
                )
        if place == 0:
            for g in range(SCALE_GROUPS):
                own_ref[g * size : (g + 1) * size, :] = pieces[g]
            continue
        steps, levels = pack_part(jnp.concatenate(pieces, axis=0))
        out = outs[place - 1]
        for g, step in enumerate(steps):
            out[g * size : (g + 1) * size, :] = step.astype(jnp.int16)
        pad = jnp.zeros((out.shape[0] - rows - len(levels), DG), F32)
        tail = jnp.concatenate(levels + [pad], axis=0).astype(jnp.int32)
        out[rows:, :] = tail.astype(jnp.int16)


def final_kernel(sizes, counts, *refs):
    out_ref, square_ref = refs[-2:]
    squares = jnp.zeros((1, DG), F32)
    place = 0
    for kind, rows in enumerate(sizes):
        own_ref, *gots = refs[sum(counts[:kind]) : sum(counts[: kind + 1])]
        size = rows // SCALE_GROUPS
        for g in range(SCALE_GROUPS):
            at = slice(g * size, (g + 1) * size)
            value = own_ref[at, :]
            for got in gots:
                value = value + unpack_part(got[at, :], got[rows:, :][g : g + 1])
            out_ref[place : place + size, :] = value
            squares = squares + jnp.sum(value * value, axis=0, keepdims=True)
            place += size
    square = jnp.sum(squares, axis=1, keepdims=True)
    square_ref[...] = jnp.broadcast_to(square[None], square_ref.shape)


def stepped(weight, first, second, grad, rate, fix1, fix2):
    first_new = FIRST_DECAY * first + (1.0 - FIRST_DECAY) * grad
    second_new = SECOND_DECAY * second + (1.0 - SECOND_DECAY) * grad * grad
    change = (first_new * fix1) / (jnp.sqrt(second_new * fix2) + EPSILON) + WEIGHT_DECAY * weight
    return weight - rate * change, second_new


def update_kernel(fix_ref, square_ref, *refs):
    pieces = refs[:4]
    dil, pw, table = refs[4:7], refs[7:10], refs[10:13]
    norm_ref = refs[13]
    dil_hbm, pw_hbm, table_hbm = refs[14:17], refs[17:20], refs[20:23]
    dil_out, pw_out, table_out = refs[23:26], refs[26:29], refs[29:32]
    sems = refs[32]
    out_rows = dil[0].shape[1]
    small = 2 * out_rows
    time = lax.axis_index("tm")
    count = KERNEL * D * HID + D * HID + SLOTS * CODES * DG
    norm = jnp.sqrt(jnp.sum(square_ref[...], axis=0)[:1, :1])
    limit = jnp.sqrt(jnp.full((1, 1), float(count), F32))
    scale = limit / jnp.maximum(norm, limit)
    norm_ref[...] = norm
    fixes = (fix_ref[0], fix_ref[1])
    copies = []
    for other in range(4):
        quarter = time ^ other
        piece = pieces[other]
        grad = piece[small:, :] * scale
        state = [v[quarter] for v in table]
        weight, second = stepped(*state, grad, RATE_CODE, *fixes)
        for kind, value in enumerate((weight, grad, second)):
            table_out[kind][quarter] = value
            copies.append(
                pltpu.make_async_copy(
                    table_out[kind].at[quarter], table_hbm[kind].at[quarter], sems.at[len(copies)]
                )
            )
            copies[-1].start()

        @pl.when(quarter < KERNEL)
        def _():
            tap = jnp.minimum(quarter, KERNEL - 1)
            for side in range(2):
                to = slice(side * DG, (side + 1) * DG)
                grad = piece[side * out_rows : (side + 1) * out_rows, :] * scale
                state = [v[tap, :, to] for v in dil]
                weight, second = stepped(*state, grad, BITRATE_FACTOR, *fixes)
                dil_out[0][tap, :, to] = weight
                dil_out[1][tap, :, to] = grad
                dil_out[2][tap, :, to] = second

        @pl.when(quarter == KERNEL)
        def _():
            grad = piece[:small, :] * scale
            weight, second = stepped(*[v[...] for v in pw], grad, BITRATE_FACTOR, *fixes)
            pw_out[0][...] = weight
            pw_out[1][...] = grad
            pw_out[2][...] = second

    for kind in range(3):
        for outs, hbms in ((dil_out, dil_hbm), (pw_out, pw_hbm)):
            copies.append(pltpu.make_async_copy(outs[kind], hbms[kind], sems.at[len(copies)]))
            copies[-1].start()
    for copy in copies:
        copy.wait()


def shards(
    features,
    cotangent,
    clip_lengths,
    code_ids,
    step_count,
    dilated_kernel_weight,
    pointwise_conv,
    codebooks,
    dilated_first_moment,
    dilated_second_moment,
    pointwise_first,
    pointwise_second,
    codebook_first,
    codebook_second,
):
    ranks, times = lax.axis_size("clip"), lax.axis_size("tm")
    rank, time = lax.axis_index("clip"), lax.axis_index("tm")
    clips, frames, _ = features.shape
    half = ranks // 2
    out_rows = HID // ranks
    block = CODES // ranks
    small = 2 * out_rows
    rows = clips * (frames + 2 * PAD)
    smem = pl.BlockSpec(memory_space=pltpu.SMEM)
    hbm = pl.BlockSpec(memory_space=pltpu.HBM)
    shape = jax.ShapeDtypeStruct

    def held(*values):
        return [pltpu.with_memory_space_constraint(v, pltpu.HBM) for v in values]

    assemble = out_rows % 16 == 0
    dil_state = [
        v.transpose(0, 2, 1)
        for v in (dilated_kernel_weight, dilated_first_moment, dilated_second_moment)
    ]
    pw_state = [v.T for v in (pointwise_conv, pointwise_first, pointwise_second)]
    table_state = [codebooks, codebook_first, codebook_second]

    if assemble:
        mine_d, mine_c = pl.pallas_call(
            prep_kernel,
            out_shape=(shape((2, small, DG), BF16), shape((block, DG), BF16)),
            in_specs=[hbm] * 3,
            out_specs=tuple(whole(2)),
            scratch_shapes=[
                pltpu.VMEM((2, out_rows, D), F32),
                pltpu.VMEM((small, DG), F32),
                pltpu.VMEM((block, DG), F32),
                pltpu.SemaphoreType.DMA((4,)),
            ],
            compiler_params=params(),
            name="prep",
        )(*held(dil_state[0], pw_state[0], codebooks))
    else:
        taps = dil_state[0].astype(BF16).reshape(KERNEL, out_rows, 2, DG).transpose(0, 2, 1, 3)
        quarters = jnp.concatenate(
            [taps.reshape(KERNEL, small, DG), pw_state[0].astype(BF16)[None]], axis=0
        )
        mine_d = jnp.take(quarters, time % 2 + jnp.array([0, 2]), axis=0)
        mine_c = lax.dynamic_index_in_dim(codebooks, time, 0, keepdims=False).astype(BF16)

    mine_c, mine_d, late_ids = lax.optimization_barrier((mine_c, mine_d, code_ids))
    near, far = pl.pallas_call(
        pack_kernel,
        out_shape=(shape((clips, 2 * PAD, 2 * D), BF16),) * 2,
        in_specs=[hbm] * 3,
        out_specs=tuple(whole(2)),
        scratch_shapes=[
            pltpu.VMEM((2, 2, clips, 2 * PAD, D), BF16),
            pltpu.VMEM(code_ids.shape, jnp.int32),
            pltpu.SemaphoreType.DMA((5,)),
        ],
        compiler_params=params(),
        name="pack",
    )(*held(features, cotangent, late_ids))
    line_c = [swap(mine_c, 2 * z, 0) for z in range(1, half)]
    across = swap(mine_d, 1, 0)
    near = lax.ppermute(near, "tm", [(i, i ^ 1) for i in range(times)])
    pairs = [(i, i + 1) for i in range(1, times - 1, 2)]
    far = lax.ppermute(far, "tm", pairs + [(b, a) for a, b in pairs])
    near, far, *line_c = lax.optimization_barrier((near, far, *line_c))
    line_c = jnp.stack([mine_c] + line_c, axis=0)
    pair_d = jnp.stack([mine_d, across], axis=0)
    line_c, late_ids = lax.optimization_barrier((line_c, code_ids))
    hot, hott = pl.pallas_call(
        functools.partial(own_kernel, ranks),
        out_shape=(
            shape((SLOTS, rows, CODES), BF16),
            shape((SLOTS, CODES, clips * frames), BF16),
        ),
        in_specs=whole(1),
        out_specs=tuple(whole(2)),
        compiler_params=params(8),
        name="own",
    )(late_ids)
    plane_c = [line_c, swap(line_c, 1, 0), swap(line_c, 0, 2), swap(line_c, 1, 2)]
    line_d = [pair_d] + [swap(pair_d, 2 * z, 0) for z in range(1, half)]

    start, act, cot, hot = pl.pallas_call(
        functools.partial(margin_kernel, ranks),
        out_shape=(
            shape((rows, D), F32),
            shape((rows, D), BF16),
            shape((2 * PAD * clips, D), F32),
            shape(hot.shape, BF16),
        ),
        in_specs=[smem] + whole(4),
        out_specs=tuple(whole(4)),
        input_output_aliases={4: 3},
        compiler_params=params(8),
        name="margin",
    )(clip_lengths, features, near, far, hot)

    act, *line_d = lax.optimization_barrier((act, *line_d))
    pieces_d = line_d + [swap(v, 0, 1) for v in line_d]
    turned = [swap(v, 0, 1) for v in plane_c]
    pieces_c = plane_c[:2] + turned[:2] + plane_c[2:] + turned[2:]

    weights = (shape((KERNEL * HID, D), BF16), shape((D, HID), BF16))
    given = pieces_d
    if not assemble:
        order = rank ^ jnp.arange(ranks)
        stacked = jnp.stack(pieces_d, axis=0).reshape(2, half, 2, 2, small, DG)
        stacked = jnp.take(stacked, time % 2 ^ jnp.arange(2), axis=0)
        stacked = stacked.transpose(3, 0, 1, 2, 4, 5).reshape(4, ranks, small, DG)
        stacked = jnp.take(stacked, order, axis=1)
        dil = stacked[:KERNEL].reshape(KERNEL, ranks, 2, out_rows, DG)
        dil = dil.transpose(0, 1, 3, 2, 4).reshape(KERNEL * HID, D)
        given = [dil, stacked[3].reshape(D, HID)]
    outs = pl.pallas_call(
        functools.partial(conv_kernel, ranks, assemble, clips),
        out_shape=(weights if assemble else ())
        + (shape((rows, HID), BF16), shape((rows, HID), F32), shape((rows, D), F32)),
        in_specs=whole(2 + len(given)),
        out_specs=tuple(whole(5 if assemble else 3)),
        scratch_shapes=[pltpu.VMEM((4, HID, D), BF16)] if assemble else [],
        compiler_params=params(10),
        name="conv",
    )(start, act, *given)
    dil, pwt, gated, hs, latent = tuple(outs) if assemble else tuple(given) + tuple(outs)

    quant, send, bg, lg, cgs = pl.pallas_call(
        functools.partial(quant_kernel, ranks),
        out_shape=(
            shape((clips, frames, D), BF16),
            shape((2, CODES, DG), F32),
            shape((rows, D), BF16),
            shape((clips * frames, D), F32),
            shape((SLOTS, clips * frames, 2 * DG), BF16),
        ),
        in_specs=[smem] + whole(5 + len(pieces_c)),
        out_specs=tuple(whole(5)),
        scratch_shapes=[
            pltpu.VMEM((SLOTS, CODES, DG), BF16),
        ],
        compiler_params=params(16),
        name="quant",
    )(clip_lengths, latent, cotangent, cot, hot, hott, *pieces_c)

    keep = pl.pallas_call(
        keep_kernel,
        out_shape=shape((2, CODES, DG), F32),
        in_specs=whole(2),
        out_specs=whole(1)[0],
        compiler_params=params(8),
        name="keep",
    )(hott, cgs)

    if assemble:
        grads = (shape((2, ranks * small, DG), F32),) * 2
    else:
        grads = (shape((KERNEL, HID, D), F32), shape((D, HID), F32))
    fg, first_grad, second_grad = pl.pallas_call(
        functools.partial(backward_kernel, ranks, assemble, clips),
        out_shape=(shape((clips, frames, D), F32),) + grads,
        in_specs=[smem] + whole(8),
        out_specs=tuple(whole(3)),
        scratch_shapes=[pltpu.VMEM((4, HID, D), F32)] if assemble else [],
        compiler_params=params(16),
        name="backward",
    )(clip_lengths, start, act, gated, bg, lg, hs, dil, pwt)

    if assemble:
        keep_d, send_d = first_grad, second_grad
    else:
        parts = jnp.concatenate(
            [
                first_grad.reshape(KERNEL, ranks, out_rows, 2, DG)
                .transpose(0, 1, 3, 2, 4)
                .reshape(KERNEL, ranks, small, DG),
                second_grad.reshape(1, ranks, small, DG),
            ],
            axis=0,
        )
        seq = jnp.concatenate([jnp.arange(0, ranks, 2), jnp.arange(1, ranks, 2)])
        parts = jnp.take(jnp.take(parts, time ^ jnp.arange(4), axis=0), rank ^ seq, axis=1)
        parts = parts.reshape(2, 2, ranks * small, DG)
        keep_d, send_d = parts[:, 0], parts[:, 1]

    def sent(keep, got, groups, size, tag):
        count = len(groups[0])
        packed = count * size + count * SCALE_GROUPS
        return pl.pallas_call(
            functools.partial(send_kernel, groups, size),
            out_shape=(shape((count, size, DG), F32),)
            + (shape((packed, DG), jnp.int16),) * (len(groups) - 1),
            in_specs=whole(2),
            out_specs=tuple(whole(len(groups))),
            compiler_params=params(),
            name="send_" + tag,
        )(keep, got)

    def passed(parts, size, tag):
        count = parts[0].shape[0]
        return pl.pallas_call(
            functools.partial(pass_kernel, size),
            out_shape=(shape((size, DG), F32),)
            + (shape((size + 16, DG), jnp.int16),) * (count - 1),
            in_specs=whole(len(parts)),
            out_specs=tuple(whole(count)),
            compiler_params=params(),
            name="pass_" + tag,
        )(*parts)

    def over_plane(parts):
        return [parts[0], swap(parts[1], 1, 0), swap(parts[2], 0, 2), swap(parts[3], 1, 2)]

    def over_line(parts):
        return [parts[0]] + [swap(parts[z], 2 * z, 0) for z in range(1, half)]

    by_plane = [[(jy, x * half + z) for z in range(half)] for jy in range(2) for x in range(2)]
    by_line = [[(jy, x * half + z) for jy in range(2) for x in range(2)] for z in range(half)]
    got_c, got_d = swap(send, 0, 1), swap(send_d, 0, 1)
    parts_c = over_plane(sent(keep, got_c, by_plane, block, "codes"))
    parts_c[0], keep_d = lax.optimization_barrier((parts_c[0], keep_d))
    parts_d = over_line(sent(keep_d, got_d, by_line, small, "conv"))
    parts_c = over_line(passed(parts_c, block, "codes"))
    parts_c[1], parts_d[0] = lax.optimization_barrier((parts_c[1], parts_d[0]))
    parts_d = over_plane(passed(parts_d, small, "conv"))
    total = small + block
    piece, squares = pl.pallas_call(
        functools.partial(final_kernel, (small, block), (4, half)),
        out_shape=(shape((total, DG), F32), shape((ranks * times, 8, 128), F32)),
        in_specs=whole(4 + half),
        out_specs=tuple(whole(2)),
        compiler_params=params(),
        name="final",
    )(*parts_d, *parts_c)

    across = swap(piece, 0, 2)
    squares = lax.all_to_all(squares, ("clip", "tm"), 0, 0, tiled=True)
    fours = [piece, swap(piece, 0, 1), across, swap(across, 0, 1)]
    steps = step_count[0].astype(F32)
    decays = jnp.stack([1.0 / (1.0 - FIRST_DECAY**steps), 1.0 / (1.0 - SECOND_DECAY**steps)])
    if assemble:
        state = dil_state + pw_state + table_state
        norm, *new = pl.pallas_call(
            update_kernel,
            out_shape=(shape((1, 1), F32),) + tuple(shape(v.shape, F32) for v in state),
            in_specs=[smem] + whole(14),
            out_specs=tuple(whole(1) + [hbm] * 9),
            scratch_shapes=[pltpu.VMEM(v.shape, F32) for v in state]
            + [pltpu.SemaphoreType.DMA((18,))],
            compiler_params=params(8),
            name="update",
        )(decays, squares, *fours, *state)
        norm = norm.reshape(1)
        dil_new, pw_new, table_new = new[:3], new[3:6], new[6:]
    else:
        four = jnp.take(jnp.stack(fours, axis=0), time ^ jnp.arange(4), axis=0)
        raw = four[:KERNEL, :small].reshape(KERNEL, 2, out_rows, DG)
        raw = raw.transpose(0, 2, 1, 3).reshape(KERNEL, out_rows, D)
        count = KERNEL * D * HID + D * HID + SLOTS * CODES * DG
        limit = jnp.sqrt(jnp.float32(count))
        norm = jnp.sqrt(jnp.sum(squares, axis=0)[0, :1])
        scale = limit / jnp.maximum(norm[0], limit)
        new = []
        for state, grad, rate in (
            (dil_state, raw, BITRATE_FACTOR),
            (pw_state, four[3, :small], BITRATE_FACTOR),
            (table_state, four[:, small:], RATE_CODE),
        ):
            grad = grad * scale
            weight, second = stepped(*state, grad, rate, decays[0], decays[1])
            new.append((weight, grad, second))
        dil_new, pw_new, table_new = new
    return (
        quant,
        fg,
        norm,
        *[v.transpose(0, 2, 1) for v in dil_new],
        *[v.T for v in pw_new],
        *table_new,
    )


def solution(mesh):
    in_specs = (
        P("clip", "tm", None),
        P("clip", "tm", None),
        P("clip"),
        P(None, "clip", "tm"),
        P(),
        P(None, None, "clip"),
        P(None, "clip"),
        P(None, "clip", None),
        P(None, None, "clip"),
        P(None, None, "clip"),
        P(None, "clip"),
        P(None, "clip"),
        P(None, "clip", None),
        P(None, "clip", None),
    )
    out_specs = (
        P("clip", "tm", None),
        P("clip", "tm", None),
        P(),
        P(None, None, "clip"),
        P(None, None, "clip"),
        P(None, None, "clip"),
        P(None, "clip"),
        P(None, "clip"),
        P(None, "clip"),
        P(None, "clip", None),
        P(None, "clip", None),
        P(None, "clip", None),
    )
    return jax.shard_map(shards, mesh=mesh, in_specs=in_specs, out_specs=out_specs, check_vma=False)
```

```python
import functools

import jax
import jax.numpy as jnp
from jax import lax
from jax.experimental import pallas as pl
from jax.experimental.pallas import tpu as pltpu
from jax.sharding import PartitionSpec as P

D = 512
HID = 256
CODES = 1024
GROUPS = 2
LEVELS = 2
SLOTS = 4
KERNEL = 3
DILATION = 3
DG = 256
PAD = 8

COMMIT = 0.25
FIRST_DECAY = 0.9
SECOND_DECAY = 0.99
EPSILON = 1e-08
WEIGHT_DECAY = 0.01
BITRATE_FACTOR = 0.02
RATE_CODE = 0.5

F32 = jnp.float32
BF16 = jnp.bfloat16
NT = (((1,), (1,)), ((), ()))
TN = (((0,), (0,)), ((), ()))
LEVEL_STEPS = 256.0
TOP = 32000.0
SCALE_GROUPS = 4
MIB = 1024 * 1024


def params(mib=6):
    return pltpu.CompilerParams(vmem_limit_bytes=mib * MIB)


def whole(count):
    return [pl.BlockSpec(memory_space=pltpu.VMEM)] * count


def mm(a, b):
    return jnp.dot(a, b, preferred_element_type=F32)


def mmg(a, b, dims):
    return lax.dot_general(a, b, dims, preferred_element_type=F32)


def slope(v):
    return jnp.where(v > 0, 1.0, jnp.exp(jnp.minimum(v, 0.0)))


def elu(v):
    return jnp.where(v > 0, v, jnp.exp(jnp.minimum(v, 0.0)) - 1.0)


def swap(value, clip_mask, time_mask):
    clips, times = lax.axis_size("clip"), lax.axis_size("tm")
    pairs = [
        (c * times + t, (c ^ clip_mask) * times + (t ^ time_mask))
        for c in range(clips)
        for t in range(times)
    ]
    return lax.ppermute(value, ("clip", "tm"), pairs)


def prep_kernel(dil_hbm, pw_hbm, table_hbm, conv_ref, code_ref, dil_ref, pw_ref, table_ref, sems):
    time = lax.axis_index("tm")
    bit = time % 2
    out_rows = pw_ref.shape[0] // 2
    second = jnp.minimum(2 + bit, KERNEL - 1)
    copies = [
        pltpu.make_async_copy(table_hbm.at[time], table_ref, sems.at[0]),
        pltpu.make_async_copy(dil_hbm.at[bit], dil_ref.at[0], sems.at[1]),
        pltpu.make_async_copy(dil_hbm.at[second], dil_ref.at[1], sems.at[2]),
        pltpu.make_async_copy(pw_hbm, pw_ref, sems.at[3]),
    ]
    for copy in copies:
        copy.start()
    copies[0].wait()
    code_ref[...] = table_ref[...].astype(BF16)
    for copy in copies[1:]:
        copy.wait()
    for side in range(2):
        for part in range(2):
            conv_ref[part, side * out_rows : (side + 1) * out_rows, :] = dil_ref[
                part, :, side * DG : (side + 1) * DG
            ].astype(BF16)

    @pl.when(bit == 1)
    def _():
        conv_ref[1] = pw_ref[...].astype(BF16)


def renamed(values, ranks):
    block = CODES // ranks
    step = (values // block) ^ lax.axis_index("clip")
    place = (step % 2) * (ranks // 2) + step // 2
    return place * block + values % block


def masks(clips, frames, len_ref, columns):
    base = lax.axis_index("tm") * frames

    def mark(first, count, clip):
        where = lax.broadcasted_iota(jnp.int32, (count, columns), 0) + first
        return jnp.where((where >= 0) & (where < len_ref[clip]), 1.0, 0.0)

    own = [mark(base, frames, c) for c in range(clips)]
    margins = [
        mark(first, PAD, c) for c in range(clips) for first in (base - PAD, base + frames)
    ]
    return jnp.concatenate(own + margins, axis=0)


def widened(value, clip, clips, frames):
    at = clips * frames + 2 * PAD * clip
    return jnp.concatenate(
        [
            value[at : at + PAD],
            value[clip * frames : (clip + 1) * frames],
            value[at + PAD : at + 2 * PAD],
        ],
        axis=0,
    )


def pack_kernel(f_hbm, c_hbm, ids_hbm, near_ref, far_ref, buf, ids_ref, sems):
    clips, frames, _ = f_hbm.shape
    edge = 2 * PAD
    odd = lax.axis_index("tm") % 2
    copies = [pltpu.make_async_copy(ids_hbm, ids_ref, sems.at[4])]
    for kind, source in enumerate((f_hbm, c_hbm)):
        for side, at in enumerate((frames - edge, 0)):
            copies.append(
                pltpu.make_async_copy(
                    source.at[:, pl.ds(at, edge), :], buf.at[kind, side], sems.at[2 * kind + side]
                )
            )
    for copy in copies:
        copy.start()
    for copy in copies:
        copy.wait()
    outs = []
    for side in range(2):
        at = slice(PAD, 2 * PAD) if side == 0 else slice(0, PAD)
        parts = []
        for c in range(clips):
            ids = ids_ref[:, c, :]
            if side == 0:
                ids = pltpu.roll(ids, PAD, 1)
            both = jnp.concatenate([ids // 32, ids % 32], axis=0).astype(F32)
            both = jnp.concatenate([both, jnp.zeros((8, 2 * D - frames), F32)], axis=1)
            ends = [buf[kind, side, c].astype(F32)[at] for kind in range(2)]
            parts.append(jnp.concatenate([jnp.concatenate(ends, axis=1), both], axis=0))
        outs.append(parts)
    for c in range(clips):
        last, first = outs[0][c], outs[1][c]
        near_ref[c] = jnp.where(odd == 1, first, last).astype(BF16)
        far_ref[c] = jnp.where(odd == 1, last, first).astype(BF16)


def own_kernel(ranks, ids_ref, hot_ref, hott_ref):
    _, clips, frames = ids_ref.shape
    codes = lax.broadcasted_iota(jnp.int32, (frames, CODES), 1)
    spots = lax.broadcasted_iota(jnp.int32, (CODES, frames), 0)
    for c in range(clips):
        ids = renamed(ids_ref[:, c, :], ranks)
        turned = jnp.concatenate([ids.astype(F32), jnp.zeros((8 - SLOTS, frames), F32)], axis=0)
        turned = turned.T.astype(jnp.int32)
        at = slice(c * frames, (c + 1) * frames)
        for slot in range(SLOTS):
            hot_ref[slot, at, :] = jnp.where(codes == turned[:, slot : slot + 1], 1.0, 0.0).astype(
                BF16
            )
            hott_ref[slot, :, at] = jnp.where(spots == ids[slot : slot + 1], 1.0, 0.0).astype(BF16)
    hot_ref[:, clips * frames :, :] = jnp.zeros((SLOTS, 2 * PAD * clips, CODES), BF16)


def moved(value, shift, clips, frames):
    span = frames + 2 * PAD
    return jnp.concatenate(
        [
            pltpu.roll(widened(value, c, clips, frames), shift % span, 0)[PAD : PAD + frames]
            for c in range(clips)
        ],
        axis=0,
    ).astype(BF16)


def margin_kernel(
    ranks,
    len_ref,
    f_ref,
    near_ref,
    far_ref,
    old_ref,
    start_ref,
    act_ref,
    window_ref,
    cot_ref,
    hot_ref,
):
    del old_ref
    clips, frames, _ = f_ref.shape
    odd = lax.axis_index("tm") % 2
    both = []
    for c in range(clips):
        near, far = near_ref[c].astype(F32), far_ref[c].astype(F32)
        both += [jnp.where(odd == 1, near, far), jnp.where(odd == 1, far, near)]
    start = masks(clips, frames, len_ref, D) * jnp.concatenate(
        [f_ref[c].astype(F32) for c in range(clips)] + [part[:PAD, :D] for part in both], axis=0
    )
    start_ref[...] = start
    act = elu(start).astype(BF16)
    act_ref[...] = act
    wide = act.astype(F32)
    for tap in range(KERNEL):
        shift = (1 - tap) * DILATION
        window_ref[:, tap * D : (tap + 1) * D] = (
            moved(wide, shift, clips, frames) if shift else act[: clips * frames]
        )
    cot_ref[...] = jnp.concatenate([part[:PAD, D:] for part in both], axis=0)
    turned = jnp.concatenate([part[PAD:, :128].T[:PAD] for part in both], axis=0)
    ids = renamed((turned[:, :SLOTS] * 32.0 + turned[:, SLOTS : 2 * SLOTS]).astype(jnp.int32), ranks)
    codes = lax.broadcasted_iota(jnp.int32, (2 * PAD * clips, CODES), 1)
    for slot in range(SLOTS):
        hot_ref[slot, clips * frames :, :] = jnp.where(
            codes == ids[:, slot : slot + 1], 1.0, 0.0
        ).astype(BF16)


def assembled(ranks, pieces, d_ref, pwt_ref, all_ref):
    half, small = ranks // 2, 2 * HID // ranks
    out_rows = small // 2
    bit, rank = lax.axis_index("tm") % 2, lax.axis_index("clip")
    for other in range(2):
        for z in range(half):
            piece = pieces[other * half + z]
            for x in range(2):
                at = pl.multiple_of((rank ^ (2 * z + x)) * out_rows, out_rows)
                for part in range(2):
                    for side in range(2):
                        all_ref[
                            2 * part + (bit ^ other),
                            pl.ds(at, out_rows),
                            side * DG : (side + 1) * DG,
                        ] = piece[x, part, side * out_rows : (side + 1) * out_rows, :]
    for tap in range(KERNEL):
        d_ref[tap * HID : (tap + 1) * HID, :] = all_ref[tap]
    for r in range(ranks):
        for side in range(2):
            to = r * small + side * out_rows
            pwt_ref[to : to + out_rows, :] = all_ref[
                KERNEL, r * out_rows : (r + 1) * out_rows, side * DG : (side + 1) * DG
            ]


def conv_kernel(ranks, assemble, clips, start_ref, act_ref, *refs):
    if assemble:
        pieces, refs = refs[:ranks], refs[ranks:]
        d_ref, pwt_ref, gated_ref, hs_ref, latent_ref, all_ref = refs
        assembled(ranks, pieces, d_ref, pwt_ref, all_ref)
    else:
        d_ref, pwt_ref, gated_ref, hs_ref, latent_ref = refs
    rows = start_ref.shape[0]
    taps = mmg(act_ref[...], d_ref[...], NT)
    frames = rows // clips - 2 * PAD
    span = frames + 2 * PAD
    own, margins = [], []
    for c in range(clips):
        wide = widened(taps, c, clips, frames)
        part = (
            pltpu.roll(wide[:, :HID], DILATION, 0)
            + wide[:, HID : 2 * HID]
            + pltpu.roll(wide[:, 2 * HID :], span - DILATION, 0)
        )
        own.append(part[PAD : PAD + frames])
        margins += [part[:PAD], part[PAD + frames :]]
    hidden = jnp.concatenate(own + margins, axis=0)
    hs_ref[...] = slope(hidden)
    gated = elu(hidden).astype(BF16)
    gated_ref[...] = gated
    latent_ref[...] = start_ref[...] + mmg(gated, pwt_ref[...], NT)


def quant_kernel(ranks, len_ref, latent_ref, c_ref, cot_ref, hot_ref, hott_ref, *refs):
    half, block = ranks // 2, CODES // ranks
    pieces, refs = refs[:8], refs[8:]
    quant_ref, send_ref, bg_ref, lg_ref, cgs_ref, tab_ref = refs
    clips, frames, _ = c_ref.shape
    time = lax.axis_index("tm")
    mask = masks(clips, frames, len_ref, DG)
    local = clips * frames
    twice = -2.0 * mask[:local]
    for other in range(SLOTS):
        slot = time ^ other
        for x in range(2):
            for z in range(half):
                spot = (x * half + z) * block
                tab_ref[slot, spot : spot + block, :] = pieces[2 * other + x][z]
    for group in range(GROUPS):
        at = slice(group * DG, (group + 1) * DG)
        first = mm(hot_ref[2 * group], tab_ref[2 * group])
        second = mm(hot_ref[2 * group + 1], tab_ref[2 * group + 1])
        cot = jnp.concatenate(
            [c_ref[c, :, at].astype(F32) for c in range(clips)] + [cot_ref[:, at]], axis=0
        )
        residual = latent_ref[:, at]
        gap = residual - first
        gap2 = gap - second
        both = gap + gap2
        grad = mask * (cot + (both if COMMIT == 0.5 else 2.0 * COMMIT * both))
        quant = (mask * (first + second))[:local].astype(BF16)
        bg_ref[:, at] = grad.astype(BF16)
        lg_ref[:, at] = grad[:local]
        for clip in range(clips):
            quant_ref[clip, :, at] = quant[clip * frames : (clip + 1) * frames]
        for level, diff in ((0, gap), (1, gap2)):
            code_grad = twice * diff[:local]
            high = code_grad.astype(BF16)
            cgs_ref[2 * group + level, :, :DG] = high
            cgs_ref[2 * group + level, :, DG:] = (code_grad - high.astype(F32)).astype(BF16)
    size = block // SCALE_GROUPS
    for far in range(2):
        total = summed(2 * far + 1, hott_ref, cgs_ref)
        levels = []
        for place in range(ranks):
            steps, more = pack_part(total[place * block : (place + 1) * block])
            for group, step in enumerate(steps):
                at = place * block + group * size
                send_ref[far, at : at + size, :] = step.astype(jnp.int16)
            levels += more
        levels = jnp.concatenate(levels, axis=0).astype(jnp.int32)
        send_ref[far, CODES:, :] = levels.astype(jnp.int16)


def summed(other, hott_ref, cgs_ref):
    slot = lax.axis_index("tm") ^ other
    pair = mm(hott_ref[slot], cgs_ref[slot])
    return pair[:, :DG] + pair[:, DG:]


def keep_kernel(hott_ref, cgs_ref, keep_ref):
    for far in range(2):
        keep_ref[far] = summed(2 * far, hott_ref, cgs_ref)


def backward_kernel(
    ranks,
    assemble,
    clips,
    window_ref,
    gated_ref,
    bg_ref,
    hs_ref,
    pwt_ref,
    hg_ref,
    *outs,
):
    local = window_ref.shape[0]
    bg = bg_ref[...]
    hidden_grad = (mm(bg, pwt_ref[...]) * hs_ref[...]).astype(BF16)
    hg_ref[...] = hidden_grad
    dil_all = mmg(hidden_grad[:local], window_ref[...], TN)
    dil_grads = [dil_all[:, tap * D : (tap + 1) * D] for tap in range(KERNEL)]
    pw_grad = mmg(bg[:local], gated_ref[:local, :], TN)
    if assemble:
        keep_ref, send_ref, all_ref = outs
        half, small = ranks // 2, 2 * HID // ranks
        out_rows = small // 2
        time, rank = lax.axis_index("tm"), lax.axis_index("clip")
        for tap in range(KERNEL):
            all_ref[tap] = dil_grads[tap]
        for r in range(ranks):
            for side in range(2):
                at = r * small + side * out_rows
                all_ref[KERNEL, r * out_rows : (r + 1) * out_rows, side * DG : (side + 1) * DG] = (
                    pw_grad[at : at + out_rows]
                )
        for other in range(4):
            out = (keep_ref, send_ref)[other % 2]
            for x in range(2):
                for z in range(half):
                    at = pl.multiple_of((rank ^ (2 * z + x)) * out_rows, out_rows)
                    to = (x * half + z) * small
                    for side in range(2):
                        out[other // 2, to + side * out_rows : to + (side + 1) * out_rows, :] = (
                            all_ref[
                                time ^ other, pl.ds(at, out_rows), side * DG : (side + 1) * DG
                            ]
                        )
    else:
        dil_ref, pw_ref = outs
        for tap in range(KERNEL):
            dil_ref[tap] = dil_grads[tap]
        pw_ref[...] = pw_grad


def features_kernel(clips, len_ref, start_ref, lg_ref, hg_ref, d_ref, fg_ref):
    frames = start_ref.shape[0] // clips - 2 * PAD
    local = clips * frames
    wide = hg_ref[...].astype(F32)
    shifted = jnp.concatenate(
        [
            moved(wide, -DILATION, clips, frames),
            hg_ref[:local, :],
            moved(wide, DILATION, clips, frames),
        ],
        axis=1,
    )
    act_grad = mm(shifted, d_ref[...])
    row = lax.broadcasted_iota(jnp.int32, (frames, D), 0) + lax.axis_index("tm") * frames
    for c in range(clips):
        to = slice(c * frames, (c + 1) * frames)
        mask = jnp.where(row < len_ref[c], 1.0, 0.0)
        fg_ref[c] = mask * (lg_ref[to, :] + slope(start_ref[to, :]) * act_grad[to])


def pack_part(value):
    count = SCALE_GROUPS
    rows = value.shape[0]
    size = rows // count
    steps, levels = [], []
    for group in range(count):
        part = value[group * size : (group + 1) * size]
        top = jnp.maximum(jnp.max(jnp.abs(part), axis=0, keepdims=True), 1e-30)
        level = jnp.ceil(jnp.log2(top) * LEVEL_STEPS)
        scale = jnp.exp2(level / -LEVEL_STEPS) * TOP
        steps.append(jnp.round(part * scale).astype(jnp.int32))
        levels.append(level)
    return steps, levels


def unpack_part(steps, level):
    return steps.astype(jnp.int32).astype(F32) * (
        jnp.exp2(level.astype(jnp.int32).astype(F32) / LEVEL_STEPS) / TOP
    )


def send_kernel(groups, rows, keep_ref, got_ref, own_ref, *outs):
    size = rows // SCALE_GROUPS
    for part, blocks in enumerate(groups):
        levels = []
        for place, (jy, start) in enumerate(blocks):
            at = slice(start * rows, (start + 1) * rows)
            if got_ref.dtype == F32:
                other = got_ref[jy, at, :]
            else:
                top = (got_ref.shape[1] // (rows + SCALE_GROUPS)) * rows + start * SCALE_GROUPS
                other = jnp.concatenate(
                    [
                        unpack_part(
                            got_ref[jy, start * rows + g * size : start * rows + (g + 1) * size, :],
                            got_ref[jy, top : top + SCALE_GROUPS, :][g : g + 1],
                        )
                        for g in range(SCALE_GROUPS)
                    ],
                    axis=0,
                )
            value = keep_ref[jy, at, :] + other
            if part == 0:
                own_ref[place] = value
                continue
            steps, more = pack_part(value)
            for group, step in enumerate(steps):
                spot = place * rows + group * size
                outs[part - 1][spot : spot + size, :] = step.astype(jnp.int16)
            levels += more
        if part:
            tail = jnp.concatenate(levels, axis=0).astype(jnp.int32)
            outs[part - 1][len(blocks) * rows :, :] = tail.astype(jnp.int16)


def pass_kernel(rows, own_in, *refs):
    blocks = own_in.shape[0]
    gots, own_ref, outs = refs[:-blocks], refs[-blocks], refs[1 - blocks :]
    size = rows // SCALE_GROUPS
    for place in range(blocks):
        value = own_in[place]
        pieces = [value[g * size : (g + 1) * size] for g in range(SCALE_GROUPS)]
        for got in gots:
            tail = got[blocks * rows :, :]
            for g in range(SCALE_GROUPS):
                index = place * SCALE_GROUPS + g
                spot = place * rows + g * size
                pieces[g] = pieces[g] + unpack_part(
                    got[spot : spot + size, :], tail[index : index + 1]
                )
        if place == 0:
            for g in range(SCALE_GROUPS):
                own_ref[g * size : (g + 1) * size, :] = pieces[g]
            continue
        steps, levels = pack_part(jnp.concatenate(pieces, axis=0))
        out = outs[place - 1]
        for g, step in enumerate(steps):
            out[g * size : (g + 1) * size, :] = step.astype(jnp.int16)
        pad = jnp.zeros((out.shape[0] - rows - len(levels), DG), F32)
        tail = jnp.concatenate(levels + [pad], axis=0).astype(jnp.int32)
        out[rows:, :] = tail.astype(jnp.int16)


def final_kernel(sizes, counts, *refs):
    out_ref, square_ref = refs[-2:]
    squares = jnp.zeros((1, DG), F32)
    place = 0
    for kind, rows in enumerate(sizes):
        own_ref, *gots = refs[sum(counts[:kind]) : sum(counts[: kind + 1])]
        size = rows // SCALE_GROUPS
        for g in range(SCALE_GROUPS):
            at = slice(g * size, (g + 1) * size)
            value = own_ref[at, :]
            for got in gots:
                value = value + unpack_part(got[at, :], got[rows:, :][g : g + 1])
            out_ref[place : place + size, :] = value
            squares = squares + jnp.sum(value * value, axis=0, keepdims=True)
            place += size
    square = jnp.sum(squares, axis=1, keepdims=True)
    square_ref[...] = jnp.broadcast_to(square[None], square_ref.shape)


def stepped(weight, first, second, grad, rate, fix1, fix2):
    first_new = FIRST_DECAY * first + (1.0 - FIRST_DECAY) * grad
    second_new = SECOND_DECAY * second + (1.0 - SECOND_DECAY) * grad * grad
    change = (first_new * fix1) / (jnp.sqrt(second_new * fix2) + EPSILON) + WEIGHT_DECAY * weight
    return weight - rate * change, second_new


def update_kernel(fix_ref, square_ref, *refs):
    pieces = refs[:4]
    dil, pw, table = refs[4:7], refs[7:10], refs[10:13]
    norm_ref = refs[13]
    dil_hbm, pw_hbm, table_hbm = refs[14:17], refs[17:20], refs[20:23]
    dil_out, pw_out, table_out = refs[23:26], refs[26:29], refs[29:32]
    sems = refs[32]
    out_rows = dil[0].shape[1]
    small = 2 * out_rows
    time = lax.axis_index("tm")
    count = KERNEL * D * HID + D * HID + SLOTS * CODES * DG
    norm = jnp.sqrt(jnp.sum(square_ref[...], axis=0)[:1, :1])
    limit = jnp.sqrt(jnp.full((1, 1), float(count), F32))
    scale = limit / jnp.maximum(norm, limit)
    norm_ref[...] = norm
    fixes = (fix_ref[0], fix_ref[1])
    copies = []
    for other in range(4):
        quarter = time ^ other
        piece = pieces[other]
        grad = piece[small:, :] * scale
        state = [v[quarter] for v in table]
        weight, second = stepped(*state, grad, RATE_CODE, *fixes)
        for kind, value in enumerate((weight, grad, second)):
            table_out[kind][quarter] = value
            copies.append(
                pltpu.make_async_copy(
                    table_out[kind].at[quarter], table_hbm[kind].at[quarter], sems.at[len(copies)]
                )
            )
            copies[-1].start()

        @pl.when(quarter < KERNEL)
        def _():
            tap = jnp.minimum(quarter, KERNEL - 1)
            for side in range(2):
                to = slice(side * DG, (side + 1) * DG)
                grad = piece[side * out_rows : (side + 1) * out_rows, :] * scale
                state = [v[tap, :, to] for v in dil]
                weight, second = stepped(*state, grad, BITRATE_FACTOR, *fixes)
                dil_out[0][tap, :, to] = weight
                dil_out[1][tap, :, to] = grad
                dil_out[2][tap, :, to] = second

        @pl.when(quarter == KERNEL)
        def _():
            grad = piece[:small, :] * scale
            weight, second = stepped(*[v[...] for v in pw], grad, BITRATE_FACTOR, *fixes)
            pw_out[0][...] = weight
            pw_out[1][...] = grad
            pw_out[2][...] = second

    for kind in range(3):
        for outs, hbms in ((dil_out, dil_hbm), (pw_out, pw_hbm)):
            copies.append(pltpu.make_async_copy(outs[kind], hbms[kind], sems.at[len(copies)]))
            copies[-1].start()
    for copy in copies:
        copy.wait()


def shards(
    features,
    cotangent,
    clip_lengths,
    code_ids,
    step_count,
    dilated_kernel_weight,
    pointwise_conv,
    codebooks,
    dilated_first_moment,
    dilated_second_moment,
    pointwise_first,
    pointwise_second,
    codebook_first,
    codebook_second,
):
    ranks, times = lax.axis_size("clip"), lax.axis_size("tm")
    rank, time = lax.axis_index("clip"), lax.axis_index("tm")
    clips, frames, _ = features.shape
    half = ranks // 2
    out_rows = HID // ranks
    block = CODES // ranks
    small = 2 * out_rows
    rows = clips * (frames + 2 * PAD)
    smem = pl.BlockSpec(memory_space=pltpu.SMEM)
    hbm = pl.BlockSpec(memory_space=pltpu.HBM)
    shape = jax.ShapeDtypeStruct

    def held(*values):
        return [pltpu.with_memory_space_constraint(v, pltpu.HBM) for v in values]

    assemble = out_rows % 16 == 0
    dil_state = [
        v.transpose(0, 2, 1)
        for v in (dilated_kernel_weight, dilated_first_moment, dilated_second_moment)
    ]
    pw_state = [v.T for v in (pointwise_conv, pointwise_first, pointwise_second)]
    table_state = [codebooks, codebook_first, codebook_second]

    if assemble:
        mine_d, mine_c = pl.pallas_call(
            prep_kernel,
            out_shape=(shape((2, small, DG), BF16), shape((block, DG), BF16)),
            in_specs=[hbm] * 3,
            out_specs=tuple(whole(2)),
            scratch_shapes=[
                pltpu.VMEM((2, out_rows, D), F32),
                pltpu.VMEM((small, DG), F32),
                pltpu.VMEM((block, DG), F32),
                pltpu.SemaphoreType.DMA((4,)),
            ],
            compiler_params=params(),
            name="prep",
        )(*held(dil_state[0], pw_state[0], codebooks))
    else:
        taps = dil_state[0].astype(BF16).reshape(KERNEL, out_rows, 2, DG).transpose(0, 2, 1, 3)
        quarters = jnp.concatenate(
            [taps.reshape(KERNEL, small, DG), pw_state[0].astype(BF16)[None]], axis=0
        )
        mine_d = jnp.take(quarters, time % 2 + jnp.array([0, 2]), axis=0)
        mine_c = lax.dynamic_index_in_dim(codebooks, time, 0, keepdims=False).astype(BF16)

    mine_c, mine_d, late_ids = lax.optimization_barrier((mine_c, mine_d, code_ids))
    near, far = pl.pallas_call(
        pack_kernel,
        out_shape=(shape((clips, 2 * PAD, 2 * D), BF16),) * 2,
        in_specs=[hbm] * 3,
        out_specs=tuple(whole(2)),
        scratch_shapes=[
            pltpu.VMEM((2, 2, clips, 2 * PAD, D), BF16),
            pltpu.VMEM(code_ids.shape, jnp.int32),
            pltpu.SemaphoreType.DMA((5,)),
        ],
        compiler_params=params(),
        name="pack",
    )(*held(features, cotangent, late_ids))
    line_c = [swap(mine_c, 2 * z, 0) for z in range(1, half)]
    across = swap(mine_d, 1, 0)
    near = lax.ppermute(near, "tm", [(i, i ^ 1) for i in range(times)])
    pairs = [(i, i + 1) for i in range(1, times - 1, 2)]
    far = lax.ppermute(far, "tm", pairs + [(b, a) for a, b in pairs])
    near, far, *line_c = lax.optimization_barrier((near, far, *line_c))
    line_c = jnp.stack([mine_c] + line_c, axis=0)
    pair_d = jnp.stack([mine_d, across], axis=0)
    line_c, late_ids = lax.optimization_barrier((line_c, code_ids))
    hot, hott = pl.pallas_call(
        functools.partial(own_kernel, ranks),
        out_shape=(
            shape((SLOTS, rows, CODES), BF16),
            shape((SLOTS, CODES, clips * frames), BF16),
        ),
        in_specs=whole(1),
        out_specs=tuple(whole(2)),
        compiler_params=params(8),
        name="own",
    )(late_ids)
    plane_c = [line_c, swap(line_c, 1, 0), swap(line_c, 0, 2), swap(line_c, 1, 2)]
    line_d = [pair_d] + [swap(pair_d, 2 * z, 0) for z in range(1, half)]

    start, act, windows, cot, hot = pl.pallas_call(
        functools.partial(margin_kernel, ranks),
        out_shape=(
            shape((rows, D), F32),
            shape((rows, D), BF16),
            shape((clips * frames, KERNEL * D), BF16),
            shape((2 * PAD * clips, D), F32),
            shape(hot.shape, BF16),
        ),
        in_specs=[smem] + whole(4),
        out_specs=tuple(whole(5)),
        input_output_aliases={4: 4},
        compiler_params=params(8),
        name="margin",
    )(clip_lengths, features, near, far, hot)

    act, *line_d = lax.optimization_barrier((act, *line_d))
    pieces_d = line_d + [swap(v, 0, 1) for v in line_d]
    turned = [swap(v, 0, 1) for v in plane_c]
    pieces_c = plane_c[:2] + turned[:2] + plane_c[2:] + turned[2:]

    weights = (shape((KERNEL * HID, D), BF16), shape((D, HID), BF16))
    given = pieces_d
    if not assemble:
        order = rank ^ jnp.arange(ranks)
        stacked = jnp.stack(pieces_d, axis=0).reshape(2, half, 2, 2, small, DG)
        stacked = jnp.take(stacked, time % 2 ^ jnp.arange(2), axis=0)
        stacked = stacked.transpose(3, 0, 1, 2, 4, 5).reshape(4, ranks, small, DG)
        stacked = jnp.take(stacked, order, axis=1)
        dil = stacked[:KERNEL].reshape(KERNEL, ranks, 2, out_rows, DG)
        dil = dil.transpose(0, 1, 3, 2, 4).reshape(KERNEL * HID, D)
        given = [dil, stacked[3].reshape(D, HID)]
    outs = pl.pallas_call(
        functools.partial(conv_kernel, ranks, assemble, clips),
        out_shape=(weights if assemble else ())
        + (shape((rows, HID), BF16), shape((rows, HID), F32), shape((rows, D), F32)),
        in_specs=whole(2 + len(given)),
        out_specs=tuple(whole(5 if assemble else 3)),
        scratch_shapes=[pltpu.VMEM((4, HID, D), BF16)] if assemble else [],
        compiler_params=params(10),
        name="conv",
    )(start, act, *given)
    dil, pwt, gated, hs, latent = tuple(outs) if assemble else tuple(given) + tuple(outs)

    quant, send, bg, lg, cgs = pl.pallas_call(
        functools.partial(quant_kernel, ranks),
        out_shape=(
            shape((clips, frames, D), BF16),
            shape((2, CODES + SCALE_GROUPS * ranks, DG), jnp.int16),
            shape((rows, D), BF16),
            shape((clips * frames, D), F32),
            shape((SLOTS, clips * frames, 2 * DG), BF16),
        ),
        in_specs=[smem] + whole(5 + len(pieces_c)),
        out_specs=tuple(whole(5)),
        scratch_shapes=[
            pltpu.VMEM((SLOTS, CODES, DG), BF16),
        ],
        compiler_params=params(16),
        name="quant",
    )(clip_lengths, latent, cotangent, cot, hot, hott, *pieces_c)

    keep = pl.pallas_call(
        keep_kernel,
        out_shape=shape((2, CODES, DG), F32),
        in_specs=whole(2),
        out_specs=whole(1)[0],
        compiler_params=params(8),
        name="keep",
    )(hott, cgs)

    if assemble:
        grads = (shape((2, ranks * small, DG), F32),) * 2
    else:
        grads = (shape((KERNEL, HID, D), F32), shape((D, HID), F32))
    hg, first_grad, second_grad = pl.pallas_call(
        functools.partial(backward_kernel, ranks, assemble, clips),
        out_shape=(shape((rows, HID), BF16),) + grads,
        in_specs=whole(5),
        out_specs=tuple(whole(3)),
        scratch_shapes=[pltpu.VMEM((4, HID, D), F32)] if assemble else [],
        compiler_params=params(16),
        name="backward",
    )(windows, gated, bg, hs, pwt)
    fg = pl.pallas_call(
        functools.partial(features_kernel, clips),
        out_shape=shape((clips, frames, D), F32),
        in_specs=[smem] + whole(4),
        out_specs=whole(1)[0],
        compiler_params=params(12),
        name="features",
    )(clip_lengths, start, lg, hg, dil)

    if assemble:
        keep_d, send_d = first_grad, second_grad
    else:
        parts = jnp.concatenate(
            [
                first_grad.reshape(KERNEL, ranks, out_rows, 2, DG)
                .transpose(0, 1, 3, 2, 4)
                .reshape(KERNEL, ranks, small, DG),
                second_grad.reshape(1, ranks, small, DG),
            ],
            axis=0,
        )
        seq = jnp.concatenate([jnp.arange(0, ranks, 2), jnp.arange(1, ranks, 2)])
        parts = jnp.take(jnp.take(parts, time ^ jnp.arange(4), axis=0), rank ^ seq, axis=1)
        parts = parts.reshape(2, 2, ranks * small, DG)
        keep_d, send_d = parts[:, 0], parts[:, 1]

    def sent(keep, got, groups, size, tag):
        count = len(groups[0])
        packed = count * size + count * SCALE_GROUPS
        return pl.pallas_call(
            functools.partial(send_kernel, groups, size),
            out_shape=(shape((count, size, DG), F32),)
            + (shape((packed, DG), jnp.int16),) * (len(groups) - 1),
            in_specs=whole(2),
            out_specs=tuple(whole(len(groups))),
            compiler_params=params(),
            name="send_" + tag,
        )(keep, got)

    def passed(parts, size, tag):
        count = parts[0].shape[0]
        return pl.pallas_call(
            functools.partial(pass_kernel, size),
            out_shape=(shape((size, DG), F32),)
            + (shape((size + 16, DG), jnp.int16),) * (count - 1),
            in_specs=whole(len(parts)),
            out_specs=tuple(whole(count)),
            compiler_params=params(),
            name="pass_" + tag,
        )(*parts)

    def over_plane(parts):
        return [parts[0], swap(parts[1], 1, 0), swap(parts[2], 0, 2), swap(parts[3], 1, 2)]

    def over_line(parts):
        return [parts[0]] + [swap(parts[z], 2 * z, 0) for z in range(1, half)]

    by_plane = [[(jy, x * half + z) for z in range(half)] for jy in range(2) for x in range(2)]
    by_line = [[(jy, x * half + z) for jy in range(2) for x in range(2)] for z in range(half)]
    got_c, got_d = swap(send, 0, 1), swap(send_d, 0, 1)
    parts_c = over_plane(sent(keep, got_c, by_plane, block, "codes"))
    parts_c[0], keep_d = lax.optimization_barrier((parts_c[0], keep_d))
    parts_d = over_line(sent(keep_d, got_d, by_line, small, "conv"))
    fg, parts_c[0] = lax.optimization_barrier((fg, parts_c[0]))
    parts_c = over_line(passed(parts_c, block, "codes"))
    parts_c[1], parts_d[0] = lax.optimization_barrier((parts_c[1], parts_d[0]))
    parts_d = over_plane(passed(parts_d, small, "conv"))
    total = small + block
    piece, squares = pl.pallas_call(
        functools.partial(final_kernel, (small, block), (4, half)),
        out_shape=(shape((total, DG), F32), shape((ranks * times, 8, 128), F32)),
        in_specs=whole(4 + half),
        out_specs=tuple(whole(2)),
        compiler_params=params(),
        name="final",
    )(*parts_d, *parts_c)

    across = swap(piece, 0, 2)
    squares = lax.all_to_all(squares, ("clip", "tm"), 0, 0, tiled=True)
    fours = [piece, swap(piece, 0, 1), across, swap(across, 0, 1)]
    steps = step_count[0].astype(F32)
    decays = jnp.stack([1.0 / (1.0 - FIRST_DECAY**steps), 1.0 / (1.0 - SECOND_DECAY**steps)])
    if assemble:
        state = dil_state + pw_state + table_state
        norm, *new = pl.pallas_call(
            update_kernel,
            out_shape=(shape((1, 1), F32),) + tuple(shape(v.shape, F32) for v in state),
            in_specs=[smem] + whole(14),
            out_specs=tuple(whole(1) + [hbm] * 9),
            scratch_shapes=[pltpu.VMEM(v.shape, F32) for v in state]
            + [pltpu.SemaphoreType.DMA((18,))],
            compiler_params=params(8),
            name="update",
        )(decays, squares, *fours, *state)
        norm = norm.reshape(1)
        dil_new, pw_new, table_new = new[:3], new[3:6], new[6:]
    else:
        four = jnp.take(jnp.stack(fours, axis=0), time ^ jnp.arange(4), axis=0)
        raw = four[:KERNEL, :small].reshape(KERNEL, 2, out_rows, DG)
        raw = raw.transpose(0, 2, 1, 3).reshape(KERNEL, out_rows, D)
        count = KERNEL * D * HID + D * HID + SLOTS * CODES * DG
        limit = jnp.sqrt(jnp.float32(count))
        norm = jnp.sqrt(jnp.sum(squares, axis=0)[0, :1])
        scale = limit / jnp.maximum(norm[0], limit)
        new = []
        for state, grad, rate in (
            (dil_state, raw, BITRATE_FACTOR),
            (pw_state, four[3, :small], BITRATE_FACTOR),
            (table_state, four[:, small:], RATE_CODE),
        ):
            grad = grad * scale
            weight, second = stepped(*state, grad, rate, decays[0], decays[1])
            new.append((weight, grad, second))
        dil_new, pw_new, table_new = new
    return (
        quant,
        fg,
        norm,
        *[v.transpose(0, 2, 1) for v in dil_new],
        *[v.T for v in pw_new],
        *table_new,
    )


def solution(mesh):
    in_specs = (
        P("clip", "tm", None),
        P("clip", "tm", None),
        P("clip"),
        P(None, "clip", "tm"),
        P(),
        P(None, None, "clip"),
        P(None, "clip"),
        P(None, "clip", None),
        P(None, None, "clip"),
        P(None, None, "clip"),
        P(None, "clip"),
        P(None, "clip"),
        P(None, "clip", None),
        P(None, "clip", None),
    )
    out_specs = (
        P("clip", "tm", None),
        P("clip", "tm", None),
        P(),
        P(None, None, "clip"),
        P(None, None, "clip"),
        P(None, None, "clip"),
        P(None, "clip"),
        P(None, "clip"),
        P(None, "clip"),
        P(None, "clip", None),
        P(None, "clip", None),
        P(None, "clip", None),
    )
    return jax.shard_map(shards, mesh=mesh, in_specs=in_specs, out_specs=out_specs, check_vma=False)
```

```python
import functools

import jax
import jax.numpy as jnp
from jax import lax
from jax.experimental import pallas as pl
from jax.experimental.pallas import tpu as pltpu
from jax.sharding import PartitionSpec as P

D = 512
HID = 256
CODES = 1024
GROUPS = 2
LEVELS = 2
SLOTS = 4
KERNEL = 3
DILATION = 3
DG = 256
PAD = 8

COMMIT = 0.25
FIRST_DECAY = 0.9
SECOND_DECAY = 0.99
EPSILON = 1e-08
WEIGHT_DECAY = 0.01
BITRATE_FACTOR = 0.02
RATE_CODE = 0.5

F32 = jnp.float32
BF16 = jnp.bfloat16
NT = (((1,), (1,)), ((), ()))
TN = (((0,), (0,)), ((), ()))
LEVEL_STEPS = 256.0
TOP = 32000.0
SCALE_GROUPS = 4
MIB = 1024 * 1024


def params(mib=6):
    return pltpu.CompilerParams(vmem_limit_bytes=mib * MIB)


def whole(count):
    return [pl.BlockSpec(memory_space=pltpu.VMEM)] * count


def mm(a, b):
    return jnp.dot(a, b, preferred_element_type=F32)


def mmg(a, b, dims):
    return lax.dot_general(a, b, dims, preferred_element_type=F32)


def slope(v):
    return jnp.where(v > 0, 1.0, jnp.exp(jnp.minimum(v, 0.0)))


def elu(v):
    return jnp.where(v > 0, v, jnp.exp(jnp.minimum(v, 0.0)) - 1.0)


def swap(value, clip_mask, time_mask):
    clips, times = lax.axis_size("clip"), lax.axis_size("tm")
    pairs = [
        (c * times + t, (c ^ clip_mask) * times + (t ^ time_mask))
        for c in range(clips)
        for t in range(times)
    ]
    return lax.ppermute(value, ("clip", "tm"), pairs)


def prep_kernel(dil_hbm, pw_hbm, table_hbm, conv_ref, code_ref, dil_ref, pw_ref, table_ref, sems):
    time = lax.axis_index("tm")
    bit = time % 2
    out_rows = pw_ref.shape[0] // 2
    second = jnp.minimum(2 + bit, KERNEL - 1)
    copies = [
        pltpu.make_async_copy(table_hbm.at[time], table_ref, sems.at[0]),
        pltpu.make_async_copy(dil_hbm.at[bit], dil_ref.at[0], sems.at[1]),
        pltpu.make_async_copy(dil_hbm.at[second], dil_ref.at[1], sems.at[2]),
        pltpu.make_async_copy(pw_hbm, pw_ref, sems.at[3]),
    ]
    for copy in copies:
        copy.start()
    copies[0].wait()
    code_ref[...] = table_ref[...].astype(BF16)
    for copy in copies[1:]:
        copy.wait()
    for side in range(2):
        for part in range(2):
            conv_ref[part, side * out_rows : (side + 1) * out_rows, :] = dil_ref[
                part, :, side * DG : (side + 1) * DG
            ].astype(BF16)

    @pl.when(bit == 1)
    def _():
        conv_ref[1] = pw_ref[...].astype(BF16)


def renamed(values, ranks):
    block = CODES // ranks
    step = (values // block) ^ lax.axis_index("clip")
    place = (step % 2) * (ranks // 2) + step // 2
    return place * block + values % block


def masks(clips, frames, len_ref, columns):
    base = lax.axis_index("tm") * frames

    def mark(first, count, clip):
        where = lax.broadcasted_iota(jnp.int32, (count, columns), 0) + first
        return jnp.where((where >= 0) & (where < len_ref[clip]), 1.0, 0.0)

    own = [mark(base, frames, c) for c in range(clips)]
    margins = [
        mark(first, PAD, c) for c in range(clips) for first in (base - PAD, base + frames)
    ]
    return jnp.concatenate(own + margins, axis=0)


def widened(value, clip, clips, frames):
    at = clips * frames + 2 * PAD * clip
    return jnp.concatenate(
        [
            value[at : at + PAD],
            value[clip * frames : (clip + 1) * frames],
            value[at + PAD : at + 2 * PAD],
        ],
        axis=0,
    )


def pack_kernel(f_hbm, c_hbm, ids_hbm, near_ref, far_ref, buf, ids_ref, sems):
    clips, frames, _ = f_hbm.shape
    edge = 2 * PAD
    odd = lax.axis_index("tm") % 2
    copies = [pltpu.make_async_copy(ids_hbm, ids_ref, sems.at[4])]
    for kind, source in enumerate((f_hbm, c_hbm)):
        for side, at in enumerate((frames - edge, 0)):
            copies.append(
                pltpu.make_async_copy(
                    source.at[:, pl.ds(at, edge), :], buf.at[kind, side], sems.at[2 * kind + side]
                )
            )
    for copy in copies:
        copy.start()
    for copy in copies:
        copy.wait()
    outs = []
    for side in range(2):
        at = slice(PAD, 2 * PAD) if side == 0 else slice(0, PAD)
        parts = []
        for c in range(clips):
            ids = ids_ref[:, c, :]
            if side == 0:
                ids = pltpu.roll(ids, PAD, 1)
            both = jnp.concatenate([ids // 32, ids % 32], axis=0).astype(F32)
            both = jnp.concatenate([both, jnp.zeros((8, 2 * D - frames), F32)], axis=1)
            ends = [buf[kind, side, c].astype(F32)[at] for kind in range(2)]
            parts.append(jnp.concatenate([jnp.concatenate(ends, axis=1), both], axis=0))
        outs.append(parts)
    for c in range(clips):
        last, first = outs[0][c], outs[1][c]
        near_ref[c] = jnp.where(odd == 1, first, last).astype(BF16)
        far_ref[c] = jnp.where(odd == 1, last, first).astype(BF16)


def own_kernel(ranks, len_ref, ids_ref, hot_ref, hott_ref):
    _, clips, frames = ids_ref.shape
    codes = lax.broadcasted_iota(jnp.int32, (frames, CODES), 1)
    spots = lax.broadcasted_iota(jnp.int32, (CODES, frames), 0)
    where = lax.broadcasted_iota(jnp.int32, (1, frames), 1) + lax.axis_index("tm") * frames
    for c in range(clips):
        weight = jnp.where(where < len_ref[c], -2.0, 0.0)
        ids = renamed(ids_ref[:, c, :], ranks)
        turned = jnp.concatenate([ids.astype(F32), jnp.zeros((8 - SLOTS, frames), F32)], axis=0)
        turned = turned.T.astype(jnp.int32)
        at = slice(c * frames, (c + 1) * frames)
        for slot in range(SLOTS):
            hot_ref[slot, at, :] = jnp.where(codes == turned[:, slot : slot + 1], 1.0, 0.0).astype(
                BF16
            )
            hott_ref[slot, :, at] = jnp.where(spots == ids[slot : slot + 1], weight, 0.0).astype(BF16)
    hot_ref[:, clips * frames :, :] = jnp.zeros((SLOTS, 2 * PAD * clips, CODES), BF16)


def moved(value, shift, clips, frames):
    span = frames + 2 * PAD
    return jnp.concatenate(
        [
            pltpu.roll(widened(value, c, clips, frames), shift % span, 0)[PAD : PAD + frames]
            for c in range(clips)
        ],
        axis=0,
    ).astype(BF16)


def margin_kernel(
    ranks,
    len_ref,
    f_ref,
    near_ref,
    far_ref,
    old_ref,
    start_ref,
    act_ref,
    window_ref,
    cot_ref,
    mask_ref,
    hot_ref,
):
    del old_ref
    clips, frames, _ = f_ref.shape
    odd = lax.axis_index("tm") % 2
    both = []
    for c in range(clips):
        near, far = near_ref[c].astype(F32), far_ref[c].astype(F32)
        both += [jnp.where(odd == 1, near, far), jnp.where(odd == 1, far, near)]
    mask = masks(clips, frames, len_ref, D)
    mask_ref[...] = mask[:, :DG]
    start = mask * jnp.concatenate(
        [f_ref[c].astype(F32) for c in range(clips)] + [part[:PAD, :D] for part in both], axis=0
    )
    start_ref[...] = start
    act = elu(start).astype(BF16)
    act_ref[...] = act
    wide = act.astype(F32)
    for tap in range(KERNEL):
        shift = (1 - tap) * DILATION
        window_ref[:, tap * D : (tap + 1) * D] = (
            moved(wide, shift, clips, frames) if shift else act[: clips * frames]
        )
    cot_ref[...] = jnp.concatenate([part[:PAD, D:] for part in both], axis=0)
    turned = jnp.concatenate([part[PAD:, :128].T[:PAD] for part in both], axis=0)
    ids = renamed((turned[:, :SLOTS] * 32.0 + turned[:, SLOTS : 2 * SLOTS]).astype(jnp.int32), ranks)
    codes = lax.broadcasted_iota(jnp.int32, (2 * PAD * clips, CODES), 1)
    for slot in range(SLOTS):
        hot_ref[slot, clips * frames :, :] = jnp.where(
            codes == ids[:, slot : slot + 1], 1.0, 0.0
        ).astype(BF16)


def assembled(ranks, pieces, d_ref, pwt_ref, all_ref):
    half, small = ranks // 2, 2 * HID // ranks
    out_rows = small // 2
    bit, rank = lax.axis_index("tm") % 2, lax.axis_index("clip")
    for other in range(2):
        for z in range(half):
            piece = pieces[other * half + z]
            for x in range(2):
                at = pl.multiple_of((rank ^ (2 * z + x)) * out_rows, out_rows)
                for part in range(2):
                    for side in range(2):
                        all_ref[
                            2 * part + (bit ^ other),
                            pl.ds(at, out_rows),
                            side * DG : (side + 1) * DG,
                        ] = piece[x, part, side * out_rows : (side + 1) * out_rows, :]
    for tap in range(KERNEL):
        d_ref[tap * HID : (tap + 1) * HID, :] = all_ref[tap]
    for r in range(ranks):
        for side in range(2):
            to = r * small + side * out_rows
            pwt_ref[to : to + out_rows, :] = all_ref[
                KERNEL, r * out_rows : (r + 1) * out_rows, side * DG : (side + 1) * DG
            ]


def conv_kernel(ranks, assemble, clips, start_ref, act_ref, *refs):
    if assemble:
        pieces, refs = refs[:ranks], refs[ranks:]
        d_ref, pwt_ref, gated_ref, hs_ref, latent_ref, all_ref = refs
        assembled(ranks, pieces, d_ref, pwt_ref, all_ref)
    else:
        d_ref, pwt_ref, gated_ref, hs_ref, latent_ref = refs
    rows = start_ref.shape[0]
    taps = mmg(act_ref[...], d_ref[...], NT)
    frames = rows // clips - 2 * PAD
    span = frames + 2 * PAD
    own, margins = [], []
    for c in range(clips):
        wide = widened(taps, c, clips, frames)
        part = (
            pltpu.roll(wide[:, :HID], DILATION, 0)
            + wide[:, HID : 2 * HID]
            + pltpu.roll(wide[:, 2 * HID :], span - DILATION, 0)
        )
        own.append(part[PAD : PAD + frames])
        margins += [part[:PAD], part[PAD + frames :]]
    hidden = jnp.concatenate(own + margins, axis=0)
    hs_ref[...] = slope(hidden)
    gated = elu(hidden).astype(BF16)
    gated_ref[...] = gated
    latent_ref[...] = start_ref[...] + mmg(gated, pwt_ref[...], NT)


def quant_kernel(ranks, mask_ref, latent_ref, c_ref, cot_ref, hot_ref, hott_ref, *refs):
    half, block = ranks // 2, CODES // ranks
    pieces, refs = refs[:8], refs[8:]
    quant_ref, send_ref, bg_ref, lg_ref, cgs_ref, tab_ref = refs
    clips, frames, _ = c_ref.shape
    time = lax.axis_index("tm")
    mask = mask_ref[...]
    local = clips * frames
    for other in range(SLOTS):
        slot = time ^ other
        for x in range(2):
            for z in range(half):
                spot = (x * half + z) * block
                tab_ref[slot, spot : spot + block, :] = pieces[2 * other + x][z]
    for group in range(GROUPS):
        at = slice(group * DG, (group + 1) * DG)
        first = mm(hot_ref[2 * group], tab_ref[2 * group])
        second = mm(hot_ref[2 * group + 1], tab_ref[2 * group + 1])
        cot = jnp.concatenate(
            [c_ref[c, :, at].astype(F32) for c in range(clips)] + [cot_ref[:, at]], axis=0
        )
        residual = latent_ref[:, at]
        gap = residual - first
        gap2 = gap - second
        both = gap + gap2
        grad = mask * (cot + (both if COMMIT == 0.5 else 2.0 * COMMIT * both))
        quant = (mask * (first + second))[:local].astype(BF16)
        bg_ref[:, at] = grad.astype(BF16)
        lg_ref[:, at] = grad[:local]
        for clip in range(clips):
            quant_ref[clip, :, at] = quant[clip * frames : (clip + 1) * frames]
        for level, diff in ((0, gap), (1, gap2)):
            diff = diff[:local]
            high = diff.astype(BF16)
            cgs_ref[2 * group + level, :, :DG] = high
            cgs_ref[2 * group + level, :, DG:] = (diff - high.astype(F32)).astype(BF16)
    size = block // SCALE_GROUPS
    for far in range(2):
        total = summed(2 * far + 1, hott_ref, cgs_ref)
        levels = []
        for place in range(ranks):
            steps, more = pack_part(total[place * block : (place + 1) * block])
            for group, step in enumerate(steps):
                at = place * block + group * size
                send_ref[far, at : at + size, :] = step.astype(jnp.int16)
            levels += more
        levels = jnp.concatenate(levels, axis=0).astype(jnp.int32)
        send_ref[far, CODES:, :] = levels.astype(jnp.int16)


def summed(other, hott_ref, cgs_ref):
    slot = lax.axis_index("tm") ^ other
    pair = mm(hott_ref[slot], cgs_ref[slot])
    return pair[:, :DG] + pair[:, DG:]


def keep_kernel(hott_ref, cgs_ref, keep_ref):
    for far in range(2):
        keep_ref[far] = summed(2 * far, hott_ref, cgs_ref)


def backward_kernel(
    ranks,
    assemble,
    clips,
    window_ref,
    gated_ref,
    bg_ref,
    hs_ref,
    pwt_ref,
    hg_ref,
    *outs,
):
    local = window_ref.shape[0]
    bg = bg_ref[...]
    hidden_grad = (mm(bg, pwt_ref[...]) * hs_ref[...]).astype(BF16)
    hg_ref[...] = hidden_grad
    dil_all = mmg(hidden_grad[:local], window_ref[...], TN)
    dil_grads = [dil_all[:, tap * D : (tap + 1) * D] for tap in range(KERNEL)]
    pw_grad = mmg(bg[:local], gated_ref[:local, :], TN)
    if assemble:
        keep_ref, send_ref, all_ref = outs
        half, small = ranks // 2, 2 * HID // ranks
        out_rows = small // 2
        time, rank = lax.axis_index("tm"), lax.axis_index("clip")
        for tap in range(KERNEL):
            all_ref[tap] = dil_grads[tap]
        for r in range(ranks):
            for side in range(2):
                at = r * small + side * out_rows
                all_ref[KERNEL, r * out_rows : (r + 1) * out_rows, side * DG : (side + 1) * DG] = (
                    pw_grad[at : at + out_rows]
                )
        for other in range(4):
            out = (keep_ref, send_ref)[other % 2]
            for x in range(2):
                for z in range(half):
                    at = pl.multiple_of((rank ^ (2 * z + x)) * out_rows, out_rows)
                    to = (x * half + z) * small
                    for side in range(2):
                        out[other // 2, to + side * out_rows : to + (side + 1) * out_rows, :] = (
                            all_ref[
                                time ^ other, pl.ds(at, out_rows), side * DG : (side + 1) * DG
                            ]
                        )
    else:
        dil_ref, pw_ref = outs
        for tap in range(KERNEL):
            dil_ref[tap] = dil_grads[tap]
        pw_ref[...] = pw_grad


def features_kernel(clips, len_ref, start_ref, lg_ref, hg_ref, d_ref, fg_ref):
    frames = start_ref.shape[0] // clips - 2 * PAD
    local = clips * frames
    wide = hg_ref[...].astype(F32)
    shifted = jnp.concatenate(
        [
            moved(wide, -DILATION, clips, frames),
            hg_ref[:local, :],
            moved(wide, DILATION, clips, frames),
        ],
        axis=1,
    )
    act_grad = mm(shifted, d_ref[...])
    row = lax.broadcasted_iota(jnp.int32, (frames, D), 0) + lax.axis_index("tm") * frames
    for c in range(clips):
        to = slice(c * frames, (c + 1) * frames)
        mask = jnp.where(row < len_ref[c], 1.0, 0.0)
        fg_ref[c] = mask * (lg_ref[to, :] + slope(start_ref[to, :]) * act_grad[to])


def pack_part(value):
    count = SCALE_GROUPS
    rows = value.shape[0]
    size = rows // count
    steps, levels = [], []
    for group in range(count):
        part = value[group * size : (group + 1) * size]
        top = jnp.maximum(jnp.max(jnp.abs(part), axis=0, keepdims=True), 1e-30)
        level = jnp.ceil(jnp.log2(top) * LEVEL_STEPS)
        scale = jnp.exp2(level / -LEVEL_STEPS) * TOP
        steps.append(jnp.round(part * scale).astype(jnp.int32))
        levels.append(level)
    return steps, levels


def unpack_part(steps, level):
    return steps.astype(jnp.int32).astype(F32) * (
        jnp.exp2(level.astype(jnp.int32).astype(F32) / LEVEL_STEPS) / TOP
    )


def send_kernel(groups, rows, keep_ref, got_ref, own_ref, *outs):
    size = rows // SCALE_GROUPS
    for part, blocks in enumerate(groups):
        levels = []
        for place, (jy, start) in enumerate(blocks):
            at = slice(start * rows, (start + 1) * rows)
            if got_ref.dtype == F32:
                other = got_ref[jy, at, :]
            else:
                top = (got_ref.shape[1] // (rows + SCALE_GROUPS)) * rows + start * SCALE_GROUPS
                other = jnp.concatenate(
                    [
                        unpack_part(
                            got_ref[jy, start * rows + g * size : start * rows + (g + 1) * size, :],
                            got_ref[jy, top : top + SCALE_GROUPS, :][g : g + 1],
                        )
                        for g in range(SCALE_GROUPS)
                    ],
                    axis=0,
                )
            value = keep_ref[jy, at, :] + other
            if part == 0:
                own_ref[place] = value
                continue
            steps, more = pack_part(value)
            for group, step in enumerate(steps):
                spot = place * rows + group * size
                outs[part - 1][spot : spot + size, :] = step.astype(jnp.int16)
            levels += more
        if part:
            tail = jnp.concatenate(levels, axis=0).astype(jnp.int32)
            outs[part - 1][len(blocks) * rows :, :] = tail.astype(jnp.int16)


def pass_kernel(rows, own_in, *refs):
    blocks = own_in.shape[0]
    gots, own_ref, outs = refs[:-blocks], refs[-blocks], refs[1 - blocks :]
    size = rows // SCALE_GROUPS
    for place in range(blocks):
        value = own_in[place]
        pieces = [value[g * size : (g + 1) * size] for g in range(SCALE_GROUPS)]
        for got in gots:
            tail = got[blocks * rows :, :]
            for g in range(SCALE_GROUPS):
                index = place * SCALE_GROUPS + g
                spot = place * rows + g * size
                pieces[g] = pieces[g] + unpack_part(
                    got[spot : spot + size, :], tail[index : index + 1]
                )
        if place == 0:
            for g in range(SCALE_GROUPS):
                own_ref[g * size : (g + 1) * size, :] = pieces[g]
            continue
        steps, levels = pack_part(jnp.concatenate(pieces, axis=0))
        out = outs[place - 1]
        for g, step in enumerate(steps):
            out[g * size : (g + 1) * size, :] = step.astype(jnp.int16)
        pad = jnp.zeros((out.shape[0] - rows - len(levels), DG), F32)
        tail = jnp.concatenate(levels + [pad], axis=0).astype(jnp.int32)
        out[rows:, :] = tail.astype(jnp.int16)


def final_kernel(sizes, counts, *refs):
    out_ref, square_ref = refs[-2:]
    squares = jnp.zeros((1, DG), F32)
    place = 0
    for kind, rows in enumerate(sizes):
        own_ref, *gots = refs[sum(counts[:kind]) : sum(counts[: kind + 1])]
        size = rows // SCALE_GROUPS
        for g in range(SCALE_GROUPS):
            at = slice(g * size, (g + 1) * size)
            value = own_ref[at, :]
            for got in gots:
                value = value + unpack_part(got[at, :], got[rows:, :][g : g + 1])
            out_ref[place : place + size, :] = value
            squares = squares + jnp.sum(value * value, axis=0, keepdims=True)
            place += size
    square = jnp.sum(squares, axis=1, keepdims=True)
    square_ref[...] = jnp.broadcast_to(square[None], square_ref.shape)


def stepped(weight, first, second, grad, rate, fix1, fix2):
    first_new = FIRST_DECAY * first + (1.0 - FIRST_DECAY) * grad
    second_new = SECOND_DECAY * second + (1.0 - SECOND_DECAY) * grad * grad
    change = (first_new * fix1) / (jnp.sqrt(second_new * fix2) + EPSILON) + WEIGHT_DECAY * weight
    return weight - rate * change, second_new


def update_kernel(fix_ref, square_ref, *refs):
    pieces = refs[:4]
    dil, pw, table = refs[4:7], refs[7:10], refs[10:13]
    norm_ref = refs[13]
    dil_hbm, pw_hbm, table_hbm = refs[14:17], refs[17:20], refs[20:23]
    dil_out, pw_out, table_out = refs[23:26], refs[26:29], refs[29:32]
    sems = refs[32]
    out_rows = dil[0].shape[1]
    small = 2 * out_rows
    time = lax.axis_index("tm")
    count = KERNEL * D * HID + D * HID + SLOTS * CODES * DG
    norm = jnp.sqrt(jnp.sum(square_ref[...], axis=0)[:1, :1])
    limit = jnp.sqrt(jnp.full((1, 1), float(count), F32))
    scale = limit / jnp.maximum(norm, limit)
    norm_ref[...] = norm
    fixes = (fix_ref[0], fix_ref[1])
    copies = []
    for other in range(4):
        quarter = time ^ other
        piece = pieces[other]
        grad = piece[small:, :] * scale
        state = [v[quarter] for v in table]
        weight, second = stepped(*state, grad, RATE_CODE, *fixes)
        for kind, value in enumerate((weight, grad, second)):
            table_out[kind][quarter] = value
            copies.append(
                pltpu.make_async_copy(
                    table_out[kind].at[quarter], table_hbm[kind].at[quarter], sems.at[len(copies)]
                )
            )
            copies[-1].start()

        @pl.when(quarter < KERNEL)
        def _():
            tap = jnp.minimum(quarter, KERNEL - 1)
            for side in range(2):
                to = slice(side * DG, (side + 1) * DG)
                grad = piece[side * out_rows : (side + 1) * out_rows, :] * scale
                state = [v[tap, :, to] for v in dil]
                weight, second = stepped(*state, grad, BITRATE_FACTOR, *fixes)
                dil_out[0][tap, :, to] = weight
                dil_out[1][tap, :, to] = grad
                dil_out[2][tap, :, to] = second

        @pl.when(quarter == KERNEL)
        def _():
            grad = piece[:small, :] * scale
            weight, second = stepped(*[v[...] for v in pw], grad, BITRATE_FACTOR, *fixes)
            pw_out[0][...] = weight
            pw_out[1][...] = grad
            pw_out[2][...] = second

    for kind in range(3):
        for outs, hbms in ((dil_out, dil_hbm), (pw_out, pw_hbm)):
            copies.append(pltpu.make_async_copy(outs[kind], hbms[kind], sems.at[len(copies)]))
            copies[-1].start()
    for copy in copies:
        copy.wait()


def shards(
    features,
    cotangent,
    clip_lengths,
    code_ids,
    step_count,
    dilated_kernel_weight,
    pointwise_conv,
    codebooks,
    dilated_first_moment,
    dilated_second_moment,
    pointwise_first,
    pointwise_second,
    codebook_first,
    codebook_second,
):
    ranks, times = lax.axis_size("clip"), lax.axis_size("tm")
    rank, time = lax.axis_index("clip"), lax.axis_index("tm")
    clips, frames, _ = features.shape
    half = ranks // 2
    out_rows = HID // ranks
    block = CODES // ranks
    small = 2 * out_rows
    rows = clips * (frames + 2 * PAD)
    smem = pl.BlockSpec(memory_space=pltpu.SMEM)
    hbm = pl.BlockSpec(memory_space=pltpu.HBM)
    shape = jax.ShapeDtypeStruct

    def held(*values):
        return [pltpu.with_memory_space_constraint(v, pltpu.HBM) for v in values]

    assemble = out_rows % 16 == 0
    dil_state = [
        v.transpose(0, 2, 1)
        for v in (dilated_kernel_weight, dilated_first_moment, dilated_second_moment)
    ]
    pw_state = [v.T for v in (pointwise_conv, pointwise_first, pointwise_second)]
    table_state = [codebooks, codebook_first, codebook_second]

    if assemble:
        mine_d, mine_c = pl.pallas_call(
            prep_kernel,
            out_shape=(shape((2, small, DG), BF16), shape((block, DG), BF16)),
            in_specs=[hbm] * 3,
            out_specs=tuple(whole(2)),
            scratch_shapes=[
                pltpu.VMEM((2, out_rows, D), F32),
                pltpu.VMEM((small, DG), F32),
                pltpu.VMEM((block, DG), F32),
                pltpu.SemaphoreType.DMA((4,)),
            ],
            compiler_params=params(),
            name="prep",
        )(*held(dil_state[0], pw_state[0], codebooks))
    else:
        taps = dil_state[0].astype(BF16).reshape(KERNEL, out_rows, 2, DG).transpose(0, 2, 1, 3)
        quarters = jnp.concatenate(
            [taps.reshape(KERNEL, small, DG), pw_state[0].astype(BF16)[None]], axis=0
        )
        mine_d = jnp.take(quarters, time % 2 + jnp.array([0, 2]), axis=0)
        mine_c = lax.dynamic_index_in_dim(codebooks, time, 0, keepdims=False).astype(BF16)

    mine_c, mine_d, late_ids = lax.optimization_barrier((mine_c, mine_d, code_ids))
    near, far = pl.pallas_call(
        pack_kernel,
        out_shape=(shape((clips, 2 * PAD, 2 * D), BF16),) * 2,
        in_specs=[hbm] * 3,
        out_specs=tuple(whole(2)),
        scratch_shapes=[
            pltpu.VMEM((2, 2, clips, 2 * PAD, D), BF16),
            pltpu.VMEM(code_ids.shape, jnp.int32),
            pltpu.SemaphoreType.DMA((5,)),
        ],
        compiler_params=params(),
        name="pack",
    )(*held(features, cotangent, late_ids))
    line_c = [swap(mine_c, 2 * z, 0) for z in range(1, half)]
    across = swap(mine_d, 1, 0)
    near = lax.ppermute(near, "tm", [(i, i ^ 1) for i in range(times)])
    pairs = [(i, i + 1) for i in range(1, times - 1, 2)]
    far = lax.ppermute(far, "tm", pairs + [(b, a) for a, b in pairs])
    near, far, *line_c = lax.optimization_barrier((near, far, *line_c))
    line_c = jnp.stack([mine_c] + line_c, axis=0)
    pair_d = jnp.stack([mine_d, across], axis=0)
    line_c, late_ids = lax.optimization_barrier((line_c, code_ids))
    hot, hott = pl.pallas_call(
        functools.partial(own_kernel, ranks),
        out_shape=(
            shape((SLOTS, rows, CODES), BF16),
            shape((SLOTS, CODES, clips * frames), BF16),
        ),
        in_specs=[smem] + whole(1),
        out_specs=tuple(whole(2)),
        compiler_params=params(8),
        name="own",
    )(clip_lengths, late_ids)
    plane_c = [line_c, swap(line_c, 1, 0), swap(line_c, 0, 2), swap(line_c, 1, 2)]
    line_d = [pair_d] + [swap(pair_d, 2 * z, 0) for z in range(1, half)]

    start, act, windows, cot, mask, hot = pl.pallas_call(
        functools.partial(margin_kernel, ranks),
        out_shape=(
            shape((rows, D), F32),
            shape((rows, D), BF16),
            shape((clips * frames, KERNEL * D), BF16),
            shape((2 * PAD * clips, D), F32),
            shape((rows, DG), F32),
            shape(hot.shape, BF16),
        ),
        in_specs=[smem] + whole(4),
        out_specs=tuple(whole(6)),
        input_output_aliases={4: 5},
        compiler_params=params(8),
        name="margin",
    )(clip_lengths, features, near, far, hot)

    act, *line_d = lax.optimization_barrier((act, *line_d))
    pieces_d = line_d + [swap(v, 0, 1) for v in line_d]
    turned = [swap(v, 0, 1) for v in plane_c]
    pieces_c = plane_c[:2] + turned[:2] + plane_c[2:] + turned[2:]

    weights = (shape((KERNEL * HID, D), BF16), shape((D, HID), BF16))
    given = pieces_d
    if not assemble:
        order = rank ^ jnp.arange(ranks)
        stacked = jnp.stack(pieces_d, axis=0).reshape(2, half, 2, 2, small, DG)
        stacked = jnp.take(stacked, time % 2 ^ jnp.arange(2), axis=0)
        stacked = stacked.transpose(3, 0, 1, 2, 4, 5).reshape(4, ranks, small, DG)
        stacked = jnp.take(stacked, order, axis=1)
        dil = stacked[:KERNEL].reshape(KERNEL, ranks, 2, out_rows, DG)
        dil = dil.transpose(0, 1, 3, 2, 4).reshape(KERNEL * HID, D)
        given = [dil, stacked[3].reshape(D, HID)]
    outs = pl.pallas_call(
        functools.partial(conv_kernel, ranks, assemble, clips),
        out_shape=(weights if assemble else ())
        + (shape((rows, HID), BF16), shape((rows, HID), F32), shape((rows, D), F32)),
        in_specs=whole(2 + len(given)),
        out_specs=tuple(whole(5 if assemble else 3)),
        scratch_shapes=[pltpu.VMEM((4, HID, D), BF16)] if assemble else [],
        compiler_params=params(10),
        name="conv",
    )(start, act, *given)
    dil, pwt, gated, hs, latent = tuple(outs) if assemble else tuple(given) + tuple(outs)

    quant, send, bg, lg, cgs = pl.pallas_call(
        functools.partial(quant_kernel, ranks),
        out_shape=(
            shape((clips, frames, D), BF16),
            shape((2, CODES + SCALE_GROUPS * ranks, DG), jnp.int16),
            shape((rows, D), BF16),
            shape((clips * frames, D), F32),
            shape((SLOTS, clips * frames, 2 * DG), BF16),
        ),
        in_specs=whole(6 + len(pieces_c)),
        out_specs=tuple(whole(5)),
        scratch_shapes=[
            pltpu.VMEM((SLOTS, CODES, DG), BF16),
        ],
        compiler_params=params(16),
        name="quant",
    )(mask, latent, cotangent, cot, hot, hott, *pieces_c)

    keep = pl.pallas_call(
        keep_kernel,
        out_shape=shape((2, CODES, DG), F32),
        in_specs=whole(2),
        out_specs=whole(1)[0],
        compiler_params=params(8),
        name="keep",
    )(hott, cgs)

    if assemble:
        grads = (shape((2, ranks * small, DG), F32),) * 2
    else:
        grads = (shape((KERNEL, HID, D), F32), shape((D, HID), F32))
    hg, first_grad, second_grad = pl.pallas_call(
        functools.partial(backward_kernel, ranks, assemble, clips),
        out_shape=(shape((rows, HID), BF16),) + grads,
        in_specs=whole(5),
        out_specs=tuple(whole(3)),
        scratch_shapes=[pltpu.VMEM((4, HID, D), F32)] if assemble else [],
        compiler_params=params(16),
        name="backward",
    )(windows, gated, bg, hs, pwt)
    fg = pl.pallas_call(
        functools.partial(features_kernel, clips),
        out_shape=shape((clips, frames, D), F32),
        in_specs=[smem] + whole(4),
        out_specs=whole(1)[0],
        compiler_params=params(12),
        name="features",
    )(clip_lengths, start, lg, hg, dil)

    if assemble:
        keep_d, send_d = first_grad, second_grad
    else:
        parts = jnp.concatenate(
            [
                first_grad.reshape(KERNEL, ranks, out_rows, 2, DG)
                .transpose(0, 1, 3, 2, 4)
                .reshape(KERNEL, ranks, small, DG),
                second_grad.reshape(1, ranks, small, DG),
            ],
            axis=0,
        )
        seq = jnp.concatenate([jnp.arange(0, ranks, 2), jnp.arange(1, ranks, 2)])
        parts = jnp.take(jnp.take(parts, time ^ jnp.arange(4), axis=0), rank ^ seq, axis=1)
        parts = parts.reshape(2, 2, ranks * small, DG)
        keep_d, send_d = parts[:, 0], parts[:, 1]

    def sent(keep, got, groups, size, tag):
        count = len(groups[0])
        packed = count * size + count * SCALE_GROUPS
        return pl.pallas_call(
            functools.partial(send_kernel, groups, size),
            out_shape=(shape((count, size, DG), F32),)
            + (shape((packed, DG), jnp.int16),) * (len(groups) - 1),
            in_specs=whole(2),
            out_specs=tuple(whole(len(groups))),
            compiler_params=params(),
            name="send_" + tag,
        )(keep, got)

    def passed(parts, size, tag):
        count = parts[0].shape[0]
        return pl.pallas_call(
            functools.partial(pass_kernel, size),
            out_shape=(shape((size, DG), F32),)
            + (shape((size + 8, DG), jnp.int16),) * (count - 1),
            in_specs=whole(len(parts)),
            out_specs=tuple(whole(count)),
            compiler_params=params(),
            name="pass_" + tag,
        )(*parts)

    def over_plane(parts):
        return [parts[0], swap(parts[1], 1, 0), swap(parts[2], 0, 2), swap(parts[3], 1, 2)]

    def over_line(parts):
        return [parts[0]] + [swap(parts[z], 2 * z, 0) for z in range(1, half)]

    by_plane = [[(jy, x * half + z) for z in range(half)] for jy in range(2) for x in range(2)]
    order = (0, 2, 1, 3) if half == 4 else tuple(range(half))
    by_line = [[(jy, x * half + z) for jy in range(2) for x in range(2)] for z in order]
    got_c, got_d = swap(send, 0, 1), swap(send_d, 0, 1)
    parts_c = over_plane(sent(keep, got_c, by_plane, block, "codes"))
    parts_c[0], keep_d = lax.optimization_barrier((parts_c[0], keep_d))
    parts_d = sent(keep_d, got_d, by_line, small, "conv")
    parts_d = [parts_d[0]] + [swap(parts_d[i], 2 * order[i], 0) for i in range(1, half)]
    fg, parts_c[0] = lax.optimization_barrier((fg, parts_c[0]))
    parts_c = over_line(passed(parts_c, block, "codes"))
    parts_c[1], parts_d[0] = lax.optimization_barrier((parts_c[1], parts_d[0]))
    parts_d = over_plane(passed(parts_d, small, "conv"))
    total = small + block
    piece, squares = pl.pallas_call(
        functools.partial(final_kernel, (small, block), (4, half)),
        out_shape=(shape((total, DG), F32), shape((ranks * times, 8, 128), F32)),
        in_specs=whole(4 + half),
        out_specs=tuple(whole(2)),
        compiler_params=params(),
        name="final",
    )(*parts_d, *parts_c)

    across = swap(piece, 0, 2)
    squares = lax.all_to_all(squares, ("clip", "tm"), 0, 0, tiled=True)
    fours = [piece, swap(piece, 0, 1), across, swap(across, 0, 1)]
    steps = step_count[0].astype(F32)
    decays = jnp.stack([1.0 / (1.0 - FIRST_DECAY**steps), 1.0 / (1.0 - SECOND_DECAY**steps)])
    if assemble:
        state = dil_state + pw_state + table_state
        norm, *new = pl.pallas_call(
            update_kernel,
            out_shape=(shape((1, 1), F32),) + tuple(shape(v.shape, F32) for v in state),
            in_specs=[smem] + whole(14),
            out_specs=tuple(whole(1) + [hbm] * 9),
            scratch_shapes=[pltpu.VMEM(v.shape, F32) for v in state]
            + [pltpu.SemaphoreType.DMA((18,))],
            compiler_params=params(8),
            name="update",
        )(decays, squares, *fours, *state)
        norm = norm.reshape(1)
        dil_new, pw_new, table_new = new[:3], new[3:6], new[6:]
    else:
        four = jnp.take(jnp.stack(fours, axis=0), time ^ jnp.arange(4), axis=0)
        raw = four[:KERNEL, :small].reshape(KERNEL, 2, out_rows, DG)
        raw = raw.transpose(0, 2, 1, 3).reshape(KERNEL, out_rows, D)
        count = KERNEL * D * HID + D * HID + SLOTS * CODES * DG
        limit = jnp.sqrt(jnp.float32(count))
        norm = jnp.sqrt(jnp.sum(squares, axis=0)[0, :1])
        scale = limit / jnp.maximum(norm[0], limit)
        new = []
        for state, grad, rate in (
            (dil_state, raw, BITRATE_FACTOR),
            (pw_state, four[3, :small], BITRATE_FACTOR),
            (table_state, four[:, small:], RATE_CODE),
        ):
            grad = grad * scale
            weight, second = stepped(*state, grad, rate, decays[0], decays[1])
            new.append((weight, grad, second))
        dil_new, pw_new, table_new = new
    return (
        quant,
        fg,
        norm,
        *[v.transpose(0, 2, 1) for v in dil_new],
        *[v.T for v in pw_new],
        *table_new,
    )


def solution(mesh):
    in_specs = (
        P("clip", "tm", None),
        P("clip", "tm", None),
        P("clip"),
        P(None, "clip", "tm"),
        P(),
        P(None, None, "clip"),
        P(None, "clip"),
        P(None, "clip", None),
        P(None, None, "clip"),
        P(None, None, "clip"),
        P(None, "clip"),
        P(None, "clip"),
        P(None, "clip", None),
        P(None, "clip", None),
    )
    out_specs = (
        P("clip", "tm", None),
        P("clip", "tm", None),
        P(),
        P(None, None, "clip"),
        P(None, None, "clip"),
        P(None, None, "clip"),
        P(None, "clip"),
        P(None, "clip"),
        P(None, "clip"),
        P(None, "clip", None),
        P(None, "clip", None),
        P(None, "clip", None),
    )
    return jax.shard_map(shards, mesh=mesh, in_specs=in_specs, out_specs=out_specs, check_vma=False)
```

```python
import functools

import jax
import jax.numpy as jnp
from jax import lax
from jax.experimental import pallas as pl
from jax.experimental.pallas import tpu as pltpu
from jax.sharding import PartitionSpec as P

D = 512
HID = 256
CODES = 1024
GROUPS = 2
LEVELS = 2
SLOTS = 4
KERNEL = 3
DILATION = 3
DG = 256
PAD = 8

COMMIT = 0.25
FIRST_DECAY = 0.9
SECOND_DECAY = 0.99
EPSILON = 1e-08
WEIGHT_DECAY = 0.01
BITRATE_FACTOR = 0.02
RATE_CODE = 0.5

F32 = jnp.float32
BF16 = jnp.bfloat16
NT = (((1,), (1,)), ((), ()))
TN = (((0,), (0,)), ((), ()))
LEVEL_STEPS = 256.0
TOP = 32000.0
SCALE_GROUPS = 4
MIB = 1024 * 1024


def params(mib=6):
    return pltpu.CompilerParams(vmem_limit_bytes=mib * MIB)


def whole(count):
    return [pl.BlockSpec(memory_space=pltpu.VMEM)] * count


def mm(a, b):
    return jnp.dot(a, b, preferred_element_type=F32)


def mmg(a, b, dims):
    return lax.dot_general(a, b, dims, preferred_element_type=F32)


def slope(v):
    return jnp.where(v > 0, 1.0, jnp.exp(jnp.minimum(v, 0.0)))


def elu(v):
    return jnp.where(v > 0, v, jnp.exp(jnp.minimum(v, 0.0)) - 1.0)


def swap(value, clip_mask, time_mask):
    clips, times = lax.axis_size("clip"), lax.axis_size("tm")
    pairs = [
        (c * times + t, (c ^ clip_mask) * times + (t ^ time_mask))
        for c in range(clips)
        for t in range(times)
    ]
    return lax.ppermute(value, ("clip", "tm"), pairs)


def prep_kernel(dil_hbm, pw_hbm, table_hbm, conv_ref, code_ref, dil_ref, pw_ref, table_ref, sems):
    time = lax.axis_index("tm")
    bit = time % 2
    out_rows = pw_ref.shape[0] // 2
    second = jnp.minimum(2 + bit, KERNEL - 1)
    copies = [
        pltpu.make_async_copy(table_hbm.at[time], table_ref, sems.at[0]),
        pltpu.make_async_copy(dil_hbm.at[bit], dil_ref.at[0], sems.at[1]),
        pltpu.make_async_copy(dil_hbm.at[second], dil_ref.at[1], sems.at[2]),
        pltpu.make_async_copy(pw_hbm, pw_ref, sems.at[3]),
    ]
    for copy in copies:
        copy.start()
    copies[0].wait()
    code_ref[...] = table_ref[...].astype(BF16)
    for copy in copies[1:]:
        copy.wait()
    for side in range(2):
        for part in range(2):
            conv_ref[part, side * out_rows : (side + 1) * out_rows, :] = dil_ref[
                part, :, side * DG : (side + 1) * DG
            ].astype(BF16)

    @pl.when(bit == 1)
    def _():
        conv_ref[1] = pw_ref[...].astype(BF16)


def renamed(values, ranks):
    block = CODES // ranks
    step = (values // block) ^ lax.axis_index("clip")
    place = (step % 2) * (ranks // 2) + step // 2
    return place * block + values % block


def masks(clips, frames, len_ref, columns):
    base = lax.axis_index("tm") * frames

    def mark(first, count, clip):
        where = lax.broadcasted_iota(jnp.int32, (count, columns), 0) + first
        return jnp.where((where >= 0) & (where < len_ref[clip]), 1.0, 0.0)

    own = [mark(base, frames, c) for c in range(clips)]
    margins = [
        mark(first, PAD, c) for c in range(clips) for first in (base - PAD, base + frames)
    ]
    return jnp.concatenate(own + margins, axis=0)


def widened(value, clip, clips, frames):
    at = clips * frames + 2 * PAD * clip
    return jnp.concatenate(
        [
            value[at : at + PAD],
            value[clip * frames : (clip + 1) * frames],
            value[at + PAD : at + 2 * PAD],
        ],
        axis=0,
    )


def pack_kernel(f_hbm, c_hbm, ids_hbm, near_ref, far_ref, buf, ids_ref, sems):
    clips, frames, _ = f_hbm.shape
    edge = 2 * PAD
    odd = lax.axis_index("tm") % 2
    copies = [pltpu.make_async_copy(ids_hbm, ids_ref, sems.at[4])]
    for kind, source in enumerate((f_hbm, c_hbm)):
        for side, at in enumerate((frames - edge, 0)):
            copies.append(
                pltpu.make_async_copy(
                    source.at[:, pl.ds(at, edge), :], buf.at[kind, side], sems.at[2 * kind + side]
                )
            )
    for copy in copies:
        copy.start()
    for copy in copies:
        copy.wait()
    outs = []
    for side in range(2):
        at = slice(PAD, 2 * PAD) if side == 0 else slice(0, PAD)
        parts = []
        for c in range(clips):
            ids = ids_ref[:, c, :]
            if side == 0:
                ids = pltpu.roll(ids, PAD, 1)
            both = jnp.concatenate([ids // 32, ids % 32], axis=0).astype(F32)
            both = jnp.concatenate([both, jnp.zeros((8, 2 * D - frames), F32)], axis=1)
            ends = [buf[kind, side, c].astype(F32)[at] for kind in range(2)]
            parts.append(jnp.concatenate([jnp.concatenate(ends, axis=1), both], axis=0))
        outs.append(parts)
    for c in range(clips):
        last, first = outs[0][c], outs[1][c]
        near_ref[c] = jnp.where(odd == 1, first, last).astype(BF16)
        far_ref[c] = jnp.where(odd == 1, last, first).astype(BF16)


def own_kernel(ranks, len_ref, ids_ref, hot_ref, hott_ref):
    _, clips, frames = ids_ref.shape
    codes = lax.broadcasted_iota(jnp.int32, (frames, CODES), 1)
    spots = lax.broadcasted_iota(jnp.int32, (CODES, frames), 0)
    where = lax.broadcasted_iota(jnp.int32, (1, frames), 1) + lax.axis_index("tm") * frames
    for c in range(clips):
        weight = jnp.where(where < len_ref[c], -2.0, 0.0)
        ids = renamed(ids_ref[:, c, :], ranks)
        turned = jnp.concatenate([ids.astype(F32), jnp.zeros((8 - SLOTS, frames), F32)], axis=0)
        turned = turned.T.astype(jnp.int32)
        at = slice(c * frames, (c + 1) * frames)
        for slot in range(SLOTS):
            hot_ref[slot, at, :] = jnp.where(codes == turned[:, slot : slot + 1], 1.0, 0.0).astype(
                BF16
            )
            hott_ref[slot, :, at] = jnp.where(spots == ids[slot : slot + 1], weight, 0.0).astype(BF16)
    hot_ref[:, clips * frames :, :] = jnp.zeros((SLOTS, 2 * PAD * clips, CODES), BF16)


def moved(value, shift, clips, frames):
    span = frames + 2 * PAD
    return jnp.concatenate(
        [
            pltpu.roll(widened(value, c, clips, frames), shift % span, 0)[PAD : PAD + frames]
            for c in range(clips)
        ],
        axis=0,
    ).astype(BF16)


def margin_kernel(
    ranks,
    len_ref,
    f_ref,
    near_ref,
    far_ref,
    old_ref,
    start_ref,
    act_ref,
    window_ref,
    cot_ref,
    mask_ref,
    hot_ref,
):
    del old_ref
    clips, frames, _ = f_ref.shape
    odd = lax.axis_index("tm") % 2
    both = []
    for c in range(clips):
        near, far = near_ref[c].astype(F32), far_ref[c].astype(F32)
        both += [jnp.where(odd == 1, near, far), jnp.where(odd == 1, far, near)]
    mask = masks(clips, frames, len_ref, D)
    mask_ref[...] = mask[:, :DG]
    start = mask * jnp.concatenate(
        [f_ref[c].astype(F32) for c in range(clips)] + [part[:PAD, :D] for part in both], axis=0
    )
    start_ref[...] = start
    act = elu(start).astype(BF16)
    act_ref[...] = act
    wide = act.astype(F32)
    for tap in range(KERNEL):
        shift = (1 - tap) * DILATION
        window_ref[:, tap * D : (tap + 1) * D] = (
            moved(wide, shift, clips, frames) if shift else act[: clips * frames]
        )
    cot_ref[...] = jnp.concatenate([part[:PAD, D:] for part in both], axis=0)
    turned = jnp.concatenate([part[PAD:, :128].T[:PAD] for part in both], axis=0)
    ids = renamed((turned[:, :SLOTS] * 32.0 + turned[:, SLOTS : 2 * SLOTS]).astype(jnp.int32), ranks)
    codes = lax.broadcasted_iota(jnp.int32, (2 * PAD * clips, CODES), 1)
    for slot in range(SLOTS):
        hot_ref[slot, clips * frames :, :] = jnp.where(
            codes == ids[:, slot : slot + 1], 1.0, 0.0
        ).astype(BF16)


def assembled(ranks, pieces, d_ref, pwt_ref, all_ref):
    half, small = ranks // 2, 2 * HID // ranks
    out_rows = small // 2
    bit, rank = lax.axis_index("tm") % 2, lax.axis_index("clip")
    for other in range(2):
        for z in range(half):
            piece = pieces[other * half + z]
            for x in range(2):
                at = pl.multiple_of((rank ^ (2 * z + x)) * out_rows, out_rows)
                for part in range(2):
                    for side in range(2):
                        all_ref[
                            2 * part + (bit ^ other),
                            pl.ds(at, out_rows),
                            side * DG : (side + 1) * DG,
                        ] = piece[x, part, side * out_rows : (side + 1) * out_rows, :]
    for tap in range(KERNEL):
        d_ref[tap * HID : (tap + 1) * HID, :] = all_ref[tap]
    for r in range(ranks):
        for side in range(2):
            to = r * small + side * out_rows
            pwt_ref[to : to + out_rows, :] = all_ref[
                KERNEL, r * out_rows : (r + 1) * out_rows, side * DG : (side + 1) * DG
            ]


def conv_kernel(ranks, assemble, clips, start_ref, act_ref, *refs):
    if assemble:
        pieces, refs = refs[:ranks], refs[ranks:]
        d_ref, pwt_ref, gated_ref, hs_ref, latent_ref, all_ref = refs
        assembled(ranks, pieces, d_ref, pwt_ref, all_ref)
    else:
        d_ref, pwt_ref, gated_ref, hs_ref, latent_ref = refs
    rows = start_ref.shape[0]
    taps = mmg(act_ref[...], d_ref[...], NT)
    frames = rows // clips - 2 * PAD
    span = frames + 2 * PAD
    own, margins = [], []
    for c in range(clips):
        wide = widened(taps, c, clips, frames)
        part = (
            pltpu.roll(wide[:, :HID], DILATION, 0)
            + wide[:, HID : 2 * HID]
            + pltpu.roll(wide[:, 2 * HID :], span - DILATION, 0)
        )
        own.append(part[PAD : PAD + frames])
        margins += [part[:PAD], part[PAD + frames :]]
    hidden = jnp.concatenate(own + margins, axis=0)
    hs_ref[...] = slope(hidden)
    gated = elu(hidden).astype(BF16)
    gated_ref[...] = gated
    latent_ref[...] = start_ref[...] + mmg(gated, pwt_ref[...], NT)


def quant_kernel(ranks, mask_ref, latent_ref, c_ref, cot_ref, hot_ref, hott_ref, *refs):
    half, block = ranks // 2, CODES // ranks
    pieces, refs = refs[:8], refs[8:]
    quant_ref, send_ref, bg_ref, lg_ref, cgs_ref, tab_ref = refs
    clips, frames, _ = c_ref.shape
    time = lax.axis_index("tm")
    mask = mask_ref[...]
    local = clips * frames
    for other in range(SLOTS):
        slot = time ^ other
        for x in range(2):
            for z in range(half):
                spot = (x * half + z) * block
                tab_ref[slot, spot : spot + block, :] = pieces[2 * other + x][z]
    for group in range(GROUPS):
        at = slice(group * DG, (group + 1) * DG)
        first = mm(hot_ref[2 * group], tab_ref[2 * group])
        second = mm(hot_ref[2 * group + 1], tab_ref[2 * group + 1])
        cot = jnp.concatenate(
            [c_ref[c, :, at].astype(F32) for c in range(clips)] + [cot_ref[:, at]], axis=0
        )
        residual = latent_ref[:, at]
        gap = residual - first
        gap2 = gap - second
        both = gap + gap2
        grad = mask * (cot + (both if COMMIT == 0.5 else 2.0 * COMMIT * both))
        quant = (mask * (first + second))[:local].astype(BF16)
        bg_ref[:, at] = grad.astype(BF16)
        lg_ref[:, at] = grad[:local]
        for clip in range(clips):
            quant_ref[clip, :, at] = quant[clip * frames : (clip + 1) * frames]
        for level, diff in ((0, gap), (1, gap2)):
            diff = diff[:local]
            high = diff.astype(BF16)
            cgs_ref[2 * group + level, :, :DG] = high
            cgs_ref[2 * group + level, :, DG:] = (diff - high.astype(F32)).astype(BF16)
    size = block // SCALE_GROUPS
    for far in range(2):
        total = summed(2 * far + 1, hott_ref, cgs_ref)
        levels = []
        for place in range(ranks):
            steps, more = pack_part(total[place * block : (place + 1) * block])
            for group, step in enumerate(steps):
                at = place * block + group * size
                send_ref[far, at : at + size, :] = step.astype(jnp.int16)
            levels += more
        levels = jnp.concatenate(levels, axis=0).astype(jnp.int32)
        send_ref[far, CODES:, :] = levels.astype(jnp.int16)


def summed(other, hott_ref, cgs_ref):
    slot = lax.axis_index("tm") ^ other
    pair = mm(hott_ref[slot], cgs_ref[slot])
    return pair[:, :DG] + pair[:, DG:]


def keep_kernel(hott_ref, cgs_ref, keep_ref):
    for far in range(2):
        keep_ref[far] = summed(2 * far, hott_ref, cgs_ref)


def backward_kernel(
    ranks,
    assemble,
    clips,
    window_ref,
    gated_ref,
    bg_ref,
    hs_ref,
    pwt_ref,
    hg_ref,
    *outs,
):
    local = window_ref.shape[0]
    bg = bg_ref[...]
    hidden_grad = (mm(bg, pwt_ref[...]) * hs_ref[...]).astype(BF16)
    hg_ref[...] = hidden_grad
    dil_all = mmg(hidden_grad[:local], window_ref[...], TN)
    dil_grads = [dil_all[:, tap * D : (tap + 1) * D] for tap in range(KERNEL)]
    pw_grad = mmg(bg[:local], gated_ref[:local, :], TN)
    if assemble:
        keep_ref, send_ref, all_ref = outs
        half, small = ranks // 2, 2 * HID // ranks
        out_rows = small // 2
        time, rank = lax.axis_index("tm"), lax.axis_index("clip")
        for tap in range(KERNEL):
            all_ref[tap] = dil_grads[tap]
        for r in range(ranks):
            for side in range(2):
                at = r * small + side * out_rows
                all_ref[KERNEL, r * out_rows : (r + 1) * out_rows, side * DG : (side + 1) * DG] = (
                    pw_grad[at : at + out_rows]
                )
        for other in range(4):
            out = (keep_ref, send_ref)[other % 2]
            for x in range(2):
                for z in range(half):
                    at = pl.multiple_of((rank ^ (2 * z + x)) * out_rows, out_rows)
                    to = (x * half + z) * small
                    for side in range(2):
                        out[other // 2, to + side * out_rows : to + (side + 1) * out_rows, :] = (
                            all_ref[
                                time ^ other, pl.ds(at, out_rows), side * DG : (side + 1) * DG
                            ]
                        )
    else:
        dil_ref, pw_ref = outs
        for tap in range(KERNEL):
            dil_ref[tap] = dil_grads[tap]
        pw_ref[...] = pw_grad


def features_kernel(clips, len_ref, start_ref, lg_ref, hg_ref, d_ref, fg_ref):
    frames = start_ref.shape[0] // clips - 2 * PAD
    local = clips * frames
    wide = hg_ref[...].astype(F32)
    shifted = jnp.concatenate(
        [
            moved(wide, -DILATION, clips, frames),
            hg_ref[:local, :],
            moved(wide, DILATION, clips, frames),
        ],
        axis=1,
    )
    act_grad = mm(shifted, d_ref[...])
    row = lax.broadcasted_iota(jnp.int32, (frames, D), 0) + lax.axis_index("tm") * frames
    for c in range(clips):
        to = slice(c * frames, (c + 1) * frames)
        mask = jnp.where(row < len_ref[c], 1.0, 0.0)
        fg_ref[c] = mask * (lg_ref[to, :] + slope(start_ref[to, :]) * act_grad[to])


def pack_part(value):
    count = SCALE_GROUPS
    rows = value.shape[0]
    size = rows // count
    steps, levels = [], []
    for group in range(count):
        part = value[group * size : (group + 1) * size]
        top = jnp.maximum(jnp.max(jnp.abs(part), axis=0, keepdims=True), 1e-30)
        level = jnp.ceil(jnp.log2(top) * LEVEL_STEPS)
        scale = jnp.exp2(level / -LEVEL_STEPS) * TOP
        steps.append(jnp.round(part * scale).astype(jnp.int32))
        levels.append(level)
    return steps, levels


def unpack_part(steps, level):
    return steps.astype(jnp.int32).astype(F32) * (
        jnp.exp2(level.astype(jnp.int32).astype(F32) / LEVEL_STEPS) / TOP
    )


def send_kernel(groups, rows, keep_ref, got_ref, own_ref, *outs):
    size = rows // SCALE_GROUPS
    for part, blocks in enumerate(groups):
        levels = []
        for place, (jy, start) in enumerate(blocks):
            at = slice(start * rows, (start + 1) * rows)
            if got_ref.dtype == F32:
                other = got_ref[jy, at, :]
            else:
                top = (got_ref.shape[1] // (rows + SCALE_GROUPS)) * rows + start * SCALE_GROUPS
                other = jnp.concatenate(
                    [
                        unpack_part(
                            got_ref[jy, start * rows + g * size : start * rows + (g + 1) * size, :],
                            got_ref[jy, top : top + SCALE_GROUPS, :][g : g + 1],
                        )
                        for g in range(SCALE_GROUPS)
                    ],
                    axis=0,
                )
            value = keep_ref[jy, at, :] + other
            if part == 0:
                own_ref[place] = value
                continue
            steps, more = pack_part(value)
            for group, step in enumerate(steps):
                spot = place * rows + group * size
                outs[part - 1][spot : spot + size, :] = step.astype(jnp.int16)
            levels += more
        if part:
            tail = jnp.concatenate(levels, axis=0).astype(jnp.int32)
            outs[part - 1][len(blocks) * rows :, :] = tail.astype(jnp.int16)


def pass_kernel(rows, own_in, *refs):
    blocks = own_in.shape[0]
    gots, own_ref, outs = refs[:-blocks], refs[-blocks], refs[1 - blocks :]
    size = rows // SCALE_GROUPS
    for place in range(blocks):
        value = own_in[place]
        pieces = [value[g * size : (g + 1) * size] for g in range(SCALE_GROUPS)]
        for got in gots:
            tail = got[blocks * rows :, :]
            for g in range(SCALE_GROUPS):
                index = place * SCALE_GROUPS + g
                spot = place * rows + g * size
                pieces[g] = pieces[g] + unpack_part(
                    got[spot : spot + size, :], tail[index : index + 1]
                )
        if place == 0:
            for g in range(SCALE_GROUPS):
                own_ref[g * size : (g + 1) * size, :] = pieces[g]
            continue
        steps, levels = pack_part(jnp.concatenate(pieces, axis=0))
        out = outs[place - 1]
        for g, step in enumerate(steps):
            out[g * size : (g + 1) * size, :] = step.astype(jnp.int16)
        pad = jnp.zeros((out.shape[0] - rows - len(levels), DG), F32)
        tail = jnp.concatenate(levels + [pad], axis=0).astype(jnp.int32)
        out[rows:, :] = tail.astype(jnp.int16)


def final_kernel(sizes, counts, *refs):
    out_ref, square_ref = refs[-2:]
    squares = jnp.zeros((1, DG), F32)
    place = 0
    for kind, rows in enumerate(sizes):
        own_ref, *gots = refs[sum(counts[:kind]) : sum(counts[: kind + 1])]
        size = rows // SCALE_GROUPS
        for g in range(SCALE_GROUPS):
            at = slice(g * size, (g + 1) * size)
            value = own_ref[at, :]
            for got in gots:
                value = value + unpack_part(got[at, :], got[rows:, :][g : g + 1])
            out_ref[place : place + size, :] = value
            squares = squares + jnp.sum(value * value, axis=0, keepdims=True)
            place += size
    square = jnp.sum(squares, axis=1, keepdims=True)
    square_ref[...] = jnp.broadcast_to(square[None], square_ref.shape)


def stepped(weight, first, second, grad, rate, fix1, fix2):
    first_new = FIRST_DECAY * first + (1.0 - FIRST_DECAY) * grad
    second_new = SECOND_DECAY * second + (1.0 - SECOND_DECAY) * grad * grad
    change = (first_new * fix1) / (jnp.sqrt(second_new * fix2) + EPSILON) + WEIGHT_DECAY * weight
    return weight - rate * change, second_new


def update_kernel(fix_ref, square_ref, *refs):
    pieces = refs[:4]
    dil, pw, table = refs[4:7], refs[7:10], refs[10:13]
    norm_ref = refs[13]
    dil_hbm, pw_hbm, table_hbm = refs[14:17], refs[17:20], refs[20:23]
    dil_out, pw_out, table_out = refs[23:26], refs[26:29], refs[29:32]
    sems = refs[32]
    out_rows = dil[0].shape[1]
    small = 2 * out_rows
    time = lax.axis_index("tm")
    count = KERNEL * D * HID + D * HID + SLOTS * CODES * DG
    norm = jnp.sqrt(jnp.sum(square_ref[...], axis=0)[:1, :1])
    limit = jnp.sqrt(jnp.full((1, 1), float(count), F32))
    scale = limit / jnp.maximum(norm, limit)
    norm_ref[...] = norm
    fixes = (fix_ref[0], fix_ref[1])
    copies = []
    for other in range(4):
        quarter = time ^ other
        piece = pieces[other]
        grad = piece[small:, :] * scale
        state = [v[quarter] for v in table]
        weight, second = stepped(*state, grad, RATE_CODE, *fixes)
        for kind, value in enumerate((weight, grad, second)):
            table_out[kind][quarter] = value
            copies.append(
                pltpu.make_async_copy(
                    table_out[kind].at[quarter], table_hbm[kind].at[quarter], sems.at[len(copies)]
                )
            )
            copies[-1].start()

        @pl.when(quarter < KERNEL)
        def _():
            tap = jnp.minimum(quarter, KERNEL - 1)
            for side in range(2):
                to = slice(side * DG, (side + 1) * DG)
                grad = piece[side * out_rows : (side + 1) * out_rows, :] * scale
                state = [v[tap, :, to] for v in dil]
                weight, second = stepped(*state, grad, BITRATE_FACTOR, *fixes)
                dil_out[0][tap, :, to] = weight
                dil_out[1][tap, :, to] = grad
                dil_out[2][tap, :, to] = second

        @pl.when(quarter == KERNEL)
        def _():
            grad = piece[:small, :] * scale
            weight, second = stepped(*[v[...] for v in pw], grad, BITRATE_FACTOR, *fixes)
            pw_out[0][...] = weight
            pw_out[1][...] = grad
            pw_out[2][...] = second

    for kind in range(3):
        for outs, hbms in ((dil_out, dil_hbm), (pw_out, pw_hbm)):
            copies.append(pltpu.make_async_copy(outs[kind], hbms[kind], sems.at[len(copies)]))
            copies[-1].start()
    for copy in copies:
        copy.wait()


def shards(
    features,
    cotangent,
    clip_lengths,
    code_ids,
    step_count,
    dilated_kernel_weight,
    pointwise_conv,
    codebooks,
    dilated_first_moment,
    dilated_second_moment,
    pointwise_first,
    pointwise_second,
    codebook_first,
    codebook_second,
):
    ranks, times = lax.axis_size("clip"), lax.axis_size("tm")
    rank, time = lax.axis_index("clip"), lax.axis_index("tm")
    clips, frames, _ = features.shape
    half = ranks // 2
    out_rows = HID // ranks
    block = CODES // ranks
    small = 2 * out_rows
    rows = clips * (frames + 2 * PAD)
    smem = pl.BlockSpec(memory_space=pltpu.SMEM)
    hbm = pl.BlockSpec(memory_space=pltpu.HBM)
    shape = jax.ShapeDtypeStruct

    def held(*values):
        return [pltpu.with_memory_space_constraint(v, pltpu.HBM) for v in values]

    assemble = out_rows % 16 == 0
    dil_state = [
        v.transpose(0, 2, 1)
        for v in (dilated_kernel_weight, dilated_first_moment, dilated_second_moment)
    ]
    pw_state = [v.T for v in (pointwise_conv, pointwise_first, pointwise_second)]
    table_state = [codebooks, codebook_first, codebook_second]

    if assemble:
        mine_d, mine_c = pl.pallas_call(
            prep_kernel,
            out_shape=(shape((2, small, DG), BF16), shape((block, DG), BF16)),
            in_specs=[hbm] * 3,
            out_specs=tuple(whole(2)),
            scratch_shapes=[
                pltpu.VMEM((2, out_rows, D), F32),
                pltpu.VMEM((small, DG), F32),
                pltpu.VMEM((block, DG), F32),
                pltpu.SemaphoreType.DMA((4,)),
            ],
            compiler_params=params(),
            name="prep",
        )(*held(dil_state[0], pw_state[0], codebooks))
    else:
        taps = dil_state[0].astype(BF16).reshape(KERNEL, out_rows, 2, DG).transpose(0, 2, 1, 3)
        quarters = jnp.concatenate(
            [taps.reshape(KERNEL, small, DG), pw_state[0].astype(BF16)[None]], axis=0
        )
        mine_d = jnp.take(quarters, time % 2 + jnp.array([0, 2]), axis=0)
        mine_c = lax.dynamic_index_in_dim(codebooks, time, 0, keepdims=False).astype(BF16)

    mine_c, mine_d, late_ids = lax.optimization_barrier((mine_c, mine_d, code_ids))
    near, far = pl.pallas_call(
        pack_kernel,
        out_shape=(shape((clips, 2 * PAD, 2 * D), BF16),) * 2,
        in_specs=[hbm] * 3,
        out_specs=tuple(whole(2)),
        scratch_shapes=[
            pltpu.VMEM((2, 2, clips, 2 * PAD, D), BF16),
            pltpu.VMEM(code_ids.shape, jnp.int32),
            pltpu.SemaphoreType.DMA((5,)),
        ],
        compiler_params=params(),
        name="pack",
    )(*held(features, cotangent, late_ids))
    line_c = [swap(mine_c, 2 * z, 0) for z in range(1, half)]
    across = swap(mine_d, 1, 0)
    near = lax.ppermute(near, "tm", [(i, i ^ 1) for i in range(times)])
    pairs = [(i, i + 1) for i in range(1, times - 1, 2)]
    far = lax.ppermute(far, "tm", pairs + [(b, a) for a, b in pairs])
    near, far, *line_c = lax.optimization_barrier((near, far, *line_c))
    line_c = jnp.stack([mine_c] + line_c, axis=0)
    pair_d = jnp.stack([mine_d, across], axis=0)
    line_c, late_ids = lax.optimization_barrier((line_c, code_ids))
    hot, hott = pl.pallas_call(
        functools.partial(own_kernel, ranks),
        out_shape=(
            shape((SLOTS, rows, CODES), BF16),
            shape((SLOTS, CODES, clips * frames), BF16),
        ),
        in_specs=[smem] + whole(1),
        out_specs=tuple(whole(2)),
        compiler_params=params(8),
        name="own",
    )(clip_lengths, late_ids)
    plane_c = [line_c, swap(line_c, 1, 0), swap(line_c, 0, 2), swap(line_c, 1, 2)]
    line_d = [pair_d] + [swap(pair_d, 2 * z, 0) for z in range(1, half)]

    start, act, windows, cot, mask, hot = pl.pallas_call(
        functools.partial(margin_kernel, ranks),
        out_shape=(
            shape((rows, D), F32),
            shape((rows, D), BF16),
            shape((clips * frames, KERNEL * D), BF16),
            shape((2 * PAD * clips, D), F32),
            shape((rows, DG), F32),
            shape(hot.shape, BF16),
        ),
        in_specs=[smem] + whole(4),
        out_specs=tuple(whole(6)),
        input_output_aliases={4: 5},
        compiler_params=params(8),
        name="margin",
    )(clip_lengths, features, near, far, hot)

    act, *line_d = lax.optimization_barrier((act, *line_d))
    pieces_d = line_d + [swap(v, 0, 1) for v in line_d]
    held = list(plane_c)
    held[3], pieces_d[4] = lax.optimization_barrier((held[3], pieces_d[4]))
    turned = [swap(v, 0, 1) for v in held]
    pieces_c = plane_c[:2] + turned[:2] + plane_c[2:] + turned[2:]

    weights = (shape((KERNEL * HID, D), BF16), shape((D, HID), BF16))
    given = pieces_d
    if not assemble:
        order = rank ^ jnp.arange(ranks)
        stacked = jnp.stack(pieces_d, axis=0).reshape(2, half, 2, 2, small, DG)
        stacked = jnp.take(stacked, time % 2 ^ jnp.arange(2), axis=0)
        stacked = stacked.transpose(3, 0, 1, 2, 4, 5).reshape(4, ranks, small, DG)
        stacked = jnp.take(stacked, order, axis=1)
        dil = stacked[:KERNEL].reshape(KERNEL, ranks, 2, out_rows, DG)
        dil = dil.transpose(0, 1, 3, 2, 4).reshape(KERNEL * HID, D)
        given = [dil, stacked[3].reshape(D, HID)]
    outs = pl.pallas_call(
        functools.partial(conv_kernel, ranks, assemble, clips),
        out_shape=(weights if assemble else ())
        + (shape((rows, HID), BF16), shape((rows, HID), F32), shape((rows, D), F32)),
        in_specs=whole(2 + len(given)),
        out_specs=tuple(whole(5 if assemble else 3)),
        scratch_shapes=[pltpu.VMEM((4, HID, D), BF16)] if assemble else [],
        compiler_params=params(10),
        name="conv",
    )(start, act, *given)
    dil, pwt, gated, hs, latent = tuple(outs) if assemble else tuple(given) + tuple(outs)

    quant, send, bg, lg, cgs = pl.pallas_call(
        functools.partial(quant_kernel, ranks),
        out_shape=(
            shape((clips, frames, D), BF16),
            shape((2, CODES + SCALE_GROUPS * ranks, DG), jnp.int16),
            shape((rows, D), BF16),
            shape((clips * frames, D), F32),
            shape((SLOTS, clips * frames, 2 * DG), BF16),
        ),
        in_specs=whole(6 + len(pieces_c)),
        out_specs=tuple(whole(5)),
        scratch_shapes=[
            pltpu.VMEM((SLOTS, CODES, DG), BF16),
        ],
        compiler_params=params(16),
        name="quant",
    )(mask, latent, cotangent, cot, hot, hott, *pieces_c)

    keep = pl.pallas_call(
        keep_kernel,
        out_shape=shape((2, CODES, DG), F32),
        in_specs=whole(2),
        out_specs=whole(1)[0],
        compiler_params=params(8),
        name="keep",
    )(hott, cgs)

    if assemble:
        grads = (shape((2, ranks * small, DG), F32),) * 2
    else:
        grads = (shape((KERNEL, HID, D), F32), shape((D, HID), F32))
    hg, first_grad, second_grad = pl.pallas_call(
        functools.partial(backward_kernel, ranks, assemble, clips),
        out_shape=(shape((rows, HID), BF16),) + grads,
        in_specs=whole(5),
        out_specs=tuple(whole(3)),
        scratch_shapes=[pltpu.VMEM((4, HID, D), F32)] if assemble else [],
        compiler_params=params(16),
        name="backward",
    )(windows, gated, bg, hs, pwt)
    fg = pl.pallas_call(
        functools.partial(features_kernel, clips),
        out_shape=shape((clips, frames, D), F32),
        in_specs=[smem] + whole(4),
        out_specs=whole(1)[0],
        compiler_params=params(12),
        name="features",
    )(clip_lengths, start, lg, hg, dil)

    if assemble:
        keep_d, send_d = first_grad, second_grad
    else:
        parts = jnp.concatenate(
            [
                first_grad.reshape(KERNEL, ranks, out_rows, 2, DG)
                .transpose(0, 1, 3, 2, 4)
                .reshape(KERNEL, ranks, small, DG),
                second_grad.reshape(1, ranks, small, DG),
            ],
            axis=0,
        )
        seq = jnp.concatenate([jnp.arange(0, ranks, 2), jnp.arange(1, ranks, 2)])
        parts = jnp.take(jnp.take(parts, time ^ jnp.arange(4), axis=0), rank ^ seq, axis=1)
        parts = parts.reshape(2, 2, ranks * small, DG)
        keep_d, send_d = parts[:, 0], parts[:, 1]

    def sent(keep, got, groups, size, tag):
        count = len(groups[0])
        packed = count * size + count * SCALE_GROUPS
        return pl.pallas_call(
            functools.partial(send_kernel, groups, size),
            out_shape=(shape((count, size, DG), F32),)
            + (shape((packed, DG), jnp.int16),) * (len(groups) - 1),
            in_specs=whole(2),
            out_specs=tuple(whole(len(groups))),
            compiler_params=params(),
            name="send_" + tag,
        )(keep, got)

    def passed(parts, size, tag):
        count = parts[0].shape[0]
        return pl.pallas_call(
            functools.partial(pass_kernel, size),
            out_shape=(shape((size, DG), F32),)
            + (shape((size + 8, DG), jnp.int16),) * (count - 1),
            in_specs=whole(len(parts)),
            out_specs=tuple(whole(count)),
            compiler_params=params(),
            name="pass_" + tag,
        )(*parts)

    def over_plane(parts):
        return [parts[0], swap(parts[1], 1, 0), swap(parts[2], 0, 2), swap(parts[3], 1, 2)]

    def over_line(parts):
        return [parts[0]] + [swap(parts[z], 2 * z, 0) for z in range(1, half)]

    by_plane = [[(jy, x * half + z) for z in range(half)] for jy in range(2) for x in range(2)]
    order = (0, 2, 1, 3) if half == 4 else tuple(range(half))
    by_line = [[(jy, x * half + z) for jy in range(2) for x in range(2)] for z in order]
    got_c, got_d = swap(send, 0, 1), swap(send_d, 0, 1)
    parts_c = over_plane(sent(keep, got_c, by_plane, block, "codes"))
    parts_c[0], keep_d = lax.optimization_barrier((parts_c[0], keep_d))
    parts_d = sent(keep_d, got_d, by_line, small, "conv")
    parts_d = [parts_d[0]] + [swap(parts_d[i], 2 * order[i], 0) for i in range(1, half)]
    fg, parts_c[0] = lax.optimization_barrier((fg, parts_c[0]))
    parts_c = over_line(passed(parts_c, block, "codes"))
    parts_c[1], parts_d[0] = lax.optimization_barrier((parts_c[1], parts_d[0]))
    parts_d = passed(parts_d, small, "conv")
    parts_d = [parts_d[0], swap(parts_d[3], 1, 2), swap(parts_d[2], 0, 2), swap(parts_d[1], 1, 0)]
    total = small + block
    piece, squares = pl.pallas_call(
        functools.partial(final_kernel, (small, block), (4, half)),
        out_shape=(shape((total, DG), F32), shape((ranks * times, 8, 128), F32)),
        in_specs=whole(4 + half),
        out_specs=tuple(whole(2)),
        compiler_params=params(),
        name="final",
    )(*parts_d, *parts_c)

    across = swap(piece, 0, 2)
    squares = lax.all_to_all(squares, ("clip", "tm"), 0, 0, tiled=True)
    fours = [piece, swap(piece, 0, 1), across, swap(across, 0, 1)]
    steps = step_count[0].astype(F32)
    decays = jnp.stack([1.0 / (1.0 - FIRST_DECAY**steps), 1.0 / (1.0 - SECOND_DECAY**steps)])
    if assemble:
        state = dil_state + pw_state + table_state
        norm, *new = pl.pallas_call(
            update_kernel,
            out_shape=(shape((1, 1), F32),) + tuple(shape(v.shape, F32) for v in state),
            in_specs=[smem] + whole(14),
            out_specs=tuple(whole(1) + [hbm] * 9),
            scratch_shapes=[pltpu.VMEM(v.shape, F32) for v in state]
            + [pltpu.SemaphoreType.DMA((18,))],
            compiler_params=params(8),
            name="update",
        )(decays, squares, *fours, *state)
        norm = norm.reshape(1)
        dil_new, pw_new, table_new = new[:3], new[3:6], new[6:]
    else:
        four = jnp.take(jnp.stack(fours, axis=0), time ^ jnp.arange(4), axis=0)
        raw = four[:KERNEL, :small].reshape(KERNEL, 2, out_rows, DG)
        raw = raw.transpose(0, 2, 1, 3).reshape(KERNEL, out_rows, D)
        count = KERNEL * D * HID + D * HID + SLOTS * CODES * DG
        limit = jnp.sqrt(jnp.float32(count))
        norm = jnp.sqrt(jnp.sum(squares, axis=0)[0, :1])
        scale = limit / jnp.maximum(norm[0], limit)
        new = []
        for state, grad, rate in (
            (dil_state, raw, BITRATE_FACTOR),
            (pw_state, four[3, :small], BITRATE_FACTOR),
            (table_state, four[:, small:], RATE_CODE),
        ):
            grad = grad * scale
            weight, second = stepped(*state, grad, rate, decays[0], decays[1])
            new.append((weight, grad, second))
        dil_new, pw_new, table_new = new
    return (
        quant,
        fg,
        norm,
        *[v.transpose(0, 2, 1) for v in dil_new],
        *[v.T for v in pw_new],
        *table_new,
    )


def solution(mesh):
    in_specs = (
        P("clip", "tm", None),
        P("clip", "tm", None),
        P("clip"),
        P(None, "clip", "tm"),
        P(),
        P(None, None, "clip"),
        P(None, "clip"),
        P(None, "clip", None),
        P(None, None, "clip"),
        P(None, None, "clip"),
        P(None, "clip"),
        P(None, "clip"),
        P(None, "clip", None),
        P(None, "clip", None),
    )
    out_specs = (
        P("clip", "tm", None),
        P("clip", "tm", None),
        P(),
        P(None, None, "clip"),
        P(None, None, "clip"),
        P(None, None, "clip"),
        P(None, "clip"),
        P(None, "clip"),
        P(None, "clip"),
        P(None, "clip", None),
        P(None, "clip", None),
        P(None, "clip", None),
    )
    return jax.shard_map(shards, mesh=mesh, in_specs=in_specs, out_specs=out_specs, check_vma=False)
```

```python
import functools

import jax
import jax.numpy as jnp
from jax import lax
from jax.experimental import pallas as pl
from jax.experimental.pallas import tpu as pltpu
from jax.sharding import PartitionSpec as P

D = 512
HID = 256
CODES = 1024
GROUPS = 2
LEVELS = 2
SLOTS = 4
KERNEL = 3
DILATION = 3
DG = 256
PAD = 8

COMMIT = 0.25
FIRST_DECAY = 0.9
SECOND_DECAY = 0.99
EPSILON = 1e-08
WEIGHT_DECAY = 0.01
BITRATE_FACTOR = 0.02
RATE_CODE = 0.5

F32 = jnp.float32
BF16 = jnp.bfloat16
NT = (((1,), (1,)), ((), ()))
TN = (((0,), (0,)), ((), ()))
LEVEL_STEPS = 256.0
TOP = 32000.0
SCALE_GROUPS = 4
MIB = 1024 * 1024


def params(mib=6):
    return pltpu.CompilerParams(vmem_limit_bytes=mib * MIB)


def whole(count):
    return [pl.BlockSpec(memory_space=pltpu.VMEM)] * count


def mm(a, b):
    return jnp.dot(a, b, preferred_element_type=F32)


def mmg(a, b, dims):
    return lax.dot_general(a, b, dims, preferred_element_type=F32)


def slope(v):
    return jnp.where(v > 0, 1.0, jnp.exp(jnp.minimum(v, 0.0)))


def elu(v):
    return jnp.where(v > 0, v, jnp.exp(jnp.minimum(v, 0.0)) - 1.0)


def swap(value, clip_mask, time_mask):
    clips, times = lax.axis_size("clip"), lax.axis_size("tm")
    pairs = [
        (c * times + t, (c ^ clip_mask) * times + (t ^ time_mask))
        for c in range(clips)
        for t in range(times)
    ]
    return lax.ppermute(value, ("clip", "tm"), pairs)


def prep_kernel(dil_hbm, pw_hbm, table_hbm, conv_ref, code_ref, dil_ref, pw_ref, table_ref, sems):
    time = lax.axis_index("tm")
    bit = time % 2
    out_rows = pw_ref.shape[0] // 2
    second = jnp.minimum(2 + bit, KERNEL - 1)
    copies = [
        pltpu.make_async_copy(table_hbm.at[time], table_ref, sems.at[0]),
        pltpu.make_async_copy(dil_hbm.at[bit], dil_ref.at[0], sems.at[1]),
        pltpu.make_async_copy(dil_hbm.at[second], dil_ref.at[1], sems.at[2]),
        pltpu.make_async_copy(pw_hbm, pw_ref, sems.at[3]),
    ]
    for copy in copies:
        copy.start()
    copies[0].wait()
    code_ref[...] = table_ref[...].astype(BF16)
    for copy in copies[1:]:
        copy.wait()
    for side in range(2):
        for part in range(2):
            conv_ref[part, side * out_rows : (side + 1) * out_rows, :] = dil_ref[
                part, :, side * DG : (side + 1) * DG
            ].astype(BF16)

    @pl.when(bit == 1)
    def _():
        conv_ref[1] = pw_ref[...].astype(BF16)


def renamed(values, ranks):
    block = CODES // ranks
    step = (values // block) ^ lax.axis_index("clip")
    place = (step % 2) * (ranks // 2) + step // 2
    return place * block + values % block


def masks(clips, frames, len_ref, columns):
    base = lax.axis_index("tm") * frames

    def mark(first, count, clip):
        where = lax.broadcasted_iota(jnp.int32, (count, columns), 0) + first
        return jnp.where((where >= 0) & (where < len_ref[clip]), 1.0, 0.0)

    own = [mark(base, frames, c) for c in range(clips)]
    margins = [
        mark(first, PAD, c) for c in range(clips) for first in (base - PAD, base + frames)
    ]
    return jnp.concatenate(own + margins, axis=0)


def widened(value, clip, clips, frames):
    at = clips * frames + 2 * PAD * clip
    return jnp.concatenate(
        [
            value[at : at + PAD],
            value[clip * frames : (clip + 1) * frames],
            value[at + PAD : at + 2 * PAD],
        ],
        axis=0,
    )


def pack_kernel(f_hbm, c_hbm, ids_hbm, near_ref, far_ref, buf, ids_ref, sems):
    clips, frames, _ = f_hbm.shape
    edge = 2 * PAD
    odd = lax.axis_index("tm") % 2
    copies = [pltpu.make_async_copy(ids_hbm, ids_ref, sems.at[4])]
    for kind, source in enumerate((f_hbm, c_hbm)):
        for side, at in enumerate((frames - edge, 0)):
            copies.append(
                pltpu.make_async_copy(
                    source.at[:, pl.ds(at, edge), :], buf.at[kind, side], sems.at[2 * kind + side]
                )
            )
    for copy in copies:
        copy.start()
    for copy in copies:
        copy.wait()
    outs = []
    for side in range(2):
        at = slice(PAD, 2 * PAD) if side == 0 else slice(0, PAD)
        parts = []
        for c in range(clips):
            ids = ids_ref[:, c, :]
            if side == 0:
                ids = pltpu.roll(ids, PAD, 1)
            both = jnp.concatenate([ids // 32, ids % 32], axis=0).astype(F32)
            both = jnp.concatenate([both, jnp.zeros((8, 2 * D - frames), F32)], axis=1)
            ends = [buf[kind, side, c].astype(F32)[at] for kind in range(2)]
            parts.append(jnp.concatenate([jnp.concatenate(ends, axis=1), both], axis=0))
        outs.append(parts)
    for c in range(clips):
        last, first = outs[0][c], outs[1][c]
        near_ref[c] = jnp.where(odd == 1, first, last).astype(BF16)
        far_ref[c] = jnp.where(odd == 1, last, first).astype(BF16)


def own_kernel(ranks, len_ref, ids_ref, hot_ref, hott_ref):
    _, clips, frames = ids_ref.shape
    codes = lax.broadcasted_iota(jnp.int32, (frames, CODES), 1)
    spots = lax.broadcasted_iota(jnp.int32, (CODES, frames), 0)
    where = lax.broadcasted_iota(jnp.int32, (1, frames), 1) + lax.axis_index("tm") * frames
    for c in range(clips):
        weight = jnp.where(where < len_ref[c], -2.0, 0.0)
        ids = renamed(ids_ref[:, c, :], ranks)
        turned = jnp.concatenate([ids.astype(F32), jnp.zeros((8 - SLOTS, frames), F32)], axis=0)
        turned = turned.T.astype(jnp.int32)
        at = slice(c * frames, (c + 1) * frames)
        for slot in range(SLOTS):
            hot_ref[slot, at, :] = jnp.where(codes == turned[:, slot : slot + 1], 1.0, 0.0).astype(
                BF16
            )
            hott_ref[slot, :, at] = jnp.where(spots == ids[slot : slot + 1], weight, 0.0).astype(BF16)
    hot_ref[:, clips * frames :, :] = jnp.zeros((SLOTS, 2 * PAD * clips, CODES), BF16)


def moved(value, shift, clips, frames):
    span = frames + 2 * PAD
    return jnp.concatenate(
        [
            pltpu.roll(widened(value, c, clips, frames), shift % span, 0)[PAD : PAD + frames]
            for c in range(clips)
        ],
        axis=0,
    ).astype(BF16)


def margin_kernel(
    ranks,
    len_ref,
    f_ref,
    near_ref,
    far_ref,
    old_ref,
    start_ref,
    act_ref,
    window_ref,
    cot_ref,
    mask_ref,
    hot_ref,
):
    del old_ref
    clips, frames, _ = f_ref.shape
    odd = lax.axis_index("tm") % 2
    both = []
    for c in range(clips):
        near, far = near_ref[c].astype(F32), far_ref[c].astype(F32)
        both += [jnp.where(odd == 1, near, far), jnp.where(odd == 1, far, near)]
    mask = masks(clips, frames, len_ref, D)
    mask_ref[...] = mask[:, :DG]
    start = mask * jnp.concatenate(
        [f_ref[c].astype(F32) for c in range(clips)] + [part[:PAD, :D] for part in both], axis=0
    )
    start_ref[...] = start
    act = elu(start).astype(BF16)
    act_ref[...] = act
    wide = act.astype(F32)
    for tap in range(KERNEL):
        shift = (1 - tap) * DILATION
        window_ref[:, tap * D : (tap + 1) * D] = (
            moved(wide, shift, clips, frames) if shift else act[: clips * frames]
        )
    cot_ref[...] = jnp.concatenate([part[:PAD, D:] for part in both], axis=0)
    turned = jnp.concatenate([part[PAD:, :128].T[:PAD] for part in both], axis=0)
    ids = renamed((turned[:, :SLOTS] * 32.0 + turned[:, SLOTS : 2 * SLOTS]).astype(jnp.int32), ranks)
    codes = lax.broadcasted_iota(jnp.int32, (2 * PAD * clips, CODES), 1)
    for slot in range(SLOTS):
        hot_ref[slot, clips * frames :, :] = jnp.where(
            codes == ids[:, slot : slot + 1], 1.0, 0.0
        ).astype(BF16)


def assembled(ranks, pieces, d_ref, pwt_ref, all_ref):
    half, small = ranks // 2, 2 * HID // ranks
    out_rows = small // 2
    bit, rank = lax.axis_index("tm") % 2, lax.axis_index("clip")
    for other in range(2):
        for z in range(half):
            piece = pieces[other * half + z]
            for x in range(2):
                at = pl.multiple_of((rank ^ (2 * z + x)) * out_rows, out_rows)
                for part in range(2):
                    for side in range(2):
                        all_ref[
                            2 * part + (bit ^ other),
                            pl.ds(at, out_rows),
                            side * DG : (side + 1) * DG,
                        ] = piece[x, part, side * out_rows : (side + 1) * out_rows, :]
    for tap in range(KERNEL):
        d_ref[tap * HID : (tap + 1) * HID, :] = all_ref[tap]
    for r in range(ranks):
        for side in range(2):
            to = r * small + side * out_rows
            pwt_ref[to : to + out_rows, :] = all_ref[
                KERNEL, r * out_rows : (r + 1) * out_rows, side * DG : (side + 1) * DG
            ]


def conv_kernel(ranks, assemble, clips, start_ref, act_ref, *refs):
    if assemble:
        pieces, refs = refs[:ranks], refs[ranks:]
        d_ref, pwt_ref, gated_ref, hs_ref, latent_ref, all_ref = refs
        assembled(ranks, pieces, d_ref, pwt_ref, all_ref)
    else:
        d_ref, pwt_ref, gated_ref, hs_ref, latent_ref = refs
    rows = start_ref.shape[0]
    taps = mmg(act_ref[...], d_ref[...], NT)
    frames = rows // clips - 2 * PAD
    span = frames + 2 * PAD
    own, margins = [], []
    for c in range(clips):
        wide = widened(taps, c, clips, frames)
        part = (
            pltpu.roll(wide[:, :HID], DILATION, 0)
            + wide[:, HID : 2 * HID]
            + pltpu.roll(wide[:, 2 * HID :], span - DILATION, 0)
        )
        own.append(part[PAD : PAD + frames])
        margins += [part[:PAD], part[PAD + frames :]]
    hidden = jnp.concatenate(own + margins, axis=0)
    hs_ref[...] = slope(hidden)
    gated = elu(hidden).astype(BF16)
    gated_ref[...] = gated
    latent_ref[...] = start_ref[...] + mmg(gated, pwt_ref[...], NT)


def quant_kernel(ranks, mask_ref, latent_ref, c_ref, cot_ref, hot_ref, hott_ref, *refs):
    half, block = ranks // 2, CODES // ranks
    pieces, refs = refs[:8], refs[8:]
    quant_ref, send_ref, bg_ref, lg_ref, cgs_ref, tab_ref = refs
    clips, frames, _ = c_ref.shape
    time = lax.axis_index("tm")
    mask = mask_ref[...]
    local = clips * frames
    for other in range(SLOTS):
        slot = time ^ other
        for x in range(2):
            for z in range(half):
                spot = (x * half + z) * block
                tab_ref[slot, spot : spot + block, :] = pieces[2 * other + x][z]
    for group in range(GROUPS):
        at = slice(group * DG, (group + 1) * DG)
        first = mm(hot_ref[2 * group], tab_ref[2 * group])
        second = mm(hot_ref[2 * group + 1], tab_ref[2 * group + 1])
        cot = jnp.concatenate(
            [c_ref[c, :, at].astype(F32) for c in range(clips)] + [cot_ref[:, at]], axis=0
        )
        residual = latent_ref[:, at]
        gap = residual - first
        gap2 = gap - second
        both = gap + gap2
        grad = mask * (cot + (both if COMMIT == 0.5 else 2.0 * COMMIT * both))
        quant = (mask * (first + second))[:local].astype(BF16)
        bg_ref[:, at] = grad.astype(BF16)
        lg_ref[:, at] = grad[:local]
        for clip in range(clips):
            quant_ref[clip, :, at] = quant[clip * frames : (clip + 1) * frames]
        for level, diff in ((0, gap), (1, gap2)):
            diff = diff[:local]
            high = diff.astype(BF16)
            cgs_ref[2 * group + level, :, :DG] = high
            cgs_ref[2 * group + level, :, DG:] = (diff - high.astype(F32)).astype(BF16)
    size = block // SCALE_GROUPS
    for far in range(2):
        total = summed(2 * far + 1, hott_ref, cgs_ref)
        levels = []
        for place in range(ranks):
            steps, more = pack_part(total[place * block : (place + 1) * block])
            for group, step in enumerate(steps):
                at = place * block + group * size
                send_ref[far, at : at + size, :] = step.astype(jnp.int16)
            levels += more
        levels = jnp.concatenate(levels, axis=0).astype(jnp.int32)
        send_ref[far, CODES:, :] = levels.astype(jnp.int16)


def summed(other, hott_ref, cgs_ref):
    slot = lax.axis_index("tm") ^ other
    pair = mm(hott_ref[slot], cgs_ref[slot])
    return pair[:, :DG] + pair[:, DG:]


def keep_kernel(hott_ref, cgs_ref, keep_ref):
    for far in range(2):
        keep_ref[far] = summed(2 * far, hott_ref, cgs_ref)


def backward_kernel(
    ranks,
    assemble,
    clips,
    window_ref,
    gated_ref,
    bg_ref,
    hs_ref,
    pwt_ref,
    hg_ref,
    *outs,
):
    local = window_ref.shape[0]
    bg = bg_ref[...]
    hidden_grad = (mm(bg, pwt_ref[...]) * hs_ref[...]).astype(BF16)
    hg_ref[...] = hidden_grad
    dil_all = mmg(hidden_grad[:local], window_ref[...], TN)
    dil_grads = [dil_all[:, tap * D : (tap + 1) * D] for tap in range(KERNEL)]
    pw_grad = mmg(bg[:local], gated_ref[:local, :], TN)
    if assemble:
        keep_ref, send_ref, all_ref = outs
        half, small = ranks // 2, 2 * HID // ranks
        out_rows = small // 2
        time, rank = lax.axis_index("tm"), lax.axis_index("clip")
        for tap in range(KERNEL):
            all_ref[tap] = dil_grads[tap]
        for r in range(ranks):
            for side in range(2):
                at = r * small + side * out_rows
                all_ref[KERNEL, r * out_rows : (r + 1) * out_rows, side * DG : (side + 1) * DG] = (
                    pw_grad[at : at + out_rows]
                )
        for other in range(4):
            out = (keep_ref, send_ref)[other % 2]
            for x in range(2):
                for z in range(half):
                    at = pl.multiple_of((rank ^ (2 * z + x)) * out_rows, out_rows)
                    to = (x * half + z) * small
                    for side in range(2):
                        out[other // 2, to + side * out_rows : to + (side + 1) * out_rows, :] = (
                            all_ref[
                                time ^ other, pl.ds(at, out_rows), side * DG : (side + 1) * DG
                            ]
                        )
    else:
        dil_ref, pw_ref = outs
        for tap in range(KERNEL):
            dil_ref[tap] = dil_grads[tap]
        pw_ref[...] = pw_grad


def features_kernel(clips, len_ref, start_ref, lg_ref, hg_ref, d_ref, fg_ref):
    frames = start_ref.shape[0] // clips - 2 * PAD
    local = clips * frames
    wide = hg_ref[...].astype(F32)
    shifted = jnp.concatenate(
        [
            moved(wide, -DILATION, clips, frames),
            hg_ref[:local, :],
            moved(wide, DILATION, clips, frames),
        ],
        axis=1,
    )
    act_grad = mm(shifted, d_ref[...])
    row = lax.broadcasted_iota(jnp.int32, (frames, D), 0) + lax.axis_index("tm") * frames
    for c in range(clips):
        to = slice(c * frames, (c + 1) * frames)
        mask = jnp.where(row < len_ref[c], 1.0, 0.0)
        fg_ref[c] = mask * (lg_ref[to, :] + slope(start_ref[to, :]) * act_grad[to])


def pack_part(value):
    count = SCALE_GROUPS
    rows = value.shape[0]
    size = rows // count
    steps, levels = [], []
    for group in range(count):
        part = value[group * size : (group + 1) * size]
        top = jnp.maximum(jnp.max(jnp.abs(part), axis=0, keepdims=True), 1e-30)
        level = jnp.ceil(jnp.log2(top) * LEVEL_STEPS)
        scale = jnp.exp2(level / -LEVEL_STEPS) * TOP
        steps.append(jnp.round(part * scale).astype(jnp.int32))
        levels.append(level)
    return steps, levels


def unpack_part(steps, level):
    return steps.astype(jnp.int32).astype(F32) * (
        jnp.exp2(level.astype(jnp.int32).astype(F32) / LEVEL_STEPS) / TOP
    )


def send_kernel(groups, rows, keep_ref, got_ref, own_ref, *outs):
    size = rows // SCALE_GROUPS
    for part, blocks in enumerate(groups):
        levels = []
        for place, (jy, start) in enumerate(blocks):
            at = slice(start * rows, (start + 1) * rows)
            if got_ref.dtype == F32:
                other = got_ref[jy, at, :]
            else:
                top = (got_ref.shape[1] // (rows + SCALE_GROUPS)) * rows + start * SCALE_GROUPS
                other = jnp.concatenate(
                    [
                        unpack_part(
                            got_ref[jy, start * rows + g * size : start * rows + (g + 1) * size, :],
                            got_ref[jy, top : top + SCALE_GROUPS, :][g : g + 1],
                        )
                        for g in range(SCALE_GROUPS)
                    ],
                    axis=0,
                )
            value = keep_ref[jy, at, :] + other
            if part == 0:
                own_ref[place] = value
                continue
            steps, more = pack_part(value)
            for group, step in enumerate(steps):
                spot = place * rows + group * size
                outs[part - 1][spot : spot + size, :] = step.astype(jnp.int16)
            levels += more
        if part:
            tail = jnp.concatenate(levels, axis=0).astype(jnp.int32)
            outs[part - 1][len(blocks) * rows :, :] = tail.astype(jnp.int16)


def pass_kernel(rows, own_in, *refs):
    blocks = own_in.shape[0]
    gots, own_ref, outs = refs[:-blocks], refs[-blocks], refs[1 - blocks :]
    size = rows // SCALE_GROUPS
    for place in range(blocks):
        value = own_in[place]
        pieces = [value[g * size : (g + 1) * size] for g in range(SCALE_GROUPS)]
        for got in gots:
            tail = got[blocks * rows :, :]
            for g in range(SCALE_GROUPS):
                index = place * SCALE_GROUPS + g
                spot = place * rows + g * size
                pieces[g] = pieces[g] + unpack_part(
                    got[spot : spot + size, :], tail[index : index + 1]
                )
        if place == 0:
            for g in range(SCALE_GROUPS):
                own_ref[g * size : (g + 1) * size, :] = pieces[g]
            continue
        steps, levels = pack_part(jnp.concatenate(pieces, axis=0))
        out = outs[place - 1]
        for g, step in enumerate(steps):
            out[g * size : (g + 1) * size, :] = step.astype(jnp.int16)
        pad = jnp.zeros((out.shape[0] - rows - len(levels), DG), F32)
        tail = jnp.concatenate(levels + [pad], axis=0).astype(jnp.int32)
        out[rows:, :] = tail.astype(jnp.int16)


def final_kernel(sizes, counts, *refs):
    out_ref, square_ref = refs[-2:]
    squares = jnp.zeros((1, DG), F32)
    place = 0
    for kind, rows in enumerate(sizes):
        own_ref, *gots = refs[sum(counts[:kind]) : sum(counts[: kind + 1])]
        size = rows // SCALE_GROUPS
        for g in range(SCALE_GROUPS):
            at = slice(g * size, (g + 1) * size)
            value = own_ref[at, :]
            for got in gots:
                value = value + unpack_part(got[at, :], got[rows:, :][g : g + 1])
            out_ref[place : place + size, :] = value
            squares = squares + jnp.sum(value * value, axis=0, keepdims=True)
            place += size
    square = jnp.sum(squares, axis=1, keepdims=True)
    square_ref[...] = jnp.broadcast_to(square[None], square_ref.shape)


def stepped(weight, first, second, grad, rate, fix1, fix2):
    first_new = FIRST_DECAY * first + (1.0 - FIRST_DECAY) * grad
    second_new = SECOND_DECAY * second + (1.0 - SECOND_DECAY) * grad * grad
    change = (first_new * fix1) / (jnp.sqrt(second_new * fix2) + EPSILON) + WEIGHT_DECAY * weight
    return weight - rate * change, second_new


def update_kernel(fix_ref, square_ref, *refs):
    pieces = refs[:4]
    dil, pw, table = refs[4:7], refs[7:10], refs[10:13]
    norm_ref = refs[13]
    dil_hbm, pw_hbm, table_hbm = refs[14:17], refs[17:20], refs[20:23]
    dil_out, pw_out, table_out = refs[23:26], refs[26:29], refs[29:32]
    sems = refs[32]
    out_rows = dil[0].shape[1]
    small = 2 * out_rows
    time = lax.axis_index("tm")
    count = KERNEL * D * HID + D * HID + SLOTS * CODES * DG
    norm = jnp.sqrt(jnp.sum(square_ref[...], axis=0)[:1, :1])
    limit = jnp.sqrt(jnp.full((1, 1), float(count), F32))
    scale = limit / jnp.maximum(norm, limit)
    norm_ref[...] = norm
    fixes = (fix_ref[0], fix_ref[1])
    copies = []
    for other in range(4):
        quarter = time ^ other
        piece = pieces[other]
        grad = piece[small:, :] * scale
        state = [v[quarter] for v in table]
        weight, second = stepped(*state, grad, RATE_CODE, *fixes)
        for kind, value in enumerate((weight, grad, second)):
            table_out[kind][quarter] = value
            copies.append(
                pltpu.make_async_copy(
                    table_out[kind].at[quarter], table_hbm[kind].at[quarter], sems.at[len(copies)]
                )
            )
            copies[-1].start()

        @pl.when(quarter < KERNEL)
        def _():
            tap = jnp.minimum(quarter, KERNEL - 1)
            for side in range(2):
                to = slice(side * DG, (side + 1) * DG)
                grad = piece[side * out_rows : (side + 1) * out_rows, :] * scale
                state = [v[tap, :, to] for v in dil]
                weight, second = stepped(*state, grad, BITRATE_FACTOR, *fixes)
                dil_out[0][tap, :, to] = weight
                dil_out[1][tap, :, to] = grad
                dil_out[2][tap, :, to] = second

        @pl.when(quarter == KERNEL)
        def _():
            grad = piece[:small, :] * scale
            weight, second = stepped(*[v[...] for v in pw], grad, BITRATE_FACTOR, *fixes)
            pw_out[0][...] = weight
            pw_out[1][...] = grad
            pw_out[2][...] = second

    for kind in range(3):
        for outs, hbms in ((dil_out, dil_hbm), (pw_out, pw_hbm)):
            copies.append(pltpu.make_async_copy(outs[kind], hbms[kind], sems.at[len(copies)]))
            copies[-1].start()
    for copy in copies:
        copy.wait()


def shards(
    features,
    cotangent,
    clip_lengths,
    code_ids,
    step_count,
    dilated_kernel_weight,
    pointwise_conv,
    codebooks,
    dilated_first_moment,
    dilated_second_moment,
    pointwise_first,
    pointwise_second,
    codebook_first,
    codebook_second,
):
    ranks, times = lax.axis_size("clip"), lax.axis_size("tm")
    rank, time = lax.axis_index("clip"), lax.axis_index("tm")
    clips, frames, _ = features.shape
    half = ranks // 2
    out_rows = HID // ranks
    block = CODES // ranks
    small = 2 * out_rows
    rows = clips * (frames + 2 * PAD)
    smem = pl.BlockSpec(memory_space=pltpu.SMEM)
    hbm = pl.BlockSpec(memory_space=pltpu.HBM)
    shape = jax.ShapeDtypeStruct

    def held(*values):
        return [pltpu.with_memory_space_constraint(v, pltpu.HBM) for v in values]

    assemble = out_rows % 16 == 0
    dil_state = [
        v.transpose(0, 2, 1)
        for v in (dilated_kernel_weight, dilated_first_moment, dilated_second_moment)
    ]
    pw_state = [v.T for v in (pointwise_conv, pointwise_first, pointwise_second)]
    table_state = [codebooks, codebook_first, codebook_second]

    if assemble:
        mine_d, mine_c = pl.pallas_call(
            prep_kernel,
            out_shape=(shape((2, small, DG), BF16), shape((block, DG), BF16)),
            in_specs=[hbm] * 3,
            out_specs=tuple(whole(2)),
            scratch_shapes=[
                pltpu.VMEM((2, out_rows, D), F32),
                pltpu.VMEM((small, DG), F32),
                pltpu.VMEM((block, DG), F32),
                pltpu.SemaphoreType.DMA((4,)),
            ],
            compiler_params=params(),
            name="prep",
        )(*held(dil_state[0], pw_state[0], codebooks))
    else:
        taps = dil_state[0].astype(BF16).reshape(KERNEL, out_rows, 2, DG).transpose(0, 2, 1, 3)
        quarters = jnp.concatenate(
            [taps.reshape(KERNEL, small, DG), pw_state[0].astype(BF16)[None]], axis=0
        )
        mine_d = jnp.take(quarters, time % 2 + jnp.array([0, 2]), axis=0)
        mine_c = lax.dynamic_index_in_dim(codebooks, time, 0, keepdims=False).astype(BF16)

    mine_c, mine_d, late_ids = lax.optimization_barrier((mine_c, mine_d, code_ids))
    near, far = pl.pallas_call(
        pack_kernel,
        out_shape=(shape((clips, 2 * PAD, 2 * D), BF16),) * 2,
        in_specs=[hbm] * 3,
        out_specs=tuple(whole(2)),
        scratch_shapes=[
            pltpu.VMEM((2, 2, clips, 2 * PAD, D), BF16),
            pltpu.VMEM(code_ids.shape, jnp.int32),
            pltpu.SemaphoreType.DMA((5,)),
        ],
        compiler_params=params(),
        name="pack",
    )(*held(features, cotangent, late_ids))
    line_c = [swap(mine_c, 2 * z, 0) for z in range(1, half)]
    across = swap(mine_d, 1, 0)
    near = lax.ppermute(near, "tm", [(i, i ^ 1) for i in range(times)])
    pairs = [(i, i + 1) for i in range(1, times - 1, 2)]
    far = lax.ppermute(far, "tm", pairs + [(b, a) for a, b in pairs])
    near, far, *line_c = lax.optimization_barrier((near, far, *line_c))
    line_c = jnp.stack([mine_c] + line_c, axis=0)
    pair_d = jnp.stack([mine_d, across], axis=0)
    line_c, late_ids = lax.optimization_barrier((line_c, code_ids))
    hot, hott = pl.pallas_call(
        functools.partial(own_kernel, ranks),
        out_shape=(
            shape((SLOTS, rows, CODES), BF16),
            shape((SLOTS, CODES, clips * frames), BF16),
        ),
        in_specs=[smem] + whole(1),
        out_specs=tuple(whole(2)),
        compiler_params=params(8),
        name="own",
    )(clip_lengths, late_ids)
    plane_c = [line_c, swap(line_c, 1, 0), swap(line_c, 0, 2), swap(line_c, 1, 2)]
    line_d = [pair_d] + [swap(pair_d, 2 * z, 0) for z in range(1, half)]

    start, act, windows, cot, mask, hot = pl.pallas_call(
        functools.partial(margin_kernel, ranks),
        out_shape=(
            shape((rows, D), F32),
            shape((rows, D), BF16),
            shape((clips * frames, KERNEL * D), BF16),
            shape((2 * PAD * clips, D), F32),
            shape((rows, DG), F32),
            shape(hot.shape, BF16),
        ),
        in_specs=[smem] + whole(4),
        out_specs=tuple(whole(6)),
        input_output_aliases={4: 5},
        compiler_params=params(8),
        name="margin",
    )(clip_lengths, features, near, far, hot)

    act, *line_d = lax.optimization_barrier((act, *line_d))
    pieces_d = line_d + [swap(pair_d, 0, 1)] + [swap(v, 0, 1) for v in line_d[1:]]
    held = list(plane_c)
    held[3], pieces_d[4] = lax.optimization_barrier((held[3], pieces_d[4]))
    turned = [swap(v, 0, 1) for v in held]
    pieces_c = plane_c[:2] + turned[:2] + plane_c[2:] + turned[2:]

    weights = (shape((KERNEL * HID, D), BF16), shape((D, HID), BF16))
    given = pieces_d
    if not assemble:
        order = rank ^ jnp.arange(ranks)
        stacked = jnp.stack(pieces_d, axis=0).reshape(2, half, 2, 2, small, DG)
        stacked = jnp.take(stacked, time % 2 ^ jnp.arange(2), axis=0)
        stacked = stacked.transpose(3, 0, 1, 2, 4, 5).reshape(4, ranks, small, DG)
        stacked = jnp.take(stacked, order, axis=1)
        dil = stacked[:KERNEL].reshape(KERNEL, ranks, 2, out_rows, DG)
        dil = dil.transpose(0, 1, 3, 2, 4).reshape(KERNEL * HID, D)
        given = [dil, stacked[3].reshape(D, HID)]
    outs = pl.pallas_call(
        functools.partial(conv_kernel, ranks, assemble, clips),
        out_shape=(weights if assemble else ())
        + (shape((rows, HID), BF16), shape((rows, HID), F32), shape((rows, D), F32)),
        in_specs=whole(2 + len(given)),
        out_specs=tuple(whole(5 if assemble else 3)),
        scratch_shapes=[pltpu.VMEM((4, HID, D), BF16)] if assemble else [],
        compiler_params=params(10),
        name="conv",
    )(start, act, *given)
    dil, pwt, gated, hs, latent = tuple(outs) if assemble else tuple(given) + tuple(outs)

    quant, send, bg, lg, cgs = pl.pallas_call(
        functools.partial(quant_kernel, ranks),
        out_shape=(
            shape((clips, frames, D), BF16),
            shape((2, CODES + SCALE_GROUPS * ranks, DG), jnp.int16),
            shape((rows, D), BF16),
            shape((clips * frames, D), F32),
            shape((SLOTS, clips * frames, 2 * DG), BF16),
        ),
        in_specs=whole(6 + len(pieces_c)),
        out_specs=tuple(whole(5)),
        scratch_shapes=[
            pltpu.VMEM((SLOTS, CODES, DG), BF16),
        ],
        compiler_params=params(16),
        name="quant",
    )(mask, latent, cotangent, cot, hot, hott, *pieces_c)

    keep = pl.pallas_call(
        keep_kernel,
        out_shape=shape((2, CODES, DG), F32),
        in_specs=whole(2),
        out_specs=whole(1)[0],
        compiler_params=params(8),
        name="keep",
    )(hott, cgs)

    if assemble:
        grads = (shape((2, ranks * small, DG), F32),) * 2
    else:
        grads = (shape((KERNEL, HID, D), F32), shape((D, HID), F32))
    hg, first_grad, second_grad = pl.pallas_call(
        functools.partial(backward_kernel, ranks, assemble, clips),
        out_shape=(shape((rows, HID), BF16),) + grads,
        in_specs=whole(5),
        out_specs=tuple(whole(3)),
        scratch_shapes=[pltpu.VMEM((4, HID, D), F32)] if assemble else [],
        compiler_params=params(16),
        name="backward",
    )(windows, gated, bg, hs, pwt)
    fg = pl.pallas_call(
        functools.partial(features_kernel, clips),
        out_shape=shape((clips, frames, D), F32),
        in_specs=[smem] + whole(4),
        out_specs=whole(1)[0],
        compiler_params=params(12),
        name="features",
    )(clip_lengths, start, lg, hg, dil)

    if assemble:
        keep_d, send_d = first_grad, second_grad
    else:
        parts = jnp.concatenate(
            [
                first_grad.reshape(KERNEL, ranks, out_rows, 2, DG)
                .transpose(0, 1, 3, 2, 4)
                .reshape(KERNEL, ranks, small, DG),
                second_grad.reshape(1, ranks, small, DG),
            ],
            axis=0,
        )
        seq = jnp.concatenate([jnp.arange(0, ranks, 2), jnp.arange(1, ranks, 2)])
        parts = jnp.take(jnp.take(parts, time ^ jnp.arange(4), axis=0), rank ^ seq, axis=1)
        parts = parts.reshape(2, 2, ranks * small, DG)
        keep_d, send_d = parts[:, 0], parts[:, 1]

    def sent(keep, got, groups, size, tag):
        count = len(groups[0])
        packed = count * size + count * SCALE_GROUPS
        return pl.pallas_call(
            functools.partial(send_kernel, groups, size),
            out_shape=(shape((count, size, DG), F32),)
            + (shape((packed, DG), jnp.int16),) * (len(groups) - 1),
            in_specs=whole(2),
            out_specs=tuple(whole(len(groups))),
            compiler_params=params(),
            name="send_" + tag,
        )(keep, got)

    def passed(parts, size, tag):
        count = parts[0].shape[0]
        return pl.pallas_call(
            functools.partial(pass_kernel, size),
            out_shape=(shape((size, DG), F32),)
            + (shape((size + 8, DG), jnp.int16),) * (count - 1),
            in_specs=whole(len(parts)),
            out_specs=tuple(whole(count)),
            compiler_params=params(),
            name="pass_" + tag,
        )(*parts)

    def over_plane(parts):
        return [parts[0], swap(parts[1], 1, 0), swap(parts[2], 0, 2), swap(parts[3], 1, 2)]

    def over_line(parts):
        return [parts[0]] + [swap(parts[z], 2 * z, 0) for z in range(1, half)]

    by_plane = [[(jy, x * half + z) for z in range(half)] for jy in range(2) for x in range(2)]
    order = (0, 2, 1, 3) if half == 4 else tuple(range(half))
    by_line = [[(jy, x * half + z) for jy in range(2) for x in range(2)] for z in order]
    got_c, got_d = swap(send, 0, 1), swap(send_d, 0, 1)
    parts_c = over_plane(sent(keep, got_c, by_plane, block, "codes"))
    parts_c[0], keep_d = lax.optimization_barrier((parts_c[0], keep_d))
    parts_d = sent(keep_d, got_d, by_line, small, "conv")
    parts_d = [parts_d[0]] + [swap(parts_d[i], 2 * order[i], 0) for i in range(1, half)]
    fg, parts_c[0] = lax.optimization_barrier((fg, parts_c[0]))
    parts_c = over_line(passed(parts_c, block, "codes"))
    parts_c[1], parts_d[0] = lax.optimization_barrier((parts_c[1], parts_d[0]))
    parts_d = passed(parts_d, small, "conv")
    parts_d = [parts_d[0], swap(parts_d[3], 1, 2), swap(parts_d[2], 0, 2), swap(parts_d[1], 1, 0)]
    total = small + block
    piece, squares = pl.pallas_call(
        functools.partial(final_kernel, (small, block), (4, half)),
        out_shape=(shape((total, DG), F32), shape((ranks * times, 8, 128), F32)),
        in_specs=whole(4 + half),
        out_specs=tuple(whole(2)),
        compiler_params=params(),
        name="final",
    )(*parts_d, *parts_c)

    across = swap(piece, 0, 2)
    squares = lax.all_to_all(squares, ("clip", "tm"), 0, 0, tiled=True)
    fours = [piece, swap(piece, 0, 1), across, swap(across, 0, 1)]
    steps = step_count[0].astype(F32)
    decays = jnp.stack([1.0 / (1.0 - FIRST_DECAY**steps), 1.0 / (1.0 - SECOND_DECAY**steps)])
    if assemble:
        state = dil_state + pw_state + table_state
        norm, *new = pl.pallas_call(
            update_kernel,
            out_shape=(shape((1, 1), F32),) + tuple(shape(v.shape, F32) for v in state),
            in_specs=[smem] + whole(14),
            out_specs=tuple(whole(1) + [hbm] * 9),
            scratch_shapes=[pltpu.VMEM(v.shape, F32) for v in state]
            + [pltpu.SemaphoreType.DMA((18,))],
            compiler_params=params(8),
            name="update",
        )(decays, squares, *fours, *state)
        norm = norm.reshape(1)
        dil_new, pw_new, table_new = new[:3], new[3:6], new[6:]
    else:
        four = jnp.take(jnp.stack(fours, axis=0), time ^ jnp.arange(4), axis=0)
        raw = four[:KERNEL, :small].reshape(KERNEL, 2, out_rows, DG)
        raw = raw.transpose(0, 2, 1, 3).reshape(KERNEL, out_rows, D)
        count = KERNEL * D * HID + D * HID + SLOTS * CODES * DG
        limit = jnp.sqrt(jnp.float32(count))
        norm = jnp.sqrt(jnp.sum(squares, axis=0)[0, :1])
        scale = limit / jnp.maximum(norm[0], limit)
        new = []
        for state, grad, rate in (
            (dil_state, raw, BITRATE_FACTOR),
            (pw_state, four[3, :small], BITRATE_FACTOR),
            (table_state, four[:, small:], RATE_CODE),
        ):
            grad = grad * scale
            weight, second = stepped(*state, grad, rate, decays[0], decays[1])
            new.append((weight, grad, second))
        dil_new, pw_new, table_new = new
    return (
        quant,
        fg,
        norm,
        *[v.transpose(0, 2, 1) for v in dil_new],
        *[v.T for v in pw_new],
        *table_new,
    )


def solution(mesh):
    in_specs = (
        P("clip", "tm", None),
        P("clip", "tm", None),
        P("clip"),
        P(None, "clip", "tm"),
        P(),
        P(None, None, "clip"),
        P(None, "clip"),
        P(None, "clip", None),
        P(None, None, "clip"),
        P(None, None, "clip"),
        P(None, "clip"),
        P(None, "clip"),
        P(None, "clip", None),
        P(None, "clip", None),
    )
    out_specs = (
        P("clip", "tm", None),
        P("clip", "tm", None),
        P(),
        P(None, None, "clip"),
        P(None, None, "clip"),
        P(None, None, "clip"),
        P(None, "clip"),
        P(None, "clip"),
        P(None, "clip"),
        P(None, "clip", None),
        P(None, "clip", None),
        P(None, "clip", None),
    )
    return jax.shard_map(shards, mesh=mesh, in_specs=in_specs, out_specs=out_specs, check_vma=False)
```
